32 devices in a mesh: dp: 8 (over y, x, core), tensor: 4 (over z).
Axes of the slice: x: 2, y: 2, z: 4, core: 2. Of those that a mesh axis runs over, the one named last changes fastest.
Arguments:
- piece_table: bfloat16 [16384, 512], replicated, may hold values from -7.5 to 7.5
- piece_ids: int32 [16384, 8], P(('dp', 'tensor')), may hold values from 0 to 16383
- piece_counts: int32 [16384], P(('dp', 'tensor')), may hold values from 1 to 7, as said below
- text_ids: int32 [8, 1024], P('dp'), may hold values from 0 to 16383
- text_lengths: int32 [8], P('dp'), may hold values from 256 to 1024, as said below
- lm_gains: bfloat16 [2, 2048], replicated, may hold values from 0.5 to 1.5
- w_query: bfloat16 [2048, 2048], P(None, 'tensor'), may hold values from -0.125 to 0.125
- w_kv: bfloat16 [2, 2048, 256], P(None, None, 'tensor'), may hold values from -0.125 to 0.125
- w_attn_out: bfloat16 [2048, 2048], P('tensor'), may hold values from -2 to 2
- w_gate_up: bfloat16 [2, 2048, 5632], P(None, None, 'tensor'), may hold values from -0.125 to 0.125
- w_down: bfloat16 [5632, 2048], P('tensor'), may hold values from -0.078125 to 0.078125
- cotangent: bfloat16 [8, 1024, 2048], P('dp'), may hold values from -6 to 6
- step_count: int32 [1], replicated, may hold values from 2 to 20
- hyper_qkv: float32 [512, 1536], P(('dp', 'tensor')), may hold values from -0.25 to 0.25
- hyper_out: float32 [512, 512], P(('dp', 'tensor')), may hold values from -0.5 to 0.5
- hyper_in: float32 [512, 2048], P(('dp', 'tensor')), may hold values from -0.25 to 0.25
- hyper_back: float32 [2048, 512], P(('dp', 'tensor')), may hold values from -0.125 to 0.125
- hyper_proj: float32 [512, 2048], P(('dp', 'tensor')), may hold values from -0.25 to 0.25
- hyper_norms: float32 [4, 512], P(None, ('dp', 'tensor')), may hold values from -0.3 to 1.85, as said below
- first_qkv: float32 [512, 1536], P(('dp', 'tensor')), may hold values from -0.00030517578 to 0.00030517578
- first_out: float32 [512, 512], P(('dp', 'tensor')), may hold values from -0.00030517578 to 0.00030517578
- first_in: float32 [512, 2048], P(('dp', 'tensor')), may hold values from -0.00030517578 to 0.00030517578
- first_back: float32 [2048, 512], P(('dp', 'tensor')), may hold values from -0.00030517578 to 0.00030517578
- first_proj: float32 [512, 2048], P(('dp', 'tensor')), may hold values from -0.00030517578 to 0.00030517578
- first_norms: float32 [4, 512], P(None, ('dp', 'tensor')), may hold values from -0.0012207031 to 0.0012207031
- second_qkv: float32 [512, 1536], P(('dp', 'tensor')), may hold values from 2.383022e-10 to 9.532088e-10
- second_out: float32 [512, 512], P(('dp', 'tensor')), may hold values from 2.383022e-10 to 9.532088e-10
- second_in: float32 [512, 2048], P(('dp', 'tensor')), may hold values from 2.383022e-10 to 9.532088e-10
- second_back: float32 [2048, 512], P(('dp', 'tensor')), may hold values from 2.383022e-10 to 9.532088e-10
- second_proj: float32 [512, 2048], P(('dp', 'tensor')), may hold values from 2.383022e-10 to 9.532088e-10
- second_norms: float32 [4, 512], P(None, ('dp', 'tensor')), may hold values from 3.8128354e-09 to 1.5251342e-08
Outputs:
- lm_output: bfloat16 [8, 1024, 2048], P('dp')
- grad_norm: float32 [], replicated
- new_qkv: float32 [512, 1536], P(('dp', 'tensor'))
- new_out: float32 [512, 512], P(('dp', 'tensor'))
- new_in: float32 [512, 2048], P(('dp', 'tensor'))
- new_back: float32 [2048, 512], P(('dp', 'tensor'))
- new_proj: float32 [512, 2048], P(('dp', 'tensor'))
- new_norms: float32 [4, 512], P(None, ('dp', 'tensor'))
- moment_qkv: float32 [512, 1536], P(('dp', 'tensor'))
- moment_out: float32 [512, 512], P(('dp', 'tensor'))
- moment_in: float32 [512, 2048], P(('dp', 'tensor'))
- moment_back: float32 [2048, 512], P(('dp', 'tensor'))
- moment_proj: float32 [512, 2048], P(('dp', 'tensor'))
- moment_norms: float32 [4, 512], P(None, ('dp', 'tensor'))
- square_qkv: float32 [512, 1536], P(('dp', 'tensor'))
- square_out: float32 [512, 512], P(('dp', 'tensor'))
- square_in: float32 [512, 2048], P(('dp', 'tensor'))
- square_back: float32 [2048, 512], P(('dp', 'tensor'))
- square_proj: float32 [512, 2048], P(('dp', 'tensor'))
- square_norms: float32 [4, 512], P(None, ('dp', 'tensor'))
The draws below stay inside these ranges and needn't reach their ends.
Inputs may be any that keep to these rules, and one draw needn't show every extreme that they name: `piece_counts`: slots at or past an entry's count are padding. `text_lengths`: positions at or past a sequence's length are padding. `hyper_norms`: rows 0 and 2 are gains, rows 1 and 3 biases.
All inputs are finite; a program needn't handle non-finite values.
Results may differ from the reference program's by a relative error of at most 0.02.
Values may be sent and summed in bfloat16 or wider, within the bound.
No kernel may reach another device: no remote copies, remote signals or barrier semaphores. Data moves between devices by JAX's collectives and lax.ppermute only.
A program may use at most 448 MiB of HBM per device.

```python
import math
import jax
import jax.numpy as jnp
import numpy as np
from jax import lax

HHD = 64
HW = 512
HFF = 2048
SLOTS = 8
PIECES = 16384
ENTRIES = 16384
LHEADS = 32
LHD = 64
D = 2048
KVG = 4
FF = 5632
TEXT_LEN = 1024
SEQS = 8
NPARAM = 4196352
N_TENSOR = 4


def draw_piece_counts(key, part):
    counts_all = jax.random.randint(jax.random.fold_in(key, 1), (ENTRIES,), 1, SLOTS)
    chosen = jax.random.randint(jax.random.fold_in(key, 2), (2,), 0, ENTRIES)
    position = jnp.arange(ENTRIES)
    counts_all = jnp.where(position == chosen[0], SLOTS - 1, counts_all)
    counts_all = jnp.where((position == chosen[1]) & (position != chosen[0]), 1, counts_all)
    return counts_all.astype(jnp.int32)


def draw_text_lengths(key, part):
    lengths_all = jax.random.randint(jax.random.fold_in(key, 3), (SEQS,), TEXT_LEN // 4, TEXT_LEN + 1)
    chosen = jax.random.randint(jax.random.fold_in(key, 4), (), 0, SEQS)
    lengths_all = jnp.where(jnp.arange(SEQS) == chosen, TEXT_LEN, lengths_all)
    return lengths_all.astype(jnp.int32)


def draw_hyper_norms(key, part):
    uniform_rows = jax.random.uniform(jax.random.fold_in(key, 5), (4, HW), jnp.float32)
    along = jnp.arange(HW, dtype=jnp.float32)[None, :] / (HW - 1)
    gain_mask = (jnp.arange(4) % 2 == 0)[:, None]
    gain_rows = (0.45 + 0.1 * uniform_rows) * jnp.power(3.0, along)
    return jnp.where(gain_mask, gain_rows, 0.6 * uniform_rows - 0.3)


def draw_piece_table(key, part):
    along = jnp.arange(HW, dtype=jnp.float32)[None, :] / (HW - 1)
    base = jnp.clip(jax.random.normal(jax.random.fold_in(key, 7), (PIECES, HW), jnp.float32), -4.0, 4.0)
    values_out = base * 0.6 * jnp.power(3.0, along)
    return values_out.astype(jnp.bfloat16)


def set_ends(result, key, smallest, top_value):
    shape = result.shape
    spot = [jax.random.randint(jax.random.fold_in(key, axis), (), 0, shape[axis]) for axis in range(len(shape))]
    result = result.at[tuple(spot)].set(smallest)
    longest = shape.index(max(shape))
    spot[longest] = (spot[longest] + 1) % shape[longest]
    return result.at[tuple(spot)].set(top_value)


def steps_of(stream_key, extent, split, smallest, top_value):
    def one(dim, blocks):
        heights = jax.random.uniform(jax.random.fold_in(jax.random.fold_in(stream_key, 6), dim), (blocks,), jnp.float32, smallest / len(split), top_value / len(split))
        return jnp.repeat(jnp.exp(heights), extent[dim] // blocks).reshape((-1,) + (1,) * (len(extent) - dim - 1))

    level = one(*split[0])
    for cut in split[1:]:
        level = level * one(*cut)
    return level


def rank_table(count, slope):
    portions = [(1 << 20) // math.isqrt(standing ** slope) + 1 for standing in range(1, count + 1)]
    width = 1 + sum(portions) // (1 << 30)
    return np.cumsum(np.array([max(1, weight // width) for weight in portions]))


def ranked(stream_key, dims, count, lean):
    grid = rank_table(count, lean)
    ticket = jax.random.randint(jax.random.fold_in(stream_key, 1), dims, 0, int(grid[count - 1]))
    grade = jnp.searchsorted(jnp.asarray(grid, jnp.int32), ticket, side="right")
    return jax.random.permutation(jax.random.fold_in(stream_key, 2), count)[grade].astype(jnp.int32)


def normal_values(stream_key, dims, scale, most, shards=(), held_as=jnp.bfloat16):
    drawn = jax.random.normal(stream_key, dims, jnp.float32) * scale
    if len(shards) > 0:
        drawn = steps_of(stream_key, dims, shards, -0.22, 0.18) * drawn
    return jnp.clip(drawn, min=-most, max=most).astype(held_as)


def setup_inputs(seed: int = 0) -> dict:
    key_list = jax.random.split(jax.random.key(seed), 32)
    return {
        "piece_table": draw_piece_table(jax.random.fold_in(key_list[31], 71), 0),
        "piece_ids": set_ends(ranked(key_list[1], (ENTRIES, SLOTS), PIECES, 2), jax.random.fold_in(key_list[1], 3), 0, PIECES - 1).astype(jnp.int32),
        "piece_counts": draw_piece_counts(jax.random.fold_in(key_list[31], 71), 0),
        "text_ids": set_ends(ranked(key_list[3], (SEQS, TEXT_LEN), ENTRIES, 2), jax.random.fold_in(key_list[3], 3), 0, ENTRIES - 1).astype(jnp.int32),
        "text_lengths": draw_text_lengths(jax.random.fold_in(key_list[31], 71), 0),
        "lm_gains": jnp.clip(1.0 + 0.1 * jax.random.normal(key_list[5], (2, D), jnp.float32), 0.5, 1.5).astype(jnp.bfloat16),
        "w_query": normal_values(key_list[6], (D, D), D ** -0.5, 0.125, ((1, 4),)),
        "w_kv": normal_values(key_list[7], (2, D, KVG * LHD), D ** -0.5, 0.125, ((2, 4),)),
        "w_attn_out": normal_values(key_list[8], (D, D), (D * 4 // TEXT_LEN) ** -0.5, 2.0, ((0, 4),)),
        "w_gate_up": normal_values(key_list[9], (2, D, FF), D ** -0.5, 0.125, ((2, 4),)),
        "w_down": normal_values(key_list[10], (FF, D), FF ** -0.5, 0.078125, ((0, 4),)),
        "cotangent": normal_values(key_list[11], (SEQS, TEXT_LEN, D), 1.0, 6.0, ((0, 8),)),
        "step_count": jax.random.randint(key_list[12], (1,), 2, 21).astype(jnp.int32),
        "hyper_qkv": normal_values(key_list[13], (HW, 3 * HW), HW ** -0.5, 0.25, ((0, 32),), jnp.float32),
        "hyper_out": normal_values(key_list[14], (HW, HW), (HW // 4) ** -0.5, 0.5, ((0, 32),), jnp.float32),
        "hyper_in": normal_values(key_list[15], (HW, HFF), HW ** -0.5, 0.25, ((0, 32),), jnp.float32),
        "hyper_back": normal_values(key_list[16], (HFF, HW), HFF ** -0.5, 0.125, ((0, 32),), jnp.float32),
        "hyper_proj": normal_values(key_list[17], (HW, D), HW ** -0.5, 0.25, ((0, 32),), jnp.float32),
        "hyper_norms": draw_hyper_norms(jax.random.fold_in(key_list[31], 71), 0),
        "first_qkv": normal_values(key_list[19], (HW, 3 * HW), (0.11 * NPARAM ** -0.5), 0.00030517578, ((0, 32),), jnp.float32),
        "first_out": normal_values(key_list[20], (HW, HW), (0.11 * NPARAM ** -0.5), 0.00030517578, ((0, 32),), jnp.float32),
        "first_in": normal_values(key_list[21], (HW, HFF), (0.11 * NPARAM ** -0.5), 0.00030517578, ((0, 32),), jnp.float32),
        "first_back": normal_values(key_list[22], (HFF, HW), (0.11 * NPARAM ** -0.5), 0.00030517578, ((0, 32),), jnp.float32),
        "first_proj": normal_values(key_list[23], (HW, D), (0.11 * NPARAM ** -0.5), 0.00030517578, ((0, 32),), jnp.float32),
        "first_norms": normal_values(key_list[24], (4, HW), (0.44 * NPARAM ** -0.5), 0.0012207031, ((1, 32),), jnp.float32),
        "second_qkv": jnp.clip(jnp.exp(math.log(9.53208845189124e-10) - 1.3862944 * jax.random.uniform(key_list[25], (HW, 3 * HW), jnp.float32) ** steps_of(key_list[25], (HW, 3 * HW), ((0, 32),), -0.2, 0.2)), 2.38302211297281e-10, 9.53208845189124e-10),
        "second_out": jnp.clip(jnp.exp(math.log(9.53208845189124e-10) - 1.3862944 * jax.random.uniform(key_list[26], (HW, HW), jnp.float32) ** steps_of(key_list[26], (HW, HW), ((0, 32),), -0.2, 0.2)), 2.38302211297281e-10, 9.53208845189124e-10),
        "second_in": jnp.clip(jnp.exp(math.log(9.53208845189124e-10) - 1.3862944 * jax.random.uniform(key_list[27], (HW, HFF), jnp.float32) ** steps_of(key_list[27], (HW, HFF), ((0, 32),), -0.2, 0.2)), 2.38302211297281e-10, 9.53208845189124e-10),
        "second_back": jnp.clip(jnp.exp(math.log(9.53208845189124e-10) - 1.3862944 * jax.random.uniform(key_list[28], (HFF, HW), jnp.float32) ** steps_of(key_list[28], (HFF, HW), ((0, 32),), -0.2, 0.2)), 2.38302211297281e-10, 9.53208845189124e-10),
        "second_proj": jnp.clip(jnp.exp(math.log(9.53208845189124e-10) - 1.3862944 * jax.random.uniform(key_list[29], (HW, D), jnp.float32) ** steps_of(key_list[29], (HW, D), ((0, 32),), -0.2, 0.2)), 2.38302211297281e-10, 9.53208845189124e-10),
        "second_norms": jnp.clip(jnp.exp(math.log(1.5251341523025985e-08) - 1.3862944 * jax.random.uniform(key_list[30], (4, HW), jnp.float32) ** steps_of(key_list[30], (4, HW), ((1, 32),), -0.2, 0.2)), 3.812835380756496e-09, 1.5251341523025985e-08),
    }


HIGH = lax.Precision.HIGHEST
eps_norm = 1e-05
learn_rate = 0.05
norms_rate = 0.5
beta_one = 0.9
beta_two = 0.999
adam_eps = 1e-08
weight_decay = 0.1
clip_max = 1.0
masked = -1e+30

@jax.custom_vjp
def low(v):
    return lax.optimization_barrier(v.astype(jnp.bfloat16)).astype(jnp.float32)

@jax.custom_vjp
def low_back(v):
    return v

def low_keep(v):
    return (low(v), None)

def low_pass(kept, grad):
    return (grad,)

def back_keep(v):
    return (v, None)

def back_low(kept, grad):
    return (low(grad),)
low.defvjp(low_keep, low_pass)
low_back.defvjp(back_keep, back_low)

def rope_tables(seq_len, head_width):
    half_width = head_width // 2
    frequency = 10000.0 ** (-jnp.arange(half_width, dtype=jnp.float32) * 2.0 / head_width)
    angles = jnp.arange(seq_len, dtype=jnp.float32)[:, None] * frequency[None, :]
    cosine = jnp.concatenate([jnp.cos(angles), jnp.cos(angles)], axis=1)
    sine_rows = jnp.concatenate([jnp.sin(angles), jnp.sin(angles)], axis=1)
    return (cosine[:, None, :], sine_rows[:, None, :])

def rotate(values_in):
    half_width = values_in.shape[-1] // 2
    return jnp.concatenate([-values_in[..., half_width:], values_in[..., :half_width]], axis=-1)

def rope(values_in, cosine, sine_rows):
    return values_in * cosine + rotate(values_in) * sine_rows

def layer_norm(values_in, gain, bias):
    centred = values_in - lax.optimization_barrier(jnp.mean(values_in, axis=-1, keepdims=True))
    return centred * lax.rsqrt(lax.optimization_barrier(jnp.mean(centred * centred, axis=-1, keepdims=True)) + eps_norm) * gain + bias

def rms_norm(values_in, gain):
    return values_in * lax.rsqrt(lax.optimization_barrier(jnp.mean(values_in * values_in, axis=-1, keepdims=True)) + eps_norm) * gain

def softmax_rows(scores):
    row_top = lax.optimization_barrier(jnp.max(scores, axis=-1, keepdims=True))
    exp_scores = jnp.exp(scores - row_top)
    return exp_scores / lax.optimization_barrier(jnp.sum(exp_scores, axis=-1, keepdims=True))

def hyper_block(low_params, table, ids_block, counts_block):
    w_qkv, w_out, w_in, w_back, w_proj, norm_rows = low_params
    entry_count, slot_count = ids_block.shape
    model_width = w_out.shape[0]
    head_count = model_width // HHD
    score_scale = HHD ** (-0.5)
    inputs = table[ids_block]
    slot_live = jnp.arange(slot_count)[None, :] < counts_block[:, None]
    lead_norm = low(layer_norm(inputs, norm_rows[0], norm_rows[1]))
    qkv_all = low(low_back(jnp.einsum('esw,wc->esc', lead_norm, w_qkv, precision=HIGH)))
    qkv_all = qkv_all.reshape(entry_count, slot_count, 3, head_count, HHD)
    scores = low_back(jnp.einsum('eshc,ethc->ehst', qkv_all[:, :, 0], qkv_all[:, :, 1], precision=HIGH) * score_scale)
    scores = jnp.where(slot_live[:, None, None, :], scores, masked)
    attn_prob = softmax_rows(scores)
    mixed_out = low(low_back(jnp.einsum('ehst,ethc->eshc', low(attn_prob), qkv_all[:, :, 2], precision=HIGH)))
    mixed_out = mixed_out.reshape(entry_count, slot_count, model_width)
    second_in = inputs + low_back(jnp.einsum('esv,vw->esw', mixed_out, w_out, precision=HIGH))
    mid_norm = low(layer_norm(second_in, norm_rows[2], norm_rows[3]))
    hidden_pre = low_back(jnp.einsum('esw,wf->esf', mid_norm, w_in, precision=HIGH))
    hidden = low(jax.nn.gelu(hidden_pre, approximate=True))
    third = second_in + low_back(jnp.einsum('esf,fw->esw', hidden, w_back, precision=HIGH))
    pooled = low(lax.optimization_barrier(jnp.sum(jnp.where(slot_live[:, :, None], third, 0.0), axis=1)) / counts_block[:, None].astype(jnp.float32))
    return low(low_back(jnp.einsum('ew,wd->ed', pooled, w_proj, precision=HIGH)))

def reference(piece_table, piece_ids, piece_counts, text_ids, text_lengths, lm_gains, w_query, w_kv, w_attn_out, w_gate_up, w_down, cotangent, step_count, hyper_qkv, hyper_out, hyper_in, hyper_back, hyper_proj, hyper_norms, first_qkv, first_out, first_in, first_back, first_proj, first_norms, second_qkv, second_out, second_in, second_back, second_proj, second_norms):
    table = piece_table.astype(jnp.float32)
    gain_rows = lm_gains.astype(jnp.float32)
    query_full = w_query.astype(jnp.float32)
    kv_full = w_kv.astype(jnp.float32)
    attn_full = w_attn_out.astype(jnp.float32)
    gate_full = w_gate_up.astype(jnp.float32)
    down_full = w_down.astype(jnp.float32)
    cot_full = cotangent.astype(jnp.float32)
    rank_heads = LHEADS // N_TENSOR
    kv_rank = KVG // N_TENSOR
    group_size = LHEADS // KVG
    rank_ff = FF // N_TENSOR
    seq_len = TEXT_LEN
    cosine, sine_rows = rope_tables(seq_len, LHD)
    score_scale = LHD ** (-0.5)
    positions = jnp.arange(seq_len)
    entry_block = min(ENTRIES, 1024)
    block_count = ENTRIES // entry_block

    def forward(params):
        low_params = tuple((low(param) for param in params))

        def one_entries(packed):
            return hyper_block(low_params, table, packed[0], packed[1])
        embed_blocks = lax.map(jax.checkpoint(one_entries), (piece_ids.reshape(block_count, entry_block, SLOTS), piece_counts.reshape(block_count, entry_block)))
        embed_table = embed_blocks.reshape(ENTRIES, D)

        def one_sequence(packed):
            token_row, length, cot_row = packed
            resid_in = embed_table[token_row]
            attn_in = low(rms_norm(resid_in, gain_rows[0]))
            spread = low_back(jnp.broadcast_to(attn_in, (N_TENSOR, seq_len, D)))
            query_raw = low_back(jnp.einsum('tld,dtc->tlc', spread, query_full.reshape(D, N_TENSOR, rank_heads * LHD), precision=HIGH))
            kv_raw = jnp.einsum('tld,sdtc->stlc', spread, kv_full.reshape(2, D, N_TENSOR, kv_rank * LHD), precision=HIGH)
            key_raw = low_back(kv_raw[0])
            value_rows = low(low_back(kv_raw[1])).reshape(N_TENSOR, seq_len, kv_rank, LHD)
            queries = low(rope(query_raw.reshape(N_TENSOR, seq_len, rank_heads, LHD), cosine, sine_rows))
            queries = queries.reshape(N_TENSOR, seq_len, kv_rank, group_size, LHD)
            key_rows = low(rope(key_raw.reshape(N_TENSOR, seq_len, kv_rank, LHD), cosine, sine_rows))
            scores = low_back(jnp.einsum('tlkgc,tmkc->tkglm', queries, key_rows, precision=HIGH) * score_scale)
            allowed = (positions[None, :] <= positions[:, None]) & (positions < length)[None, :]
            scores = jnp.where(allowed, scores, masked)
            attn_prob = softmax_rows(scores)
            attn_out = low(low_back(jnp.einsum('tkglm,tmkc->tlkgc', low(attn_prob), value_rows, precision=HIGH)))
            attn_out = attn_out.reshape(N_TENSOR, seq_len, rank_heads * LHD)
            attn_part = low(low_back(jnp.einsum('tlc,tcd->tld', attn_out, attn_full.reshape(N_TENSOR, rank_heads * LHD, D), precision=HIGH)))
            resid_mid = resid_in + lax.optimization_barrier(jnp.sum(attn_part, axis=0))
            mlp_in = low(rms_norm(resid_mid, gain_rows[1]))
            spread_two = low_back(jnp.broadcast_to(mlp_in, (N_TENSOR, seq_len, D)))
            gate_up = low_back(jnp.einsum('tld,sdtf->stlf', spread_two, gate_full.reshape(2, D, N_TENSOR, rank_ff), precision=HIGH))
            product = low(jax.nn.silu(gate_up[0]) * gate_up[1])
            down_part = low(low_back(jnp.einsum('tlf,tfd->tld', product, down_full.reshape(N_TENSOR, rank_ff, D), precision=HIGH)))
            layer_out = resid_mid + lax.optimization_barrier(jnp.sum(down_part, axis=0))
            live_rows = (positions < length)[:, None]
            loss_part = jnp.sum(jnp.where(live_rows, layer_out * cot_row, 0.0))
            return (layer_out, loss_part)
        outputs, losses = lax.map(jax.checkpoint(one_sequence), (text_ids, text_lengths, cot_full))
        return (jnp.sum(losses), outputs)
    masters = (hyper_qkv, hyper_out, hyper_in, hyper_back, hyper_proj, hyper_norms)
    loss_value, pull_back, outputs = jax.vjp(forward, masters, has_aux=True)
    grads = pull_back(jnp.ones_like(loss_value))[0]
    square_sum = sum((jnp.sum(grad * grad) for grad in grads))
    grad_norm = jnp.sqrt(square_sum)
    clip_scale = jnp.minimum(1.0, clip_max / (grad_norm + 1e-06))
    step_value = step_count[0].astype(jnp.float32)
    first_fix = 1.0 - jnp.power(beta_one, step_value)
    second_fix = 1.0 - jnp.power(beta_two, step_value)
    firsts = (first_qkv, first_out, first_in, first_back, first_proj, first_norms)
    seconds = (second_qkv, second_out, second_in, second_back, second_proj, second_norms)
    new_params = []
    new_firsts = []
    new_seconds = []
    for position, (master, first_old, second_old, grad) in enumerate(zip(masters, firsts, seconds, grads)):
        clipped = grad * clip_scale
        moment = beta_one * first_old + (1.0 - beta_one) * clipped
        square = beta_two * second_old + (1.0 - beta_two) * clipped * clipped
        update = moment / first_fix / (jnp.sqrt(square / second_fix) + adam_eps)
        rate_now = learn_rate
        if position < 5:
            update = update + weight_decay * master
        else:
            rate_now = norms_rate
        new_params.append(master - rate_now * update)
        new_firsts.append(moment)
        new_seconds.append(square)
    return (outputs.astype(jnp.bfloat16), grad_norm, new_params[0], new_params[1], new_params[2], new_params[3], new_params[4], new_params[5], new_firsts[0], new_firsts[1], new_firsts[2], new_firsts[3], new_firsts[4], new_firsts[5], new_seconds[0], new_seconds[1], new_seconds[2], new_seconds[3], new_seconds[4], new_seconds[5])
```

```python
import jax
import jax.numpy as jnp
from jax import lax
from jax.sharding import PartitionSpec as P

HHD = 64
LHD = 64


eps_norm = 1e-05
learn_rate = 0.05
norms_rate = 0.5
beta_one = 0.9
beta_two = 0.999
adam_eps = 1e-08
weight_decay = 0.1
clip_max = 1.0
masked = -1e30


def rope_tables(seq_len, head_width):
    half_width = head_width // 2
    frequency = 10000.0 ** (-jnp.arange(half_width, dtype=jnp.float32) * 2.0 / head_width)
    angles = jnp.arange(seq_len, dtype=jnp.float32)[:, None] * frequency[None, :]
    cosine = jnp.concatenate([jnp.cos(angles), jnp.cos(angles)], axis=1)
    sine_rows = jnp.concatenate([jnp.sin(angles), jnp.sin(angles)], axis=1)
    return (cosine[:, None, :], sine_rows[:, None, :])


def rotate(values_in):
    half_width = values_in.shape[-1] // 2
    return jnp.concatenate([-values_in[..., half_width:], values_in[..., :half_width]], axis=-1)


def rotate_back(grad_in):
    half_width = grad_in.shape[-1] // 2
    return jnp.concatenate([grad_in[..., half_width:], -grad_in[..., :half_width]], axis=-1)


def rope(values_in, cosine, sine_rows):
    return values_in * cosine + rotate(values_in) * sine_rows


def rope_back(grad_in, cosine, sine_rows):
    return grad_in * cosine + rotate_back(grad_in * sine_rows)


def layer_norm(values_in, gain, bias):
    centred = values_in - jnp.mean(values_in, axis=-1, keepdims=True)
    return (
        centred * lax.rsqrt(jnp.mean(centred * centred, axis=-1, keepdims=True) + eps_norm) * gain
        + bias
    )


def rms_norm(values_in, gain):
    return (
        values_in
        * lax.rsqrt(jnp.mean(values_in * values_in, axis=-1, keepdims=True) + eps_norm)
        * gain
    )


def softmax_rows(scores):
    row_top = jnp.max(scores, axis=-1, keepdims=True)
    exp_scores = jnp.exp(scores - row_top)
    return exp_scores / jnp.sum(exp_scores, axis=-1, keepdims=True)


def hyper_forward(weights, piece_table, piece_ids, piece_counts):
    w_qkv, w_out, w_in, w_back, w_proj, norm_low = weights
    norm_rows = norm_low.astype(jnp.float32)
    entry_count, slot_count = piece_ids.shape
    model_width = w_out.shape[0]
    head_count = model_width // HHD
    row_count = entry_count * slot_count
    score_scale = HHD ** (-0.5)
    inputs = piece_table[piece_ids].astype(jnp.float32)
    slot_live = jnp.arange(slot_count)[None, :] < piece_counts[:, None]
    lead_norm = (
        layer_norm(inputs, norm_rows[0], norm_rows[1])
        .astype(jnp.bfloat16)
        .reshape(row_count, model_width)
    )
    qkv_all = jnp.dot(lead_norm, w_qkv, preferred_element_type=jnp.float32).astype(jnp.bfloat16)
    qkv_all = qkv_all.reshape(entry_count, slot_count, 3, head_count, HHD)
    queries = qkv_all[:, :, 0]
    key_rows = qkv_all[:, :, 1]
    value_rows = qkv_all[:, :, 2]
    scores = (
        jnp.einsum("eshc,ethc->ehst", queries, key_rows, preferred_element_type=jnp.float32)
        * score_scale
    )
    scores = jnp.where(slot_live[:, None, None, :], scores, masked)
    attn_prob = softmax_rows(scores)
    mixed_out = jnp.einsum(
        "ehst,ethc->eshc",
        attn_prob.astype(jnp.bfloat16),
        value_rows,
        preferred_element_type=jnp.float32,
    )
    mixed_out = mixed_out.astype(jnp.bfloat16).reshape(row_count, model_width)
    second_in = inputs + jnp.dot(mixed_out, w_out, preferred_element_type=jnp.float32).reshape(
        entry_count, slot_count, model_width
    )
    mid_norm = (
        layer_norm(second_in, norm_rows[2], norm_rows[3])
        .astype(jnp.bfloat16)
        .reshape(row_count, model_width)
    )
    hidden_pre = jnp.dot(mid_norm, w_in, preferred_element_type=jnp.float32)
    hidden = jax.nn.gelu(hidden_pre, approximate=True).astype(jnp.bfloat16)
    third = second_in + jnp.dot(hidden, w_back, preferred_element_type=jnp.float32).reshape(
        entry_count, slot_count, model_width
    )
    count_rows = piece_counts.astype(jnp.float32)[:, None]
    pooled = (jnp.sum(jnp.where(slot_live[:, :, None], third, 0.0), axis=1) / count_rows).astype(
        jnp.bfloat16
    )
    embeddings = jnp.dot(pooled, w_proj, preferred_element_type=jnp.float32).astype(jnp.bfloat16)
    stash_all = (
        inputs,
        slot_live,
        lead_norm,
        queries,
        key_rows,
        value_rows,
        attn_prob,
        mixed_out,
        second_in,
        mid_norm,
        hidden_pre,
        hidden,
        pooled,
        count_rows,
        norm_rows,
    )
    return (embeddings, stash_all)


def hyper_backward(weights, stash_all, embed_grad):
    w_qkv, w_out, w_in, w_back, w_proj, norm_low = weights
    (
        inputs,
        slot_live,
        lead_norm,
        queries,
        key_rows,
        value_rows,
        attn_prob,
        mixed_out,
        second_in,
        mid_norm,
        hidden_pre,
        hidden,
        pooled,
        count_rows,
        norm_rows,
    ) = stash_all
    entry_count, slot_count, model_width = inputs.shape
    head_count = model_width // HHD
    row_count = entry_count * slot_count
    score_scale = HHD ** (-0.5)
    grad_proj = jnp.einsum("ew,ed->wd", pooled, embed_grad, preferred_element_type=jnp.float32)
    pool_grad = (
        jnp.einsum("ed,wd->ew", embed_grad, w_proj, preferred_element_type=jnp.float32) / count_rows
    )
    third_grad = jnp.where(slot_live[:, :, None], pool_grad[:, None, :], 0.0)
    back_in = third_grad.reshape(row_count, model_width).astype(jnp.bfloat16)
    grad_back = jnp.einsum("rf,rw->fw", hidden, back_in, preferred_element_type=jnp.float32)
    hidden_grad = jnp.einsum("rw,fw->rf", back_in, w_back, preferred_element_type=jnp.float32)
    gelu_pull = jax.vjp(lambda value_in: jax.nn.gelu(value_in, approximate=True), hidden_pre)[1]
    pre_grad = gelu_pull(hidden_grad)[0].astype(jnp.bfloat16)
    grad_in = jnp.einsum("rw,rf->wf", mid_norm, pre_grad, preferred_element_type=jnp.float32)
    mid_grad = jnp.einsum("rf,wf->rw", pre_grad, w_in, preferred_element_type=jnp.float32).reshape(
        entry_count, slot_count, model_width
    )
    norm_pull = jax.vjp(layer_norm, second_in, norm_rows[2], norm_rows[3])[1]
    resid_grad, gain_two, bias_two = norm_pull(mid_grad)
    resid_grad = resid_grad + third_grad
    out_in = resid_grad.reshape(row_count, model_width).astype(jnp.bfloat16)
    grad_out = jnp.einsum("rv,rw->vw", mixed_out, out_in, preferred_element_type=jnp.float32)
    mix_grad = jnp.einsum("rw,vw->rv", out_in, w_out, preferred_element_type=jnp.float32).astype(
        jnp.bfloat16
    )
    mix_grad = mix_grad.reshape(entry_count, slot_count, head_count, HHD)
    prob_grad = jnp.einsum(
        "eshc,ethc->ehst", mix_grad, value_rows, preferred_element_type=jnp.float32
    )
    value_grad = jnp.einsum(
        "ehst,eshc->ethc",
        attn_prob.astype(jnp.bfloat16),
        mix_grad,
        preferred_element_type=jnp.float32,
    )
    score_grad = attn_prob * (prob_grad - jnp.sum(attn_prob * prob_grad, axis=-1, keepdims=True))
    score_grad = score_grad.astype(jnp.bfloat16)
    query_grad = (
        jnp.einsum("ehst,ethc->eshc", score_grad, key_rows, preferred_element_type=jnp.float32)
        * score_scale
    )
    key_grad = (
        jnp.einsum("ehst,eshc->ethc", score_grad, queries, preferred_element_type=jnp.float32)
        * score_scale
    )
    qkv_grad = (
        jnp.stack([query_grad, key_grad, value_grad], axis=2)
        .astype(jnp.bfloat16)
        .reshape(row_count, 3 * model_width)
    )
    grad_qkv = jnp.einsum("rw,rc->wc", lead_norm, qkv_grad, preferred_element_type=jnp.float32)
    lead_grad = jnp.einsum(
        "rc,wc->rw", qkv_grad, w_qkv, preferred_element_type=jnp.float32
    ).reshape(entry_count, slot_count, model_width)
    first_pull = jax.vjp(layer_norm, inputs, norm_rows[0], norm_rows[1])[1]
    unused_grad, gain_one, bias_one = first_pull(lead_grad)
    grad_norms = jnp.stack([gain_one, bias_one, gain_two, bias_two])
    return (grad_qkv, grad_out, grad_in, grad_back, grad_proj, grad_norms)


def on_device(
    piece_table,
    piece_ids,
    piece_counts,
    text_ids,
    text_lengths,
    lm_gains,
    w_query,
    w_kv,
    w_attn_out,
    w_gate_up,
    w_down,
    cotangent,
    step_count,
    hyper_qkv,
    hyper_out,
    hyper_in,
    hyper_back,
    hyper_proj,
    hyper_norms,
    first_qkv,
    first_out,
    first_in,
    first_back,
    first_proj,
    first_norms,
    second_qkv,
    second_out,
    second_in,
    second_back,
    second_proj,
    second_norms,
):
    axes = ("dp", "tensor")
    rank = lax.axis_index("tensor")
    ranks = lax.axis_size("tensor")
    entry_rows = piece_ids.shape[0]
    pairs = piece_ids[:, 0::2] + piece_ids[:, 1::2] * 65536
    words = jnp.concatenate(
        [pairs, piece_counts[:, None], jnp.zeros((entry_rows, 3), jnp.int32)], axis=1
    )
    words = words.reshape(entry_rows * 8 // 128, 128)
    words_all = lax.all_gather(words, axes, axis=0, tiled=True)
    rows = hyper_qkv.shape[0]
    width = hyper_out.shape[1]
    fold = hyper_in.shape[1] // width
    packed = jnp.concatenate(
        [
            hyper_qkv,
            hyper_out,
            hyper_in.reshape(rows, width, fold).swapaxes(1, 2).reshape(rows, fold * width),
            hyper_proj,
            hyper_back.reshape(rows, fold * width),
            jnp.pad(hyper_norms.T, ((0, 0), (0, 124))),
        ],
        axis=1,
    ).astype(jnp.bfloat16)
    params_all = lax.all_gather(packed, axes, axis=0, tiled=True)
    cut = [0]
    for extent in (3 * width, width, fold * width, hyper_proj.shape[1], fold * width, 128):
        cut.append(cut[-1] + extent)
    w_back_all = params_all[:, cut[4] : cut[5]].reshape(width, fold, width)
    weights = (
        params_all[:, cut[0] : cut[1]],
        params_all[:, cut[1] : cut[2]],
        params_all[:, cut[2] : cut[3]],
        w_back_all.swapaxes(0, 1).reshape(fold * width, width),
        params_all[:, cut[3] : cut[4]],
        params_all[:, cut[5] : cut[5] + 4].T,
    )
    dim = w_query.shape[0]
    chunk = 256
    chunk_count = dim // chunk
    head_cols = w_query.shape[1]
    kv_cols = w_kv.shape[2]

    def attn_chunk(index):
        start = index * chunk
        out_cols = lax.dynamic_slice_in_dim(w_attn_out, start, chunk, 1)
        return jnp.concatenate(
            [
                lax.dynamic_slice_in_dim(w_query, start, chunk, 0),
                lax.dynamic_slice_in_dim(w_kv[0], start, chunk, 0),
                lax.dynamic_slice_in_dim(w_kv[1], start, chunk, 0),
            ]
            + [out_cols[k : k + chunk] for k in range(0, head_cols, chunk)],
            axis=1,
        )

    if lax.axis_size("dp") == chunk_count:
        attn_all = lax.all_gather(attn_chunk(lax.axis_index("dp")), axes, axis=0, tiled=True)
        attn_all = attn_all.reshape(chunk_count, ranks, chunk, -1)
    else:
        attn_all = jnp.stack([attn_chunk(k) for k in range(chunk_count)])
        attn_all = lax.all_gather(attn_all, "tensor", axis=1, tiled=False)
    by_rank = attn_all.swapaxes(0, 1)
    wq_all = by_rank[..., :head_cols].reshape(ranks, dim, head_cols)
    wk_all = by_rank[..., head_cols : head_cols + kv_cols].reshape(ranks, dim, kv_cols)
    wv_all = by_rank[..., head_cols + kv_cols : head_cols + 2 * kv_cols].reshape(
        ranks, dim, kv_cols
    )
    wo_all = by_rank[..., head_cols + 2 * kv_cols :].reshape(
        ranks, chunk_count, chunk, head_cols // chunk, chunk
    )
    wo_all = wo_all.transpose(0, 3, 2, 1, 4).reshape(ranks, head_cols, dim)

    seq_len = text_ids.shape[1]
    local = seq_len // ranks
    length = text_lengths[0]
    my_ids = lax.dynamic_slice_in_dim(text_ids[0], rank * local, local, 0)
    my_words = words_all[my_ids // 16].reshape(local, 16, 8)
    pick = (jnp.arange(16)[None, :] == (my_ids % 16)[:, None])[:, :, None]
    my_words = jnp.sum(jnp.where(pick, my_words, 0), axis=1)
    low_ids = my_words[:, :4] % 65536
    high_ids = my_words[:, :4] // 65536
    my_pieces = jnp.stack([low_ids, high_ids], axis=2).reshape(local, 8)
    my_counts = my_words[:, 4]
    embeddings, stash_all = hyper_forward(weights, piece_table, my_pieces, my_counts)
    resid_in = embeddings.astype(jnp.float32)

    gain_rows = lm_gains.astype(jnp.float32)
    rank_heads = head_cols // LHD
    kv_rank = kv_cols // LHD
    group_size = rank_heads // kv_rank
    groups = ranks * kv_rank
    cosine, sine_rows = rope_tables(seq_len, LHD)
    cosine = lax.dynamic_slice_in_dim(cosine, rank * local, local, 0)
    sine_rows = lax.dynamic_slice_in_dim(sine_rows, rank * local, local, 0)
    attn_in = rms_norm(resid_in, gain_rows[0]).astype(jnp.bfloat16)
    query_raw = jnp.einsum("ld,tdc->ltc", attn_in, wq_all, preferred_element_type=jnp.float32)
    key_raw = jnp.einsum("ld,tdc->ltc", attn_in, wk_all, preferred_element_type=jnp.float32)
    value_raw = jnp.einsum("ld,tdc->ltc", attn_in, wv_all, preferred_element_type=jnp.float32)
    queries = rope(query_raw.reshape(local, -1, LHD), cosine, sine_rows).astype(jnp.bfloat16)
    queries = queries.reshape(local, groups, group_size, LHD)
    my_keys = rope(key_raw.reshape(local, groups, LHD), cosine, sine_rows).astype(jnp.bfloat16)
    my_values = value_raw.reshape(local, groups, LHD).astype(jnp.bfloat16)
    both = jnp.concatenate(
        [my_keys.reshape(local, groups * LHD), my_values.reshape(local, groups * LHD)], axis=1
    )
    both = lax.all_gather(both, "tensor", axis=0, tiled=True)
    key_rows = both[:, : groups * LHD].reshape(seq_len, groups, LHD)
    value_rows = both[:, groups * LHD :].reshape(seq_len, groups, LHD)
    score_scale = LHD ** (-0.5)
    positions = jnp.arange(seq_len)
    row_ids = rank * local + jnp.arange(local)
    allowed = (positions[None, :] <= row_ids[:, None]) & (positions < length)[None, :]
    scores = (
        jnp.einsum("qkgc,mkc->kgqm", queries, key_rows, preferred_element_type=jnp.float32)
        * score_scale
    )
    attn_prob = softmax_rows(jnp.where(allowed, scores, masked))
    prob_low = attn_prob.astype(jnp.bfloat16)
    attn_out = jnp.einsum(
        "kgqm,mkc->qkgc", prob_low, value_rows, preferred_element_type=jnp.float32
    ).astype(jnp.bfloat16)
    attn_out = attn_out.reshape(local, ranks, head_cols)
    attn_sum = jnp.einsum("ltc,tcd->ld", attn_out, wo_all, preferred_element_type=jnp.float32)
    resid_mid = resid_in + attn_sum
    mlp_own = rms_norm(resid_mid, gain_rows[1]).astype(jnp.bfloat16)
    mlp_in = lax.all_gather(mlp_own, "tensor", axis=0, tiled=True)
    live_rows = (positions < length).astype(jnp.float32)[:, None]
    out_grad = cotangent[0].astype(jnp.float32) * live_rows
    out_low = out_grad.astype(jnp.bfloat16)
    product_grad = jnp.einsum("ld,fd->lf", out_low, w_down, preferred_element_type=jnp.float32)
    gate_up = jnp.einsum("ld,tdf->tlf", mlp_in, w_gate_up, preferred_element_type=jnp.float32)
    gate_pull = jax.vjp(
        lambda gate_val, up_val: jax.nn.silu(gate_val) * up_val, gate_up[0], gate_up[1]
    )[1]
    gate_grad, up_grad = gate_pull(product_grad)
    pair_grad = jnp.stack([gate_grad, up_grad]).astype(jnp.bfloat16)
    mlp_part = jnp.einsum("tlf,tdf->ld", pair_grad, w_gate_up, preferred_element_type=jnp.float32)
    mlp_grad = lax.psum_scatter(
        mlp_part.astype(jnp.bfloat16), "tensor", scatter_dimension=0, tiled=True
    ).astype(jnp.float32)
    product = (jax.nn.silu(gate_up[0]) * gate_up[1]).astype(jnp.bfloat16)
    down_part = jnp.dot(product, w_down, preferred_element_type=jnp.float32).astype(jnp.bfloat16)
    down_own = lax.psum_scatter(down_part, "tensor", scatter_dimension=0, tiled=True)
    layer_out = (resid_mid + down_own.astype(jnp.float32)).astype(jnp.bfloat16)
    lm_output = lax.all_gather(layer_out, "tensor", axis=0, tiled=True)[None]
    own_grad = lax.dynamic_slice_in_dim(out_grad, rank * local, local, 0)
    second_pull = jax.vjp(lambda resid_val: rms_norm(resid_val, gain_rows[1]), resid_mid)[1]
    mid_grad = own_grad + second_pull(mlp_grad)[0]
    attn_grad_out = jnp.einsum(
        "ld,tcd->ltc", mid_grad.astype(jnp.bfloat16), wo_all, preferred_element_type=jnp.float32
    )
    attn_grad_out = attn_grad_out.astype(jnp.bfloat16).reshape(local, groups, group_size, LHD)
    prob_grad = jnp.einsum(
        "qkgc,mkc->kgqm", attn_grad_out, value_rows, preferred_element_type=jnp.float32
    )
    score_grad = attn_prob * (prob_grad - jnp.sum(attn_prob * prob_grad, axis=-1, keepdims=True))
    score_grad = score_grad.astype(jnp.bfloat16)
    query_grad = (
        jnp.einsum("kgqm,mkc->qkgc", score_grad, key_rows, preferred_element_type=jnp.float32)
        * score_scale
    )
    key_grad = (
        jnp.einsum("kgqm,qkgc->mkc", score_grad, queries, preferred_element_type=jnp.float32)
        * score_scale
    )
    value_grad = jnp.einsum(
        "kgqm,qkgc->mkc", prob_low, attn_grad_out, preferred_element_type=jnp.float32
    )
    both_grad = jnp.concatenate(
        [key_grad.reshape(seq_len, groups * LHD), value_grad.reshape(seq_len, groups * LHD)],
        axis=1,
    )
    both_grad = lax.psum_scatter(both_grad, "tensor", scatter_dimension=0, tiled=True)
    key_grad = both_grad[:, : groups * LHD].reshape(local, groups, LHD)
    value_grad = both_grad[:, groups * LHD :].reshape(local, ranks, kv_cols)
    query_back = rope_back(query_grad.reshape(local, -1, LHD), cosine, sine_rows)
    query_back = query_back.astype(jnp.bfloat16).reshape(local, ranks, head_cols)
    key_back = rope_back(key_grad, cosine, sine_rows).reshape(local, ranks, kv_cols)
    attn_grad = (
        jnp.einsum("ltc,tdc->ld", query_back, wq_all, preferred_element_type=jnp.float32)
        + jnp.einsum(
            "ltc,tdc->ld",
            key_back.astype(jnp.bfloat16),
            wk_all,
            preferred_element_type=jnp.float32,
        )
        + jnp.einsum(
            "ltc,tdc->ld",
            value_grad.astype(jnp.bfloat16),
            wv_all,
            preferred_element_type=jnp.float32,
        )
    )
    first_pull = jax.vjp(lambda resid_val: rms_norm(resid_val, gain_rows[0]), resid_in)[1]
    embed_grad = (mid_grad + first_pull(attn_grad)[0]).astype(jnp.bfloat16)
    grad_qkv, grad_out, grad_in, grad_back, grad_proj, grad_norms = hyper_backward(
        weights, stash_all, embed_grad
    )

    def scatter(parts):
        joined = jnp.concatenate(parts, axis=1).astype(jnp.bfloat16)
        for axis in axes:
            joined = lax.psum_scatter(joined, axis, scatter_dimension=0, tiled=True)
        return joined.astype(jnp.float32)

    back_rows = grad_back.reshape(fold, width, width).swapaxes(0, 1).reshape(width, fold * width)
    late = scatter([grad_qkv, jnp.pad(grad_norms.T, ((0, 0), (0, 124)))])
    early = scatter([grad_out, grad_in, grad_proj, back_rows])
    square_sum = jnp.sum(early * early) + jnp.sum(late * late)
    in_shard = early[:, width : (1 + fold) * width].reshape(rows, fold, width)
    proj_end = (1 + fold) * width + hyper_proj.shape[1]
    grad_shards = (
        late[:, : 3 * width],
        early[:, :width],
        in_shard.swapaxes(1, 2).reshape(rows, fold * width),
        early[:, proj_end:].reshape(rows * fold, width),
        early[:, (1 + fold) * width : proj_end],
        late[:, 3 * width : 3 * width + 4].T,
    )
    for axis in axes:
        square_sum = lax.psum(square_sum, axis)
    grad_norm = jnp.sqrt(square_sum)
    clip_scale = jnp.minimum(1.0, clip_max / (grad_norm + 1e-06))
    step_value = step_count[0].astype(jnp.float32)
    first_fix = 1.0 - jnp.power(beta_one, step_value)
    second_fix = 1.0 - jnp.power(beta_two, step_value)
    masters = (hyper_qkv, hyper_out, hyper_in, hyper_back, hyper_proj, hyper_norms)
    firsts = (first_qkv, first_out, first_in, first_back, first_proj, first_norms)
    seconds = (second_qkv, second_out, second_in, second_back, second_proj, second_norms)
    new_params = []
    new_firsts = []
    new_seconds = []
    for position, (master, first_old, second_old, shard_grad) in enumerate(
        zip(masters, firsts, seconds, grad_shards)
    ):
        clipped = shard_grad * clip_scale
        moment = beta_one * first_old + (1.0 - beta_one) * clipped
        square = beta_two * second_old + (1.0 - beta_two) * clipped * clipped
        update = moment / first_fix / (jnp.sqrt(square / second_fix) + adam_eps)
        rate_now = learn_rate
        if position < 5:
            update = update + weight_decay * master
        else:
            rate_now = norms_rate
        new_params.append(master - rate_now * update)
        new_firsts.append(moment)
        new_seconds.append(square)
    return (
        lm_output,
        grad_norm,
        new_params[0],
        new_params[1],
        new_params[2],
        new_params[3],
        new_params[4],
        new_params[5],
        new_firsts[0],
        new_firsts[1],
        new_firsts[2],
        new_firsts[3],
        new_firsts[4],
        new_firsts[5],
        new_seconds[0],
        new_seconds[1],
        new_seconds[2],
        new_seconds[3],
        new_seconds[4],
        new_seconds[5],
    )


def solution(mesh):
    in_specs = (
        P(),
        P(("dp", "tensor"), None),
        P(("dp", "tensor")),
        P("dp", None),
        P("dp"),
        P(),
        P(None, "tensor"),
        P(None, None, "tensor"),
        P("tensor", None),
        P(None, None, "tensor"),
        P("tensor", None),
        P("dp", None, None),
        P(),
        P(("dp", "tensor"), None),
        P(("dp", "tensor"), None),
        P(("dp", "tensor"), None),
        P(("dp", "tensor"), None),
        P(("dp", "tensor"), None),
        P(None, ("dp", "tensor")),
        P(("dp", "tensor"), None),
        P(("dp", "tensor"), None),
        P(("dp", "tensor"), None),
        P(("dp", "tensor"), None),
        P(("dp", "tensor"), None),
        P(None, ("dp", "tensor")),
        P(("dp", "tensor"), None),
        P(("dp", "tensor"), None),
        P(("dp", "tensor"), None),
        P(("dp", "tensor"), None),
        P(("dp", "tensor"), None),
        P(None, ("dp", "tensor")),
    )
    out_specs = (
        P("dp", None, None),
        P(),
        P(("dp", "tensor"), None),
        P(("dp", "tensor"), None),
        P(("dp", "tensor"), None),
        P(("dp", "tensor"), None),
        P(("dp", "tensor"), None),
        P(None, ("dp", "tensor")),
        P(("dp", "tensor"), None),
        P(("dp", "tensor"), None),
        P(("dp", "tensor"), None),
        P(("dp", "tensor"), None),
        P(("dp", "tensor"), None),
        P(None, ("dp", "tensor")),
        P(("dp", "tensor"), None),
        P(("dp", "tensor"), None),
        P(("dp", "tensor"), None),
        P(("dp", "tensor"), None),
        P(("dp", "tensor"), None),
        P(None, ("dp", "tensor")),
    )
    return jax.shard_map(
        on_device, mesh=mesh, in_specs=in_specs, out_specs=out_specs, check_vma=False
    )
```

```python
import functools

import jax
import jax.numpy as jnp
from jax import lax
from jax.experimental import pallas as pl
from jax.experimental.pallas import tpu as pltpu
from jax.sharding import PartitionSpec as P

HHD = 64
LHD = 64


eps_norm = 1e-05
learn_rate = 0.05
norms_rate = 0.5
beta_one = 0.9
beta_two = 0.999
adam_eps = 1e-08
weight_decay = 0.1
clip_max = 1.0
masked = -1e30


def rope_tables(seq_len, head_width):
    half_width = head_width // 2
    frequency = 10000.0 ** (-jnp.arange(half_width, dtype=jnp.float32) * 2.0 / head_width)
    angles = jnp.arange(seq_len, dtype=jnp.float32)[:, None] * frequency[None, :]
    cosine = jnp.concatenate([jnp.cos(angles), jnp.cos(angles)], axis=1)
    sine_rows = jnp.concatenate([jnp.sin(angles), jnp.sin(angles)], axis=1)
    return (cosine[:, None, :], sine_rows[:, None, :])


def rms_norm(values_in, gain):
    return (
        values_in
        * lax.rsqrt(jnp.mean(values_in * values_in, axis=-1, keepdims=True) + eps_norm)
        * gain
    )


def softmax_rows(scores):
    row_top = jnp.max(scores, axis=-1, keepdims=True)
    exp_scores = jnp.exp(scores - row_top)
    return exp_scores / jnp.sum(exp_scores, axis=-1, keepdims=True)


low_type = jnp.bfloat16
wide_type = jnp.float32
vmem_bytes = 62 * 1024 * 1024


def mm(left, right):
    return lax.dot_general(
        left, right, (((1,), (0,)), ((), ())), preferred_element_type=wide_type
    )


def mm_nt(left, right):
    return lax.dot_general(
        left, right, (((1,), (1,)), ((), ())), preferred_element_type=wide_type
    )


def mm_tn(left, right):
    return lax.dot_general(
        left, right, (((0,), (0,)), ((), ())), preferred_element_type=wide_type
    )


def half_masks():
    lane = lax.broadcasted_iota(jnp.int32, (1, 128), 1)
    first = (lane < LHD).astype(wide_type).astype(low_type)
    second = (lane >= LHD).astype(wide_type).astype(low_type)
    return first, second


def stack_heads(pair, first, second):
    return jnp.concatenate([pair * first, pair * second], axis=0)


def norm_hat(values_in):
    centred = values_in - jnp.mean(values_in, axis=-1, keepdims=True)
    scale = lax.rsqrt(jnp.mean(centred * centred, axis=-1, keepdims=True) + eps_norm)
    return centred * scale, scale


def norm_back(hat, scale, grad):
    return scale * (
        grad
        - jnp.mean(grad, axis=-1, keepdims=True)
        - hat * jnp.mean(grad * hat, axis=-1, keepdims=True)
    )


def rms_back(values_in, gain, grad):
    scale = lax.rsqrt(jnp.mean(values_in * values_in, axis=-1, keepdims=True) + eps_norm)
    scaled = grad * gain
    hat = values_in * scale
    return scale * (scaled - hat * jnp.mean(scaled * hat, axis=-1, keepdims=True))


gelu_in = 0.7978845608028654
gelu_cube = 0.044715


def slot_mask(lane_row, slots):
    row_entry = lax.broadcasted_iota(jnp.int32, (128, 128), 0) // slots
    col_entry = lax.broadcasted_iota(jnp.int32, (128, 128), 1) // slots
    keep = jnp.where(row_entry == col_entry, lane_row, 0.0)
    bias = jnp.where(keep > 0.0, 0.0, masked)
    return jnp.concatenate([bias, bias], axis=0)


def slot_softmax(stacked, keys, bias):
    scores = mm_nt(stacked, keys) * (HHD ** (-0.5)) + bias
    return softmax_rows(scores)


def hyper_forward_kernel(
    slots, piece_ref, live_ref, lane_ref, count_ref, param_ref, norm_ref,
    qkv_ref, mixed_ref, second_ref, pre_ref, pool_ref, embed_ref,
):
    tile, width = piece_ref.shape
    first, second = half_masks()
    inputs = piece_ref[...].astype(wide_type)
    lead = (norm_hat(inputs)[0] * norm_ref[0:1] + norm_ref[1:2]).astype(low_type)
    for k in range(3):
        part = slice(k * width, (k + 1) * width)
        qkv_ref[:, part] = mm(lead, param_ref[:, part]).astype(low_type)

    for block in range(tile // 128):
        rows = slice(block * 128, (block + 1) * 128)
        bias = slot_mask(lane_ref[:, rows], slots)
        for col in range(0, width, 128):
            stacked = stack_heads(qkv_ref[rows, col : col + 128], first, second)
            keys = qkv_ref[rows, width + col : width + col + 128]
            values = qkv_ref[rows, 2 * width + col : 2 * width + col + 128]
            prob = slot_softmax(stacked, keys, bias).astype(low_type)
            both = jnp.concatenate([prob[:128], prob[128:]], axis=1)
            mixed_ref[rows, col : col + 128] = mm(
                both, stack_heads(values, first, second)
            ).astype(low_type)
    start = 3 * width
    second_in = inputs + mm(mixed_ref[...], param_ref[:, start : start + width])
    second_ref[...] = second_in
    mid = (norm_hat(second_in)[0] * norm_ref[2:3] + norm_ref[3:4]).astype(low_type)
    hidden_count = pre_ref.shape[1]
    start = start + width
    proj = start + hidden_count
    back = proj + embed_ref.shape[1]
    third = second_in
    for col in range(0, hidden_count, width):
        pre = mm(mid, param_ref[:, start + col : start + col + width])
        pre_ref[:, col : col + width] = pre.astype(low_type)
        hidden = (
            0.5 * pre * (1.0 + jnp.tanh(gelu_in * (pre + gelu_cube * pre * pre * pre)))
        ).astype(low_type)
        third = third + mm(hidden, param_ref[:, back + col : back + col + width])
    third = jnp.where(live_ref[...] > 0.0, third, 0.0)
    pooled = jnp.sum(third.reshape(tile // slots, slots, width), axis=1) / count_ref[...]
    pooled = pooled.astype(low_type)
    pool_ref[...] = pooled
    embed_ref[...] = mm(pooled, param_ref[:, proj:back]).astype(low_type)


def hyper_forward(
    params, param_cols, norms, pieces, live_rows, live_lanes, counts, slots, dim
):
    row_count, width = pieces.shape
    tile = 256
    fold = (param_cols - 128 - dim - 4 * width) // 2
    by_row = lambda cols: pl.BlockSpec((tile, cols), lambda i: (i, 0))
    by_entry = lambda cols: pl.BlockSpec((tile // slots, cols), lambda i: (i, 0))
    entries = row_count // slots
    struct = jax.ShapeDtypeStruct
    return pl.pallas_call(
        functools.partial(hyper_forward_kernel, slots),
        grid=(row_count // tile,),
        in_specs=[
            by_row(width),
            by_row(1),
            pl.BlockSpec((1, tile), lambda i: (0, i)),
            by_entry(1),
            pl.BlockSpec((width, param_cols), lambda i: (0, 0), pipeline_mode=pl.Buffered(1)),
            pl.BlockSpec(norms.shape, lambda i: (0, 0)),
        ],
        out_specs=[
            by_row(3 * width), by_row(width), by_row(width), by_row(fold),
            by_entry(width), by_entry(dim),
        ],
        out_shape=[
            struct((row_count, 3 * width), low_type),
            struct((row_count, width), low_type),
            struct((row_count, width), wide_type),
            struct((row_count, fold), low_type),
            struct((entries, width), low_type),
            struct((entries, dim), low_type),
        ],
        compiler_params=pltpu.CompilerParams(vmem_limit_bytes=vmem_bytes),
        cost_estimate=pl.CostEstimate(
            flops=2 * row_count * width * 12 * width,
            bytes_accessed=2 * params.size + 12 * row_count * width,
            transcendentals=row_count * fold,
        ),
        name="hyper_forward",
    )(pieces, live_rows, live_lanes, counts, params, norms)


def hyper_backward_kernel(
    slots, grad_ref, pool_ref, piece_ref, live_ref, lane_ref, count_ref, qkv_ref, mixed_ref,
    second_ref, pre_ref, param_ref, norm_ref, out_ref,
    sums, norm_sums, mix_grad, qkv_grad, pre_grad, hidden_ref,
):
    tile, width = piece_ref.shape
    hidden_count = pre_ref.shape[1]
    dim = grad_ref.shape[1]
    out_at = 3 * width
    in_at = out_at + width
    proj = in_at + hidden_count
    back = proj + dim
    first, second = half_masks()

    @pl.when(pl.program_id(0) == 0)
    def _():
        sums[...] = jnp.zeros_like(sums)
        norm_sums[...] = jnp.zeros_like(norm_sums)

    embed_grad = grad_ref[...]
    pooled = pool_ref[...]
    for col in range(0, dim, width):
        part = slice(proj + col, proj + col + width)
        sums[:, part] += mm_tn(pooled, embed_grad[:, col : col + width])
    pool_grad = mm_nt(embed_grad, param_ref[:, proj:back]) / count_ref[...]
    spread = jnp.broadcast_to(pool_grad[:, None, :], (tile // slots, slots, width))
    third_grad = jnp.where(live_ref[...] > 0.0, spread.reshape(tile, width), 0.0)
    back_in = third_grad.astype(low_type)
    for col in range(0, hidden_count, width):
        pre = pre_ref[:, col : col + width].astype(wide_type)
        square = pre * pre
        bend = jnp.tanh(gelu_in * pre * (1.0 + gelu_cube * square))
        hidden = (0.5 * pre * (1.0 + bend)).astype(low_type)
        hidden_ref[...] = hidden
        slope = 0.5 * (1.0 + bend) + 0.5 * pre * (1.0 - bend * bend) * gelu_in * (
            1.0 + 3.0 * gelu_cube * square
        )
        hidden_grad = mm_nt(back_in, param_ref[:, back + col : back + col + width])
        pre_grad[:, col : col + width] = (slope * hidden_grad).astype(low_type)
        part = slice(back + col, back + col + width)
        sums[:, part] += mm_tn(back_in, hidden_ref[...])
    second_in = second_ref[...]
    hat, scale = norm_hat(second_in)
    mid = (hat * norm_ref[2:3] + norm_ref[3:4]).astype(low_type)
    mid_grad = jnp.zeros((tile, width), wide_type)
    for col in range(0, hidden_count, width):
        part = slice(in_at + col, in_at + col + width)
        grads = pre_grad[:, col : col + width]
        sums[:, part] += mm_tn(mid, grads)
        mid_grad = mid_grad + mm_nt(grads, param_ref[:, part])
    norm_sums[2:3] += jnp.sum(mid_grad * hat, axis=0, keepdims=True)
    norm_sums[3:4] += jnp.sum(mid_grad, axis=0, keepdims=True)
    second_grad = third_grad + norm_back(hat, scale, mid_grad * norm_ref[2:3])
    out_in = second_grad.astype(low_type)
    sums[:, out_at:in_at] += mm_tn(mixed_ref[...], out_in)
    mix_grad[...] = mm_nt(out_in, param_ref[:, out_at:in_at]).astype(low_type)

    score_scale = HHD ** (-0.5)
    for block in range(tile // 128):
        rows = slice(block * 128, (block + 1) * 128)
        bias = slot_mask(lane_ref[:, rows], slots)
        for col in range(0, width, 128):
            stacked = stack_heads(qkv_ref[rows, col : col + 128], first, second)
            keys = qkv_ref[rows, width + col : width + col + 128]
            values = qkv_ref[rows, 2 * width + col : 2 * width + col + 128]
            prob = slot_softmax(stacked, keys, bias)
            grads = stack_heads(mix_grad[rows, col : col + 128], first, second)
            prob_grad = mm_nt(grads, values)
            score_grad = prob * (
                prob_grad - jnp.sum(prob * prob_grad, axis=-1, keepdims=True)
            )
            score_grad = score_grad.astype(low_type)
            both = jnp.concatenate([score_grad[:128], score_grad[128:]], axis=1)
            query_grad = mm(both, stack_heads(keys, first, second)) * score_scale
            key_grad = mm_tn(score_grad, stacked) * score_scale
            value_grad = mm_tn(prob.astype(low_type), grads)
            qkv_grad[rows, col : col + 128] = query_grad.astype(low_type)
            qkv_grad[rows, width + col : width + col + 128] = key_grad.astype(low_type)
            qkv_grad[rows, 2 * width + col : 2 * width + col + 128] = value_grad.astype(low_type)

    inputs = piece_ref[...].astype(wide_type)
    hat_one = norm_hat(inputs)[0]
    lead = (hat_one * norm_ref[0:1] + norm_ref[1:2]).astype(low_type)
    lead_grad = jnp.zeros((tile, width), wide_type)
    for col in range(0, 3 * width, width):
        part = slice(col, col + width)
        grads = qkv_grad[:, part]
        sums[:, part] += mm_tn(lead, grads)
        lead_grad = lead_grad + mm_nt(grads, param_ref[:, part])
    norm_sums[0:1] += jnp.sum(lead_grad * hat_one, axis=0, keepdims=True)
    norm_sums[1:2] += jnp.sum(lead_grad, axis=0, keepdims=True)

    @pl.when(pl.program_id(0) == pl.num_programs(0) - 1)
    def _():
        out_ref[:, :back] = sums[:, :back].astype(low_type)
        for col in range(back, back + hidden_count, width):
            out_ref[:, col : col + width] = sums[:, col : col + width].T.astype(low_type)
        out_ref[:, back + hidden_count :] = norm_sums[...].T.astype(low_type)


def hyper_backward(
    params, param_cols, norms, embed_grad, pooled, pieces, live_rows, live_lanes, counts, qkv, mixed,
    second_in, pre, slots,
):
    row_count, width = pieces.shape
    dim = embed_grad.shape[1]
    fold = pre.shape[1]
    tile = 512
    by_row = lambda cols: pl.BlockSpec((tile, cols), lambda i: (i, 0))
    by_entry = lambda cols: pl.BlockSpec((tile // slots, cols), lambda i: (i, 0))
    whole = lambda shape: pl.BlockSpec(shape, lambda i: (0, 0), pipeline_mode=pl.Buffered(1))
    return pl.pallas_call(
        functools.partial(hyper_backward_kernel, slots),
        grid=(row_count // tile,),
        in_specs=[
            by_entry(dim),
            by_entry(width),
            by_row(width),
            by_row(1),
            pl.BlockSpec((1, tile), lambda i: (0, i)),
            by_entry(1),
            by_row(3 * width),
            by_row(width),
            by_row(width),
            by_row(fold),
            whole((width, param_cols)),
            whole(norms.shape),
        ],
        out_specs=whole((width, param_cols)),
        out_shape=jax.ShapeDtypeStruct((width, param_cols), low_type),
        scratch_shapes=[
            pltpu.VMEM((width, param_cols - 128), wide_type),
            pltpu.VMEM((128, width), wide_type),
            pltpu.VMEM((tile, width), low_type),
            pltpu.VMEM((tile, 3 * width), low_type),
            pltpu.VMEM((tile, fold), low_type),
            pltpu.VMEM((tile, width), low_type),
        ],
        compiler_params=pltpu.CompilerParams(vmem_limit_bytes=vmem_bytes),
        cost_estimate=pl.CostEstimate(
            flops=4 * row_count * width * 12 * width,
            bytes_accessed=4 * params.size + 24 * row_count * width,
            transcendentals=row_count * fold,
        ),
        name="hyper_backward",
    )(
        embed_grad, pooled, pieces, live_rows, live_lanes, counts, qkv, mixed, second_in, pre,
        params, norms,
    )


def turn(values_in, cosine, sine_low, sine_high):
    parts = []
    for col in range(0, values_in.shape[1], 128):
        part = values_in[:, col : col + 128]
        parts.append(
            part * cosine
            + pltpu.roll(part, 96, axis=1) * sine_low
            + pltpu.roll(part, 32, axis=1) * sine_high
        )
    return parts[0] if len(parts) == 1 else jnp.concatenate(parts, axis=1)


def project_both_kernel(
    scalar_ref, embed_ref, gain_ref, kcos_ref, klow_ref, khigh_ref, wkv_ref, both_ref, lead_ref
):
    @pl.when(pl.program_id(0) == 0)
    def _():
        inputs = embed_ref[...].astype(wide_type)
        lead_ref[...] = rms_norm(inputs, gain_ref[0:1]).astype(low_type)

    chunk_count, _, chunk, _ = wkv_ref.shape
    both = jnp.zeros(both_ref.shape, wide_type)
    for k in range(chunk_count):
        both = both + mm(lead_ref[:, k * chunk : (k + 1) * chunk], wkv_ref[k, 0])
    both_ref[...] = turn(both, kcos_ref[...], klow_ref[...], khigh_ref[...]).astype(low_type)


def project_both(scalars, embed, gains, tables, wkv_all):
    local, dim = embed.shape
    chunk_count, ranks, chunk, _ = wkv_all.shape
    whole = lambda shape: pl.BlockSpec(shape, lambda t, place: (0, 0))
    return pl.pallas_call(
        project_both_kernel,
        grid_spec=pltpu.PrefetchScalarGridSpec(
            num_scalar_prefetch=1,
            grid=(ranks,),
            in_specs=[whole((local, dim)), whole(gains.shape)]
            + [whole((local, 128))] * 3
            + [
                pl.BlockSpec(
                    (chunk_count, 1, chunk, 128),
                    lambda t, place: (0, lax.rem(place[2] - t + ranks, ranks), 0, 0),
                )
            ],
            out_specs=[
                pl.BlockSpec((local, 128), lambda t, place: (0, t)), whole((local, dim)),
            ],
        ),
        out_shape=[
            jax.ShapeDtypeStruct((local, ranks * 128), low_type),
            jax.ShapeDtypeStruct((local, dim), low_type),
        ],
        compiler_params=pltpu.CompilerParams(vmem_limit_bytes=vmem_bytes),
        cost_estimate=pl.CostEstimate(
            flops=2 * local * dim * ranks * 128,
            bytes_accessed=2 * dim * ranks * 128 + 4 * local * dim,
            transcendentals=0,
        ),
        name="project_both",
    )(scalars, embed, gains, *tables[3:], wkv_all)


def own_or_rest(own_ref, rest_ref, use):
    @pl.when(pl.program_id(0) == 0)
    def _():
        use(own_ref)

    @pl.when(pl.program_id(0) > 0)
    def _():
        use(rest_ref)


def weight_specs(own_all, side):
    chunk_count, _, chunk, cols = own_all.shape
    shape = (chunk_count, 1, chunk, cols // 2)
    return [
        pl.BlockSpec(shape, lambda t: (0, 0, 0, side)),
        pl.BlockSpec(shape, lambda t: (0, jnp.maximum(t - 1, 0), 0, side)),
    ]


def block_specs(local, count):
    return [
        pl.BlockSpec((local, 128), lambda t, k=k: (0, lax.rem(t - k + count, count)))
        for k in range(count)
    ]


def project_kernel(lead_ref, cos_ref, low_ref, high_ref, own_ref, rest_ref, query_ref):
    def use(wq_ref):
        chunk_count, _, chunk, cols = wq_ref.shape
        query = jnp.zeros((lead_ref.shape[0], cols), wide_type)
        for k in range(chunk_count):
            query = query + mm(lead_ref[:, k * chunk : (k + 1) * chunk], wq_ref[k, 0])
        query = turn(query, cos_ref[...], low_ref[...], high_ref[...])
        query_ref[...] = (query * (LHD ** (-0.5))).astype(low_type)

    own_or_rest(own_ref, rest_ref, use)


def project(lead, tables, own_all, rest_all):
    local, dim = lead.shape
    ranks = rest_all.shape[1] + 1
    cols = own_all.shape[3] // 2
    whole = lambda shape: pl.BlockSpec(shape, lambda t: (0, 0))
    return pl.pallas_call(
        project_kernel,
        grid=(ranks,),
        in_specs=[whole((local, dim))] + [whole((local, 128))] * 3 + weight_specs(own_all, 0),
        out_specs=pl.BlockSpec((local, cols), lambda t: (0, t)),
        out_shape=jax.ShapeDtypeStruct((local, ranks * cols), low_type),
        compiler_params=pltpu.CompilerParams(vmem_limit_bytes=vmem_bytes),
        cost_estimate=pl.CostEstimate(
            flops=2 * local * dim * ranks * cols,
            bytes_accessed=2 * dim * ranks * cols + 4 * local * dim,
            transcendentals=0,
        ),
        name="project",
    )(lead, *tables[:3], own_all, rest_all)


def key_place(start, index, local, seq_len):
    block = index // local
    return lax.rem(start + seq_len - block * local, seq_len) + index - block * local


def attend_kernel(
    scalar_ref, query_ref, own_ref, one_ref, two_ref, three_ref, embed_ref, gain_ref, wo_own, wo_rest,
    mixed_ref, log_ref, mid_ref, lead_ref, total, bias_ref,
):
    local = query_ref.shape[0]
    seq_len = bias_ref.shape[1]
    step = pl.program_id(0)

    @pl.when(step == 0)
    def _():
        total[...] = embed_ref[...].astype(wide_type)
        row = scalar_ref[0] + lax.broadcasted_iota(jnp.int32, (local, seq_len), 0)
        col = lax.broadcasted_iota(jnp.int32, (1, seq_len), 1)
        col = key_place(scalar_ref[0], col, local, seq_len)
        allowed = jnp.where(col <= row, jnp.where(col < scalar_ref[1], 0.0, masked), masked)
        bias_ref[...] = allowed

    first, second = half_masks()
    lane = lax.broadcasted_iota(jnp.int32, (1, 128), 1)
    both = jnp.concatenate([own_ref[...], one_ref[...], two_ref[...], three_ref[...]], axis=0)
    swapped = pltpu.roll(both.astype(wide_type), LHD, axis=1).astype(low_type)
    keys = both * first + swapped * second
    value_low = swapped * first
    value_high = both * second
    logs = jnp.zeros((local, 128), wide_type)
    for pair in range(query_ref.shape[1] // 128):
        cols = slice(pair * 128, (pair + 1) * 128)
        mixed = jnp.zeros((local, 128), wide_type)
        for half, (mask, values) in enumerate(((first, value_low), (second, value_high))):
            scores = mm_nt(query_ref[:, cols] * mask, keys) + bias_ref[...]
            row_top = jnp.max(scores, axis=-1, keepdims=True)
            exp_scores = jnp.exp(scores - row_top)
            exp_total = jnp.sum(exp_scores, axis=-1, keepdims=True)
            prob = (exp_scores * (1.0 / exp_total)).astype(low_type)
            mixed = mixed + mm(prob, values)
            logs = jnp.where(lane == 2 * pair + half, row_top + jnp.log(exp_total), logs)
        mixed_ref[:, cols] = mixed.astype(low_type)
    log_ref[...] = logs.T[0:8]

    def use(wo_ref):
        chunk_count, _, chunk, cols = wo_ref.shape
        for k in range(chunk_count):
            part = slice(k * chunk, (k + 1) * chunk)
            for col in range(0, cols, chunk):
                total[:, part] += mm(
                    mixed_ref[:, col : col + chunk], wo_ref[k, 0, :, col : col + chunk]
                )

    own_or_rest(wo_own, wo_rest, use)

    @pl.when(step == pl.num_programs(0) - 1)
    def _():
        mid_ref[...] = total[...]
        lead_ref[...] = rms_norm(total[...], gain_ref[1:2]).astype(low_type)


def attend(scalars, query, blocks, embed, gains, own_all, rest_all):
    local, dim = embed.shape
    ranks = len(blocks)
    seq_len = local * ranks
    cols = own_all.shape[3] // 2
    whole = lambda shape: pl.BlockSpec(shape, lambda t: (0, 0))
    return pl.pallas_call(
        attend_kernel,
        grid=(ranks,),
        in_specs=[
            pl.BlockSpec(memory_space=pltpu.SMEM),
            pl.BlockSpec((local, cols), lambda t: (0, t)),
        ]
        + block_specs(local, ranks)
        + [whole((local, dim)), whole(gains.shape)]
        + weight_specs(own_all, 1),
        out_specs=[
            pl.BlockSpec((local, cols), lambda t: (0, t)),
            pl.BlockSpec((8, local), lambda t: (t, 0)),
            whole((local, dim)),
            whole((local, dim)),
        ],
        out_shape=[
            jax.ShapeDtypeStruct((local, ranks * cols), low_type),
            jax.ShapeDtypeStruct((8 * ranks, local), wide_type),
            jax.ShapeDtypeStruct((local, dim), wide_type),
            jax.ShapeDtypeStruct((local, dim), low_type),
        ],
        scratch_shapes=[
            pltpu.VMEM((local, dim), wide_type),
            pltpu.VMEM((local, seq_len), wide_type),
        ],
        compiler_params=pltpu.CompilerParams(vmem_limit_bytes=vmem_bytes),
        cost_estimate=pl.CostEstimate(
            flops=2 * local * dim * dim + 16 * local * seq_len * dim,
            bytes_accessed=2 * dim * dim + 8 * local * dim,
            transcendentals=local * seq_len * dim // LHD,
        ),
        name="attend",
    )(scalars, query, *blocks, embed, gains, own_all, rest_all)


def attend_back_kernel(
    scalar_ref, mlp_ref, cot_ref, mid_ref, gain_ref, query_ref, own_ref, one_ref, two_ref,
    three_ref, mixed_ref, log_ref, cos_ref, low_ref, high_ref, wo_own, wo_rest,
    resid_ref, qgrad_ref, own_grad, one_grad, two_grad, three_grad, low_grad, bias_ref, out_grad,
):
    local = query_ref.shape[0]
    seq_len = bias_ref.shape[0]

    @pl.when(pl.program_id(0) == 0)
    def _():
        row = scalar_ref[0] + lax.broadcasted_iota(jnp.int32, (local, 1), 0)
        own = jnp.where(row < scalar_ref[1], cot_ref[...].astype(wide_type), 0.0)
        grad = own + rms_back(mid_ref[...], gain_ref[1:2], mlp_ref[...].astype(wide_type))
        resid_ref[...] = grad
        low_grad[...] = grad.astype(low_type)
        col = scalar_ref[0] + lax.broadcasted_iota(jnp.int32, (seq_len, local), 1)
        key = lax.broadcasted_iota(jnp.int32, (seq_len, 1), 0)
        key = key_place(scalar_ref[0], key, local, seq_len)
        bias_ref[...] = jnp.where(
            key <= col, jnp.where(key < scalar_ref[1], 0.0, masked), masked
        )

    def use(wo_ref):
        chunk_count, _, chunk, cols = wo_ref.shape
        for col in range(0, cols, chunk):
            part_sum = jnp.zeros((local, chunk), wide_type)
            for k in range(chunk_count):
                part_sum = part_sum + mm_nt(
                    low_grad[:, k * chunk : (k + 1) * chunk], wo_ref[k, 0, :, col : col + chunk]
                )
            out_grad[:, col : col + chunk] = part_sum.astype(low_type)

    own_or_rest(wo_own, wo_rest, use)
    first, second = half_masks()
    lane = lax.broadcasted_iota(jnp.int32, (1, 128), 1)
    low_lane = lane < LHD
    both = jnp.concatenate([own_ref[...], one_ref[...], two_ref[...], three_ref[...]], axis=0)
    swapped = pltpu.roll(both.astype(wide_type), LHD, axis=1).astype(low_type)
    keys = both * first + swapped * second
    values = swapped * first + both * second
    key_low = both * first
    key_high = swapped * second
    sums = jnp.zeros((local, 128), wide_type)
    for pair in range(query_ref.shape[1] // 128):
        part = slice(pair * 128, (pair + 1) * 128)
        product = mixed_ref[:, part].astype(wide_type) * out_grad[:, part].astype(wide_type)
        one = jnp.sum(jnp.where(low_lane, product, 0.0), axis=-1, keepdims=True)
        two = jnp.sum(jnp.where(low_lane, 0.0, product), axis=-1, keepdims=True)
        sums = jnp.where(lane == 2 * pair, one, sums)
        sums = jnp.where(lane == 2 * pair + 1, two, sums)
    sums = sums.T[0:8]
    key_sum = jnp.zeros((seq_len, 128), wide_type)
    value_sum = jnp.zeros((seq_len, 128), wide_type)
    for pair in range(query_ref.shape[1] // 128):
        part = slice(pair * 128, (pair + 1) * 128)
        query_grad = jnp.zeros((local, 128), wide_type)
        for half, (mask, key_side) in enumerate(((first, key_low), (second, key_high))):
            head = 2 * pair + half
            query = query_ref[:, part] * mask
            grads = out_grad[:, part] * mask
            scores = mm_nt(keys, query) + bias_ref[...]
            prob = jnp.exp(scores - log_ref[head : head + 1])
            prob_grad = mm_nt(values, grads)
            score_grad = (prob * (prob_grad - sums[head : head + 1])).astype(low_type)
            key_sum = key_sum + mm(score_grad, query)
            value_sum = value_sum + mm(prob.astype(low_type), grads)
            query_grad = query_grad + mm_tn(score_grad, key_side)
        query_grad = query_grad * (LHD ** (-0.5))
        spun = query_grad * low_ref[...]
        spin = query_grad * high_ref[...]
        query_grad = (
            query_grad * cos_ref[...]
            + pltpu.roll(spin, 96, axis=1)
            + pltpu.roll(spun, 32, axis=1)
        )
        qgrad_ref[:, part] = query_grad.astype(low_type)
    key_sum = key_sum + pltpu.roll(key_sum, LHD, axis=1)
    value_sum = value_sum + pltpu.roll(value_sum, LHD, axis=1)
    both_grad = jnp.where(low_lane, key_sum, value_sum).astype(low_type)
    for k, ref in enumerate((own_grad, one_grad, two_grad, three_grad)):
        ref[...] = both_grad[k * local : (k + 1) * local]


def attend_back(
    scalars, mlp_grad, cot_own, mid, gains, query, blocks, mixed, logs, tables, own_all, rest_all
):
    local, dim = mid.shape
    ranks = len(blocks)
    seq_len = local * ranks
    cols = own_all.shape[3] // 2
    whole = lambda shape: pl.BlockSpec(shape, lambda t: (0, 0))
    by_block = block_specs(local, ranks)
    by_rank = pl.BlockSpec((local, cols), lambda t: (0, t))
    return pl.pallas_call(
        attend_back_kernel,
        grid=(ranks,),
        in_specs=[
            pl.BlockSpec(memory_space=pltpu.SMEM),
            whole((local, dim)),
            whole((local, dim)),
            whole((local, dim)),
            whole(gains.shape),
            by_rank,
        ]
        + by_block
        + [
            by_rank,
            pl.BlockSpec((8, local), lambda t: (t, 0)),
            whole((local, 128)),
            whole((local, 128)),
            whole((local, 128)),
        ]
        + weight_specs(own_all, 1),
        out_specs=[
            whole((local, dim)),
            by_rank,
        ]
        + by_block,
        out_shape=[
            jax.ShapeDtypeStruct((local, dim), wide_type),
            jax.ShapeDtypeStruct((local, ranks * cols), low_type),
        ]
        + [jax.ShapeDtypeStruct((local, ranks * 128), low_type)] * len(blocks),
        scratch_shapes=[
            pltpu.VMEM((local, dim), low_type),
            pltpu.VMEM((seq_len, local), wide_type),
            pltpu.VMEM((local, cols), low_type),
        ],
        compiler_params=pltpu.CompilerParams(vmem_limit_bytes=vmem_bytes),
        cost_estimate=pl.CostEstimate(
            flops=2 * local * dim * dim + 40 * local * seq_len * dim,
            bytes_accessed=2 * dim * dim + 20 * local * dim,
            transcendentals=local * seq_len * dim // LHD,
        ),
        name="attend_back",
    )(
        scalars, mlp_grad, cot_own, mid, gains, query, *blocks, mixed, logs, *tables[:3], own_all,
        rest_all,
    )


def project_back_query_kernel(qgrad_ref, own_ref, rest_ref, total_ref):
    @pl.when(pl.program_id(0) == 0)
    def _():
        total_ref[...] = jnp.zeros_like(total_ref)

    def use(wq_ref):
        chunk_count, _, chunk, _ = wq_ref.shape
        for k in range(chunk_count):
            total_ref[:, k * chunk : (k + 1) * chunk] += mm_nt(qgrad_ref[...], wq_ref[k, 0])

    own_or_rest(own_ref, rest_ref, use)


def project_back_query(query_grad, own_all, rest_all):
    chunk_count, _, chunk, _ = own_all.shape
    ranks = rest_all.shape[1] + 1
    cols = own_all.shape[3] // 2
    local = query_grad.shape[0]
    dim = chunk_count * chunk
    return pl.pallas_call(
        project_back_query_kernel,
        grid=(ranks,),
        in_specs=[pl.BlockSpec((local, cols), lambda t: (0, t))] + weight_specs(own_all, 0),
        out_specs=pl.BlockSpec((local, dim), lambda t: (0, 0)),
        out_shape=jax.ShapeDtypeStruct((local, dim), wide_type),
        compiler_params=pltpu.CompilerParams(vmem_limit_bytes=vmem_bytes),
        cost_estimate=pl.CostEstimate(
            flops=2 * local * dim * ranks * cols,
            bytes_accessed=2 * dim * ranks * cols + 8 * local * dim,
            transcendentals=0,
        ),
        name="project_back_query",
    )(query_grad, own_all, rest_all)


def project_back_kernel(
    scalar_ref, embed_ref, gain_ref, resid_ref, part_ref, kcos_ref, klow_ref, khigh_ref, own_ref, one_ref,
    two_ref, three_ref, wkv_ref, grad_ref, total,
):
    step = pl.program_id(0)

    @pl.when(step == 0)
    def _():
        total[...] = part_ref[...]

    both = own_ref[...].astype(wide_type)
    for ref in (one_ref, two_ref, three_ref):
        both = both + ref[...].astype(wide_type)
    both = (
        both * kcos_ref[...]
        + pltpu.roll(both * khigh_ref[...], 96, axis=1)
        + pltpu.roll(both * klow_ref[...], 32, axis=1)
    ).astype(low_type)
    chunk_count, _, chunk, _ = wkv_ref.shape
    for k in range(chunk_count):
        total[:, k * chunk : (k + 1) * chunk] += mm_nt(both, wkv_ref[k, 0])

    @pl.when(step == pl.num_programs(0) - 1)
    def _():
        grad = resid_ref[...] + rms_back(
            embed_ref[...].astype(wide_type), gain_ref[0:1], total[...]
        )
        grad_ref[...] = grad.astype(low_type)


def project_back(scalars, embed, gains, resid, part, tables, blocks, wkv_all):
    local, dim = embed.shape
    chunk_count, ranks, chunk, _ = wkv_all.shape
    whole = lambda shape: pl.BlockSpec(shape, lambda t, place: (0, 0))
    return pl.pallas_call(
        project_back_kernel,
        grid_spec=pltpu.PrefetchScalarGridSpec(
            num_scalar_prefetch=1,
            grid=(ranks,),
            in_specs=[whole((local, dim)), whole(gains.shape)]
            + [whole((local, dim))] * 2
            + [whole((local, 128))] * 3
            + [pl.BlockSpec((local, 128), lambda t, place: (0, t))] * len(blocks)
            + [
                pl.BlockSpec(
                    (chunk_count, 1, chunk, 128),
                    lambda t, place: (0, lax.rem(place[2] - t + ranks, ranks), 0, 0),
                )
            ],
            out_specs=whole((local, dim)),
            scratch_shapes=[pltpu.VMEM((local, dim), wide_type)],
        ),
        out_shape=jax.ShapeDtypeStruct((local, dim), low_type),
        compiler_params=pltpu.CompilerParams(vmem_limit_bytes=vmem_bytes),
        cost_estimate=pl.CostEstimate(
            flops=2 * local * dim * ranks * 128,
            bytes_accessed=2 * dim * ranks * 128 + 16 * local * dim,
            transcendentals=0,
        ),
        name="project_back",
    )(scalars, embed, gains, resid, part, *tables[3:], *blocks, wkv_all)


def update_kernel(count, scalar_ref, *refs):
    ins, outs = refs[: 4 * count], refs[4 * count :]
    clip_scale, first_fix, second_fix = scalar_ref[0], scalar_ref[1], scalar_ref[2]
    for k in range(count):
        grad, master, first_old, second_old = (ins[j * count + k][...] for j in range(4))
        clipped = grad * clip_scale
        moment = beta_one * first_old + (1.0 - beta_one) * clipped
        square = beta_two * second_old + (1.0 - beta_two) * clipped * clipped
        update = moment / first_fix / (jnp.sqrt(square / second_fix) + adam_eps)
        if k < count - 1:
            new = master - learn_rate * (update + weight_decay * master)
        else:
            new = master - norms_rate * update
        outs[k][...] = new
        outs[count + k][...] = moment
        outs[2 * count + k][...] = square


def update_params(scalars, grads, masters, firsts, seconds):
    count = len(grads)
    arrays = [*grads, *masters, *firsts, *seconds]
    vmem = pl.BlockSpec(memory_space=pltpu.VMEM)
    return pl.pallas_call(
        functools.partial(update_kernel, count),
        in_specs=[pl.BlockSpec(memory_space=pltpu.SMEM)] + [vmem] * len(arrays),
        out_specs=[vmem] * (3 * count),
        out_shape=[jax.ShapeDtypeStruct(x.shape, wide_type) for x in masters] * 3,
        name="update_params",
    )(scalars, *arrays)


def feed_kernel(
    place_ref, rows_ref, grad_ref, weight_ref, part_ref, product_ref, gate, up, gate_grad, up_grad
):
    step = pl.program_id(0)
    half = pl.num_programs(0) // 2
    depth = weight_ref.shape[1]

    @pl.when(step < half)
    def _():
        part = rows_ref[:, pl.ds(pl.multiple_of(step * depth, depth), depth)]

        @pl.when(step == 0)
        def _():
            gate[...] = mm(part, weight_ref[0])
            up[...] = mm(part, weight_ref[1])

        @pl.when(step > 0)
        def _():
            gate[...] += mm(part, weight_ref[0])
            up[...] += mm(part, weight_ref[1])

    @pl.when(step == half)
    def _():
        gate_val, up_val, grad = gate[...], up[...], grad_ref[...].astype(wide_type)
        sigma = 1.0 / (1.0 + jnp.exp(-gate_val))
        swish = gate_val * sigma
        product_ref[...] = (swish * up_val).astype(low_type)
        up_grad[...] = (swish * grad).astype(low_type)
        slope = sigma * (1.0 + gate_val * (1.0 - sigma))
        gate_grad[...] = (slope * up_val * grad).astype(low_type)

    @pl.when(step >= half)
    def _():
        part_ref[...] = (
            mm_nt(gate_grad[...], weight_ref[0]) + mm_nt(up_grad[...], weight_ref[1])
        ).astype(low_type)


def feed(place, rows_in, product_grad, w_gate_up):
    local, dim = rows_in.shape
    hidden = w_gate_up.shape[2]
    depth = 512
    half = dim // depth
    return pl.pallas_call(
        feed_kernel,
        grid_spec=pltpu.PrefetchScalarGridSpec(
            num_scalar_prefetch=1,
            grid=(2 * half,),
            in_specs=[
                pl.BlockSpec((local, dim), lambda i, place: (0, 0)),
                pl.BlockSpec((local, hidden), lambda i, place: (place[0], 0)),
                pl.BlockSpec((2, depth, hidden), lambda i, place: (0, lax.rem(i, half), 0)),
            ],
            out_specs=[
                pl.BlockSpec((local, depth), lambda i, place: (0, jnp.maximum(i - half, 0))),
                pl.BlockSpec((local, hidden), lambda i, place: (0, 0)),
            ],
            scratch_shapes=[
                pltpu.VMEM((local, hidden), wide_type),
                pltpu.VMEM((local, hidden), wide_type),
                pltpu.VMEM((local, hidden), low_type),
                pltpu.VMEM((local, hidden), low_type),
            ],
        ),
        out_shape=[
            jax.ShapeDtypeStruct((local, dim), low_type),
            jax.ShapeDtypeStruct((local, hidden), low_type),
        ],
        compiler_params=pltpu.CompilerParams(vmem_limit_bytes=vmem_bytes),
        cost_estimate=pl.CostEstimate(
            flops=8 * local * dim * hidden,
            bytes_accessed=4 * w_gate_up.size,
            transcendentals=local * hidden,
        ),
        name="feed",
    )(place, rows_in, product_grad, w_gate_up)


def shift(values_in, step, first, last, ranks):
    pairs = [(k, k + step) for k in range(first, last + 1) if 0 <= k + step < ranks]
    return lax.ppermute(values_in, "tensor", pairs)


def scatter_sum(joined, tensor_ranks):
    bits = lax.axis_size("dp").bit_length() - 1
    place = lax.axis_index("dp")
    size = lax.axis_size("dp")
    cols = joined.shape[1]
    depth = joined.shape[0] // size
    split = cols // 256 * 128

    def halve(block, spans, bit):
        axis = spans.index(bit)
        mine = (place >> bit) & 1
        away = lax.dynamic_index_in_dim(block, 1 - mine, axis, keepdims=False)
        kept = lax.dynamic_index_in_dim(block, mine, axis, keepdims=False)
        came = lax.ppermute(away, "dp", [(k, k ^ (1 << bit)) for k in range(size)])
        total = kept.astype(wide_type) + came.astype(wide_type)
        return total.astype(low_type), spans[:axis] + spans[axis + 1 :]

    spans = list(range(bits - 1, -1, -1))
    block = joined.reshape((2,) * bits + (depth, cols))
    block, spans = halve(block, spans, 0)
    parts = []
    for index, part in enumerate((block[..., :split], block[..., split:])):
        left = list(spans)
        order = list(reversed(spans)) if index == 0 else list(spans)
        for bit in order:
            part, left = halve(part, left, bit)
        parts.append(part)
    block = jnp.concatenate(parts, axis=1).reshape(tensor_ranks, depth // tensor_ranks, cols)
    rank = lax.axis_index("tensor")
    total = lax.dynamic_index_in_dim(block, rank, 0, keepdims=False).astype(wide_type)
    for k in range(1, tensor_ranks):
        away = lax.dynamic_index_in_dim(block, (rank + k) % tensor_ranks, 0, keepdims=False)
        pairs = [(j, (j + k) % tensor_ranks) for j in range(tensor_ranks)]
        total = total + lax.ppermute(away, "tensor", pairs).astype(wide_type)
    return total


def on_device(
    piece_table,
    piece_ids,
    piece_counts,
    text_ids,
    text_lengths,
    lm_gains,
    w_query,
    w_kv,
    w_attn_out,
    w_gate_up,
    w_down,
    cotangent,
    step_count,
    hyper_qkv,
    hyper_out,
    hyper_in,
    hyper_back,
    hyper_proj,
    hyper_norms,
    first_qkv,
    first_out,
    first_in,
    first_back,
    first_proj,
    first_norms,
    second_qkv,
    second_out,
    second_in,
    second_back,
    second_proj,
    second_norms,
):
    axes = ("dp", "tensor")
    rank = lax.axis_index("tensor")
    ranks = lax.axis_size("tensor")
    entry_rows, slots = piece_ids.shape
    pairs = piece_ids[:, 0::2] + piece_ids[:, 1::2] * 65536
    words = jnp.concatenate(
        [pairs, piece_counts[:, None], jnp.zeros((entry_rows, 3), jnp.int32)], axis=1
    )
    words = words.reshape(entry_rows * 8 // 128, 128)
    words = lax.all_gather(words, "dp", axis=0, tiled=True)
    words = lax.all_gather(words, "tensor", axis=0, tiled=True)

    def from_rank(values_in, step):
        pairs = [(j, (j + step) % ranks) for j in range(ranks)]
        return lax.ppermute(values_in, "tensor", pairs)

    rows = hyper_qkv.shape[0]
    width = hyper_out.shape[1]
    fold = hyper_in.shape[1] // width
    packed = jnp.concatenate(
        [
            hyper_qkv,
            hyper_out,
            hyper_in.reshape(rows, width, fold).swapaxes(1, 2).reshape(rows, fold * width),
            hyper_proj,
            hyper_back.reshape(rows, fold * width),
            jnp.pad(hyper_norms.T, ((0, 0), (0, 124))),
        ],
        axis=1,
    ).astype(jnp.bfloat16)
    dim = w_query.shape[0]
    chunk = 256
    chunk_count = dim // chunk
    head_cols = w_query.shape[1]
    kv_local = jnp.concatenate([w_kv[0], w_kv[1]], axis=1)
    spread_out = lax.axis_size("dp") == chunk_count
    if spread_out:
        mine = lax.dynamic_slice_in_dim(kv_local, lax.axis_index("dp") * chunk, chunk, 0)
        mine = mine.reshape(chunk // rows, rows, 128).swapaxes(0, 1).reshape(rows, -1)
        packed = jnp.concatenate([packed, mine], axis=1)
    stacked = jnp.stack([packed] + [from_rank(packed, k) for k in range(1, ranks)])
    packed = jnp.concatenate(
        [
            lax.dynamic_index_in_dim(stacked, (rank - k) % ranks, 0, keepdims=False)
            for k in range(ranks)
        ],
        axis=0,
    )
    words, packed, rank_done = lax.optimization_barrier((words, packed, lax.axis_index("dp")))
    gathered = lax.all_gather(packed, "dp", axis=0, tiled=True)
    param_cols = hyper_qkv.shape[1] + width + 2 * fold * width + dim + 128
    params = gathered
    norms = jnp.pad(gathered[:, param_cols - 128 : param_cols - 124].T.astype(jnp.float32), ((0, 4), (0, 0)))

    def attn_chunk(index):
        start = index * chunk
        out_cols = lax.dynamic_slice_in_dim(w_attn_out, start, chunk, 1)
        return jnp.concatenate(
            [lax.dynamic_slice_in_dim(w_query, start, chunk, 0)]
            + [out_cols[k : k + chunk] for k in range(0, head_cols, chunk)],
            axis=1,
        )

    own_all = jnp.stack([attn_chunk(k) for k in range(chunk_count)])[:, None]
    if spread_out:
        mine = attn_chunk(rank_done)
        rest_all = jnp.concatenate([from_rank(mine, k) for k in range(1, ranks)], axis=0)
        wkv_all = gathered[:, param_cols:].reshape(
            chunk_count, ranks, rows, chunk // rows, 128
        )
        wkv_all = wkv_all.swapaxes(2, 3).reshape(chunk_count, ranks, chunk, 128)
    else:
        rest_all = jnp.concatenate([from_rank(own_all, k) for k in range(1, ranks)], axis=1)
        wkv_all = lax.all_gather(
            kv_local.reshape(chunk_count, chunk, 128), "tensor", axis=1, tiled=False
        )

    seq_len = text_ids.shape[1]
    local = seq_len // ranks
    length = text_lengths[0]
    my_ids = lax.dynamic_slice_in_dim(text_ids[0], rank * local, local, 0)
    owner = my_ids // entry_rows
    place = (owner % ranks) * lax.axis_size("dp") + owner // ranks
    my_words = words[place * (entry_rows // 16) + (my_ids % entry_rows) // 16]
    pick = (jnp.arange(16)[None, :] == (my_ids % 16)[:, None])[:, :, None]
    my_words = jnp.sum(jnp.where(pick, my_words.reshape(local, 16, 8), 0), axis=1)
    my_pieces = jnp.stack([my_words[:, :4] % 65536, my_words[:, :4] // 65536], axis=2)
    my_counts = my_words[:, 4]
    pieces = piece_table[my_pieces.reshape(local * slots)]
    live = (jnp.arange(slots)[None, :] < my_counts[:, None]).astype(jnp.float32)
    live_rows = live.reshape(local * slots, 1)
    live_lanes = live.reshape(1, local * slots)
    counts = my_counts.astype(jnp.float32)[:, None]
    alive = (jnp.arange(seq_len) < length)[:, None]
    out_low = jnp.where(alive, cotangent[0], jnp.zeros((), jnp.bfloat16))
    product_grad = jnp.einsum("ld,fd->lf", out_low, w_down, preferred_element_type=jnp.float32)
    pieces, rest_all, product_grad = lax.optimization_barrier((pieces, rest_all, product_grad))
    if spread_out:
        rest_all = lax.all_gather(rest_all, "dp", axis=0, tiled=True)
        rest_all = rest_all.reshape(chunk_count, ranks - 1, chunk, -1)
    qkv, mixed, mid_rows, pre, pooled, embed = hyper_forward(
        params, param_cols, norms, pieces, live_rows, live_lanes, counts, slots, dim
    )


    gains = lm_gains.astype(jnp.float32)
    cosine, sine_rows = rope_tables(seq_len, LHD)
    start_row = rank * local
    cosine = lax.dynamic_slice_in_dim(cosine[:, 0], start_row, local, 0)
    sine_rows = lax.dynamic_slice_in_dim(sine_rows[:, 0], start_row, local, 0)
    early_half = (jnp.arange(LHD) < LHD // 2)[None, :]
    sine_low = jnp.where(early_half, -sine_rows, 0.0)
    sine_high = jnp.where(early_half, 0.0, sine_rows)
    zeros = jnp.zeros_like(sine_rows)
    tables = [jnp.concatenate([part, part], axis=1) for part in (cosine, sine_low, sine_high)]
    tables += [
        jnp.concatenate(part, axis=1)
        for part in ((cosine, zeros + 1.0), (sine_low, zeros), (sine_high, zeros))
    ]
    scalars = jnp.stack([start_row, length, rank]).astype(jnp.int32)
    both, lead = project_both(scalars, embed, gains, tables, wkv_all)
    blocks = [both] + [from_rank(both, k) for k in range(1, ranks)]
    query = project(lead, tables, own_all, rest_all)
    attn_mixed, logs, resid_mid, mlp_own = attend(
        scalars, query, blocks, embed, gains, own_all, rest_all
    )

    def plus(left, right):
        return (left.astype(wide_type) + right.astype(wide_type)).astype(low_type)

    top = ranks - 1
    table_of = lambda *values_in: jnp.array(values_in, jnp.int32)[rank]
    near, mid_index, far = table_of(1, 2, 3, 2), table_of(2, 0, 1, 1), table_of(3, 3, 0, 0)
    order = (rank.astype(jnp.int32), near, mid_index, far)
    up_one, down_one = shift(mlp_own, 1, 0, top, ranks), shift(mlp_own, -1, 0, top, ranks)
    own_done = feed(order[0][None], mlp_own, product_grad, w_gate_up)
    up_one, down_one, own_done = lax.optimization_barrier((up_one, down_one, own_done))
    up_two, down_two = shift(up_one, 1, 1, top, ranks), shift(down_one, -1, 0, top - 1, ranks)
    near_rows = jnp.where(rank == top, up_one, down_one)
    near_done = feed(near[None], near_rows, product_grad, w_gate_up)
    up_two, down_two, near_done = lax.optimization_barrier((up_two, down_two, near_done))
    up_three, down_three = shift(up_two, 1, 2, top, ranks), shift(down_two, -1, 0, 1, ranks)
    mid_in = jnp.where(rank == 0, down_two, jnp.where(rank == top, up_two, up_one))
    mid_done = feed(mid_index[None], mid_in, product_grad, w_gate_up)
    up_three, down_three, mid_done = lax.optimization_barrier((up_three, down_three, mid_done))
    far_rows = jnp.where(
        rank == 0,
        down_three,
        jnp.where(rank == 1, down_two, jnp.where(rank == 2, up_two, up_three)),
    )
    far_done = feed(far[None], far_rows, product_grad, w_gate_up)
    products = jnp.zeros((seq_len, w_down.shape[0]), low_type)
    sums = []
    for index, (part, product) in zip(order, (own_done, near_done, mid_done, far_done)):
        sums.append(part)
        products = lax.dynamic_update_slice_in_dim(products, product, index * local, 0)
    part_own, part_near, part_mid, part_far = sums
    down_came = shift(part_far, -1, top, top, ranks)
    up_came = shift(part_far, 1, 0, 0, ranks)
    down_came = shift(
        plus(jnp.where(rank == top, part_mid, part_far), down_came), -1, top - 1, top, ranks
    )
    up_came = shift(plus(jnp.where(rank == 0, part_mid, part_far), up_came), 1, 0, 1, ranks)
    down_came = shift(
        plus(jnp.where(rank == top, part_near, part_mid), down_came), -1, 1, top, ranks
    )
    up_came = shift(plus(part_near, up_came), 1, 0, top - 1, ranks)
    mlp_grad = (
        part_own.astype(wide_type) + down_came.astype(wide_type) + up_came.astype(wide_type)
    ).astype(low_type)
    down_part = jnp.dot(products, w_down, preferred_element_type=jnp.float32).astype(jnp.bfloat16)
    mlp_grad, down_low, down_high = lax.optimization_barrier(
        (mlp_grad, down_part[:, : dim // 2], down_part[:, dim // 2 :])
    )
    low_own = lax.psum_scatter(down_low, "tensor", scatter_dimension=0, tiled=True)
    cot_own = lax.dynamic_slice_in_dim(cotangent[0], start_row, local, 0)
    resid_grad, query_grad, *block_grads = attend_back(
        scalars, mlp_grad, cot_own, resid_mid, gains, query, blocks, attn_mixed, logs, tables,
        own_all, rest_all,
    )
    for k in range(1, ranks):
        block_grads[k] = from_rank(block_grads[k], -k)
    query_part = project_back_query(query_grad, own_all, rest_all)
    block_grads, query_part, down_high = lax.optimization_barrier(
        (block_grads, query_part, down_high)
    )
    high_own = lax.psum_scatter(down_high, "tensor", scatter_dimension=0, tiled=True)
    down_own = jnp.concatenate([low_own, high_own], axis=1)
    layer_out = (resid_mid + down_own.astype(jnp.float32)).astype(jnp.bfloat16)
    embed_grad = project_back(
        scalars, embed, gains, resid_grad, query_part, tables, block_grads, wkv_all
    )
    shard = hyper_backward(
        params, param_cols, norms, embed_grad, pooled, pieces, live_rows, live_lanes, counts, qkv,
        mixed, mid_rows, pre, slots,
    )
    shard, layer_out = lax.optimization_barrier((shard, layer_out))
    lm_output = lax.all_gather(layer_out, "tensor", axis=0, tiled=True)[None]
    shard = scatter_sum(shard, ranks)
    square_sum = jnp.sum(shard * shard)
    cut = [0]
    for extent in (3 * width, width, fold * width, dim, fold * width):
        cut.append(cut[-1] + extent)
    in_shard = shard[:, cut[2] : cut[3]].reshape(rows, fold, width)
    grad_shards = (
        shard[:, : cut[1]],
        shard[:, cut[1] : cut[2]],
        in_shard.swapaxes(1, 2).reshape(rows, fold * width),
        shard[:, cut[4] : cut[5]].reshape(rows * fold, width),
        shard[:, cut[3] : cut[4]],
        shard[:, cut[5] : cut[5] + 4].T,
    )
    square_sum, grad_shards, lm_output = lax.optimization_barrier(
        (square_sum, grad_shards, lm_output)
    )
    for axis in axes:
        square_sum = lax.psum(square_sum, axis)
    grad_norm = jnp.sqrt(square_sum)
    clip_scale = jnp.minimum(1.0, clip_max / (grad_norm + 1e-06))
    step_value = step_count[0].astype(jnp.float32)
    first_fix = 1.0 - jnp.power(beta_one, step_value)
    second_fix = 1.0 - jnp.power(beta_two, step_value)
    masters = (hyper_qkv, hyper_out, hyper_in, hyper_back, hyper_proj, hyper_norms)
    firsts = (first_qkv, first_out, first_in, first_back, first_proj, first_norms)
    seconds = (second_qkv, second_out, second_in, second_back, second_proj, second_norms)
    factors = jnp.stack([clip_scale, first_fix, second_fix])
    return (
        lm_output,
        grad_norm,
        *update_params(factors, grad_shards, masters, firsts, seconds),
    )


def solution(mesh):
    in_specs = (
        P(),
        P(("dp", "tensor"), None),
        P(("dp", "tensor")),
        P("dp", None),
        P("dp"),
        P(),
        P(None, "tensor"),
        P(None, None, "tensor"),
        P("tensor", None),
        P(None, None, "tensor"),
        P("tensor", None),
        P("dp", None, None),
        P(),
        P(("dp", "tensor"), None),
        P(("dp", "tensor"), None),
        P(("dp", "tensor"), None),
        P(("dp", "tensor"), None),
        P(("dp", "tensor"), None),
        P(None, ("dp", "tensor")),
        P(("dp", "tensor"), None),
        P(("dp", "tensor"), None),
        P(("dp", "tensor"), None),
        P(("dp", "tensor"), None),
        P(("dp", "tensor"), None),
        P(None, ("dp", "tensor")),
        P(("dp", "tensor"), None),
        P(("dp", "tensor"), None),
        P(("dp", "tensor"), None),
        P(("dp", "tensor"), None),
        P(("dp", "tensor"), None),
        P(None, ("dp", "tensor")),
    )
    out_specs = (
        P("dp", None, None),
        P(),
        P(("dp", "tensor"), None),
        P(("dp", "tensor"), None),
        P(("dp", "tensor"), None),
        P(("dp", "tensor"), None),
        P(("dp", "tensor"), None),
        P(None, ("dp", "tensor")),
        P(("dp", "tensor"), None),
        P(("dp", "tensor"), None),
        P(("dp", "tensor"), None),
        P(("dp", "tensor"), None),
        P(("dp", "tensor"), None),
        P(None, ("dp", "tensor")),
        P(("dp", "tensor"), None),
        P(("dp", "tensor"), None),
        P(("dp", "tensor"), None),
        P(("dp", "tensor"), None),
        P(("dp", "tensor"), None),
        P(None, ("dp", "tensor")),
    )
    return jax.shard_map(
        on_device, mesh=mesh, in_specs=in_specs, out_specs=out_specs, check_vma=False
    )
```

```python
import functools

import jax
import jax.numpy as jnp
from jax import lax
from jax.experimental import pallas as pl
from jax.experimental.pallas import tpu as pltpu
from jax.sharding import PartitionSpec as P

HHD = 64
LHD = 64


eps_norm = 1e-05
learn_rate = 0.05
norms_rate = 0.5
beta_one = 0.9
beta_two = 0.999
adam_eps = 1e-08
weight_decay = 0.1
clip_max = 1.0
masked = -1e30


def rope_tables(seq_len, head_width):
    half_width = head_width // 2
    frequency = 10000.0 ** (-jnp.arange(half_width, dtype=jnp.float32) * 2.0 / head_width)
    angles = jnp.arange(seq_len, dtype=jnp.float32)[:, None] * frequency[None, :]
    cosine = jnp.concatenate([jnp.cos(angles), jnp.cos(angles)], axis=1)
    sine_rows = jnp.concatenate([jnp.sin(angles), jnp.sin(angles)], axis=1)
    return (cosine[:, None, :], sine_rows[:, None, :])


def rms_norm(values_in, gain):
    return (
        values_in
        * lax.rsqrt(jnp.mean(values_in * values_in, axis=-1, keepdims=True) + eps_norm)
        * gain
    )


def softmax_rows(scores):
    row_top = jnp.max(scores, axis=-1, keepdims=True)
    exp_scores = jnp.exp(scores - row_top)
    return exp_scores / jnp.sum(exp_scores, axis=-1, keepdims=True)


low_type = jnp.bfloat16
wide_type = jnp.float32
vmem_bytes = 62 * 1024 * 1024


def mm(left, right):
    return lax.dot_general(
        left, right, (((1,), (0,)), ((), ())), preferred_element_type=wide_type
    )


def mm_nt(left, right):
    return lax.dot_general(
        left, right, (((1,), (1,)), ((), ())), preferred_element_type=wide_type
    )


def mm_tn(left, right):
    return lax.dot_general(
        left, right, (((0,), (0,)), ((), ())), preferred_element_type=wide_type
    )


def half_masks():
    lane = lax.broadcasted_iota(jnp.int32, (1, 128), 1)
    first = (lane < LHD).astype(wide_type).astype(low_type)
    second = (lane >= LHD).astype(wide_type).astype(low_type)
    return first, second


def stack_heads(pair, first, second):
    return jnp.concatenate([pair * first, pair * second], axis=0)


def norm_hat(values_in):
    centred = values_in - jnp.mean(values_in, axis=-1, keepdims=True)
    scale = lax.rsqrt(jnp.mean(centred * centred, axis=-1, keepdims=True) + eps_norm)
    return centred * scale, scale


def norm_back(hat, scale, grad):
    return scale * (
        grad
        - jnp.mean(grad, axis=-1, keepdims=True)
        - hat * jnp.mean(grad * hat, axis=-1, keepdims=True)
    )


def rms_back(values_in, gain, grad):
    scale = lax.rsqrt(jnp.mean(values_in * values_in, axis=-1, keepdims=True) + eps_norm)
    scaled = grad * gain
    hat = values_in * scale
    return scale * (scaled - hat * jnp.mean(scaled * hat, axis=-1, keepdims=True))


gelu_in = 0.7978845608028654
gelu_cube = 0.044715


def slot_mask(live, slots, axis=0):
    row_entry = lax.broadcasted_iota(jnp.int32, (128, 128), 0) // slots
    col_entry = lax.broadcasted_iota(jnp.int32, (128, 128), 1) // slots
    keep = jnp.where(row_entry == col_entry, live, 0.0)
    bias = jnp.where(keep > 0.0, 0.0, masked)
    return jnp.concatenate([bias, bias], axis=axis)


def slot_softmax(stacked, keys, bias):
    scores = mm_nt(stacked, keys) * (HHD ** (-0.5)) + bias
    return softmax_rows(scores)


def hyper_forward_kernel(
    slots, piece_ref, live_ref, lane_ref, count_ref, param_ref,
    qkv_ref, mixed_ref, second_ref, pre_ref, pool_ref, embed_ref, norm_ref,
):
    tile, width = piece_ref.shape

    @pl.when(pl.program_id(0) == 0)
    def _():
        norm_ref[...] = param_ref[:, param_ref.shape[1] - 128 :].astype(wide_type).T[0:8]

    first, second = half_masks()
    inputs = piece_ref[...].astype(wide_type)
    lead = (norm_hat(inputs)[0] * norm_ref[0:1] + norm_ref[1:2]).astype(low_type)
    for k in range(3):
        part = slice(k * width, (k + 1) * width)
        qkv_ref[:, part] = mm(lead, param_ref[:, part]).astype(low_type)

    for block in range(tile // 128):
        rows = slice(block * 128, (block + 1) * 128)
        bias = slot_mask(lane_ref[:, rows], slots)
        for col in range(0, width, 128):
            stacked = stack_heads(qkv_ref[rows, col : col + 128], first, second)
            keys = qkv_ref[rows, width + col : width + col + 128]
            values = qkv_ref[rows, 2 * width + col : 2 * width + col + 128]
            prob = slot_softmax(stacked, keys, bias).astype(low_type)
            both = jnp.concatenate([prob[:128], prob[128:]], axis=1)
            mixed_ref[rows, col : col + 128] = mm(
                both, stack_heads(values, first, second)
            ).astype(low_type)
    start = 3 * width
    second_in = inputs + mm(mixed_ref[...], param_ref[:, start : start + width])
    second_ref[...] = second_in
    mid = (norm_hat(second_in)[0] * norm_ref[2:3] + norm_ref[3:4]).astype(low_type)
    hidden_count = pre_ref.shape[1]
    start = start + width
    proj = start + hidden_count
    back = proj + embed_ref.shape[1]
    third = second_in
    for col in range(0, hidden_count, width):
        pre = mm(mid, param_ref[:, start + col : start + col + width])
        pre_ref[:, col : col + width] = pre.astype(low_type)
        hidden = (
            0.5 * pre * (1.0 + jnp.tanh(gelu_in * (pre + gelu_cube * pre * pre * pre)))
        ).astype(low_type)
        third = third + mm(hidden, param_ref[:, back + col : back + col + width])
    third = jnp.where(live_ref[...] > 0.0, third, 0.0)
    pooled = jnp.sum(third.reshape(tile // slots, slots, width), axis=1) / count_ref[...]
    pooled = pooled.astype(low_type)
    pool_ref[...] = pooled
    embed_ref[...] = mm(pooled, param_ref[:, proj:back]).astype(low_type)


def hyper_forward(
    params, param_cols, pieces, live_rows, live_lanes, counts, slots, dim
):
    row_count, width = pieces.shape
    tile = 256
    fold = (param_cols - 128 - dim - 4 * width) // 2
    by_row = lambda cols: pl.BlockSpec((tile, cols), lambda i: (i, 0))
    by_entry = lambda cols: pl.BlockSpec((tile // slots, cols), lambda i: (i, 0))
    entries = row_count // slots
    struct = jax.ShapeDtypeStruct
    return pl.pallas_call(
        functools.partial(hyper_forward_kernel, slots),
        grid=(row_count // tile,),
        in_specs=[
            by_row(width),
            by_row(1),
            pl.BlockSpec((1, tile), lambda i: (0, i)),
            by_entry(1),
            pl.BlockSpec((width, param_cols), lambda i: (0, 0), pipeline_mode=pl.Buffered(1)),
        ],
        out_specs=[
            by_row(3 * width), by_row(width), by_row(width), by_row(fold),
            by_entry(width), by_entry(dim), pl.BlockSpec((8, width), lambda i: (0, 0)),
        ],
        out_shape=[
            struct((row_count, 3 * width), low_type),
            struct((row_count, width), low_type),
            struct((row_count, width), wide_type),
            struct((row_count, fold), low_type),
            struct((entries, width), low_type),
            struct((entries, dim), low_type),
            struct((8, width), wide_type),
        ],
        compiler_params=pltpu.CompilerParams(vmem_limit_bytes=vmem_bytes),
        cost_estimate=pl.CostEstimate(
            flops=2 * row_count * width * 12 * width,
            bytes_accessed=2 * params.size + 12 * row_count * width,
            transcendentals=row_count * fold,
        ),
        name="hyper_forward",
    )(pieces, live_rows, live_lanes, counts, params)


def bend_kernel(pre_ref, hidden_ref, slope_ref):
    for col in range(0, pre_ref.shape[1], 512):
        part = slice(col, col + 512)
        pre = pre_ref[:, part].astype(wide_type)
        square = pre * pre
        bend = jnp.tanh(gelu_in * pre * (1.0 + gelu_cube * square))
        hidden_ref[:, part] = (0.5 * pre * (1.0 + bend)).astype(low_type)
        slope = 0.5 * (1.0 + bend) + 0.5 * pre * (1.0 - bend * bend) * gelu_in * (
            1.0 + 3.0 * gelu_cube * square
        )
        slope_ref[:, part] = slope.astype(low_type)


def bends(pre):
    rows, cols = pre.shape
    tile = 256
    spec = pl.BlockSpec((tile, cols), lambda i: (i, 0))
    struct = jax.ShapeDtypeStruct(pre.shape, low_type)
    return pl.pallas_call(
        bend_kernel,
        grid=(rows // tile,),
        in_specs=[spec],
        out_specs=[spec, spec],
        out_shape=[struct, struct],
        cost_estimate=pl.CostEstimate(
            flops=20 * pre.size, bytes_accessed=6 * pre.size, transcendentals=pre.size
        ),
        name="bends",
    )(pre)


def slot_prob_kernel(slots, qkv_ref, live_ref, prob_ref):
    tile = live_ref.shape[0]
    width = qkv_ref.shape[1] // 3
    first, second = half_masks()
    for block in range(tile // 128):
        rows = slice(block * 128, (block + 1) * 128)
        bias = slot_mask(live_ref[rows], slots, 1)
        for col in range(0, width, 128):
            stacked = stack_heads(qkv_ref[rows, col : col + 128], first, second)
            keys = qkv_ref[rows, width + col : width + col + 128]
            scores = mm_nt(keys, stacked) * (HHD ** (-0.5)) + bias
            exp_scores = jnp.exp(scores - jnp.max(scores, axis=0, keepdims=True))
            prob = exp_scores / jnp.sum(exp_scores, axis=0, keepdims=True)
            prob_ref[rows, 2 * col : 2 * col + 256] = prob.astype(low_type)


def slot_probs(qkv, live_rows, slots):
    rows, cols = qkv.shape
    tile = 256
    width = cols // 3
    return pl.pallas_call(
        functools.partial(slot_prob_kernel, slots),
        grid=(rows // tile,),
        in_specs=[
            pl.BlockSpec((tile, cols), lambda i: (i, 0)),
            pl.BlockSpec((tile, 1), lambda i: (i, 0)),
        ],
        out_specs=pl.BlockSpec((tile, 2 * width), lambda i: (i, 0)),
        out_shape=jax.ShapeDtypeStruct((rows, 2 * width), low_type),
        cost_estimate=pl.CostEstimate(
            flops=600 * rows * width, bytes_accessed=10 * rows * width,
            transcendentals=2 * rows * width,
        ),
        name="slot_probs",
    )(qkv, live_rows)


def hyper_backward_kernel(
    slots, grad_ref, pool_ref, piece_ref, live_ref, count_ref, qkv_ref, mixed_ref, second_ref,
    hidden_ref, slope_ref, prob_ref, param_ref, norm_ref, out_ref,
    sums, norm_sums, mix_grad, qkv_grad, pre_grad,
):
    tile, width = piece_ref.shape
    hidden_count = hidden_ref.shape[1]
    dim = grad_ref.shape[1]
    out_at = 3 * width
    in_at = out_at + width
    proj = in_at + hidden_count
    back = proj + dim
    first, second = half_masks()

    @pl.when(pl.program_id(0) == 0)
    def _():
        sums[...] = jnp.zeros_like(sums)
        norm_sums[...] = jnp.zeros_like(norm_sums)

    embed_grad = grad_ref[...]
    pooled = pool_ref[...]
    for col in range(0, dim, width):
        part = slice(proj + col, proj + col + width)
        sums[:, part] += mm_tn(pooled, embed_grad[:, col : col + width])
    pool_grad = mm_nt(embed_grad, param_ref[:, proj:back]) / count_ref[...]
    spread = jnp.broadcast_to(pool_grad[:, None, :], (tile // slots, slots, width))
    third_grad = jnp.where(live_ref[...] > 0.0, spread.reshape(tile, width), 0.0)
    back_in = third_grad.astype(low_type)
    for col in range(0, hidden_count, width):
        hidden_grad = mm_nt(back_in, param_ref[:, back + col : back + col + width])
        slope = slope_ref[:, col : col + width].astype(wide_type)
        pre_grad[:, col : col + width] = (slope * hidden_grad).astype(low_type)
        part = slice(back + col, back + col + width)
        sums[:, part] += mm_tn(back_in, hidden_ref[:, col : col + width])
    second_in = second_ref[...]
    hat, scale = norm_hat(second_in)
    mid = (hat * norm_ref[2:3] + norm_ref[3:4]).astype(low_type)
    mid_grad = jnp.zeros((tile, width), wide_type)
    for col in range(0, hidden_count, width):
        part = slice(in_at + col, in_at + col + width)
        grads = pre_grad[:, col : col + width]
        sums[:, part] += mm_tn(mid, grads)
        mid_grad = mid_grad + mm_nt(grads, param_ref[:, part])
    norm_sums[2:3] += jnp.sum(mid_grad * hat, axis=0, keepdims=True)
    norm_sums[3:4] += jnp.sum(mid_grad, axis=0, keepdims=True)
    second_grad = third_grad + norm_back(hat, scale, mid_grad * norm_ref[2:3])
    out_in = second_grad.astype(low_type)
    sums[:, out_at:in_at] += mm_tn(mixed_ref[...], out_in)
    mix_grad[...] = mm_nt(out_in, param_ref[:, out_at:in_at]).astype(low_type)

    score_scale = HHD ** (-0.5)
    low_lane = lax.broadcasted_iota(jnp.int32, (1, 128), 1) < HHD
    for block in range(tile // 128):
        rows = slice(block * 128, (block + 1) * 128)
        for col in range(0, width, 128):
            stacked = stack_heads(qkv_ref[rows, col : col + 128], first, second)
            keys = qkv_ref[rows, width + col : width + col + 128]
            values = qkv_ref[rows, 2 * width + col : 2 * width + col + 128]
            prob_low = prob_ref[rows, 2 * col : 2 * col + 256]
            prob = prob_low.astype(wide_type)
            grads = stack_heads(mix_grad[rows, col : col + 128], first, second)
            prob_grad = mm_nt(values, grads)
            score_grad = prob * (prob_grad - jnp.sum(prob * prob_grad, axis=0, keepdims=True))
            score_grad = score_grad.astype(low_type)
            key_grad = mm(score_grad, stacked) * score_scale
            value_grad = mm(prob_low, grads)
            both = mm_tn(score_grad, keys)
            query_grad = jnp.where(low_lane, both[:128], both[128:]) * score_scale
            qkv_grad[rows, col : col + 128] = query_grad.astype(low_type)
            qkv_grad[rows, width + col : width + col + 128] = key_grad.astype(low_type)
            qkv_grad[rows, 2 * width + col : 2 * width + col + 128] = value_grad.astype(low_type)

    inputs = piece_ref[...].astype(wide_type)
    hat_one = norm_hat(inputs)[0]
    lead = (hat_one * norm_ref[0:1] + norm_ref[1:2]).astype(low_type)
    lead_grad = jnp.zeros((tile, width), wide_type)
    for col in range(0, 3 * width, width):
        part = slice(col, col + width)
        grads = qkv_grad[:, part]
        sums[:, part] += mm_tn(lead, grads)
        lead_grad = lead_grad + mm_nt(grads, param_ref[:, part])
    norm_sums[0:1] += jnp.sum(lead_grad * hat_one, axis=0, keepdims=True)
    norm_sums[1:2] += jnp.sum(lead_grad, axis=0, keepdims=True)

    @pl.when(pl.program_id(0) == pl.num_programs(0) - 1)
    def _():
        out_ref[:, :back] = sums[:, :back].astype(low_type)
        for col in range(back, back + hidden_count, width):
            out_ref[:, col : col + width] = sums[:, col : col + width].T.astype(low_type)
        out_ref[:, back + hidden_count :] = norm_sums[...].T.astype(low_type)


def hyper_backward(
    params, param_cols, norms, embed_grad, pooled, pieces, live_rows, counts, qkv, mixed,
    second_in, hidden, slope, probs, slots,
):
    row_count, width = pieces.shape
    dim = embed_grad.shape[1]
    fold = hidden.shape[1]
    tile = 512
    by_row = lambda cols: pl.BlockSpec((tile, cols), lambda i: (i, 0))
    by_entry = lambda cols: pl.BlockSpec((tile // slots, cols), lambda i: (i, 0))
    whole = lambda shape: pl.BlockSpec(shape, lambda i: (0, 0), pipeline_mode=pl.Buffered(1))
    return pl.pallas_call(
        functools.partial(hyper_backward_kernel, slots),
        grid=(row_count // tile,),
        in_specs=[
            by_entry(dim),
            by_entry(width),
            by_row(width),
            by_row(1),
            by_entry(1),
            by_row(3 * width),
            by_row(width),
            by_row(width),
            by_row(fold),
            by_row(fold),
            by_row(2 * width),
            whole((width, param_cols)),
            whole(norms.shape),
        ],
        out_specs=whole((width, param_cols)),
        out_shape=jax.ShapeDtypeStruct((width, param_cols), low_type),
        scratch_shapes=[
            pltpu.VMEM((width, param_cols - 128), wide_type),
            pltpu.VMEM((128, width), wide_type),
            pltpu.VMEM((tile, width), low_type),
            pltpu.VMEM((tile, 3 * width), low_type),
            pltpu.VMEM((tile, fold), low_type),
        ],
        compiler_params=pltpu.CompilerParams(vmem_limit_bytes=vmem_bytes),
        cost_estimate=pl.CostEstimate(
            flops=4 * row_count * width * 12 * width,
            bytes_accessed=4 * params.size + 24 * row_count * width,
            transcendentals=row_count * fold,
        ),
        name="hyper_backward",
    )(
        embed_grad, pooled, pieces, live_rows, counts, qkv, mixed, second_in, hidden, slope, probs,
        params, norms,
    )


def turn(values_in, cosine, sine_low, sine_high):
    parts = []
    for col in range(0, values_in.shape[1], 128):
        part = values_in[:, col : col + 128]
        parts.append(
            part * cosine
            + pltpu.roll(part, 96, axis=1) * sine_low
            + pltpu.roll(part, 32, axis=1) * sine_high
        )
    return parts[0] if len(parts) == 1 else jnp.concatenate(parts, axis=1)


def project_both_kernel(
    scalar_ref, embed_ref, gain_ref, kcos_ref, klow_ref, khigh_ref, wkv_ref, both_ref, lead_ref
):
    @pl.when(pl.program_id(0) == 0)
    def _():
        inputs = embed_ref[...].astype(wide_type)
        lead_ref[...] = rms_norm(inputs, gain_ref[0:1]).astype(low_type)

    chunk_count, _, chunk, _ = wkv_ref.shape
    both = jnp.zeros(both_ref.shape, wide_type)
    for k in range(chunk_count):
        both = both + mm(lead_ref[:, k * chunk : (k + 1) * chunk], wkv_ref[k, 0])
    both_ref[...] = turn(both, kcos_ref[...], klow_ref[...], khigh_ref[...]).astype(low_type)


def project_both(scalars, embed, gains, tables, wkv_all):
    local, dim = embed.shape
    chunk_count, ranks, chunk, _ = wkv_all.shape
    whole = lambda shape: pl.BlockSpec(shape, lambda t, place: (0, 0))
    return pl.pallas_call(
        project_both_kernel,
        grid_spec=pltpu.PrefetchScalarGridSpec(
            num_scalar_prefetch=1,
            grid=(ranks,),
            in_specs=[whole((local, dim)), whole(gains.shape)]
            + [whole((local, 128))] * 3
            + [
                pl.BlockSpec(
                    (chunk_count, 1, chunk, 128),
                    lambda t, place: (0, lax.rem(place[2] - t + ranks, ranks), 0, 0),
                )
            ],
            out_specs=[
                pl.BlockSpec((local, 128), lambda t, place: (0, t)), whole((local, dim)),
            ],
        ),
        out_shape=[
            jax.ShapeDtypeStruct((local, ranks * 128), low_type),
            jax.ShapeDtypeStruct((local, dim), low_type),
        ],
        compiler_params=pltpu.CompilerParams(vmem_limit_bytes=vmem_bytes),
        cost_estimate=pl.CostEstimate(
            flops=2 * local * dim * ranks * 128,
            bytes_accessed=2 * dim * ranks * 128 + 4 * local * dim,
            transcendentals=0,
        ),
        name="project_both",
    )(scalars, embed, gains, *tables[3:], wkv_all)


def own_or_rest(own_ref, rest_ref, use):
    @pl.when(pl.program_id(0) == 0)
    def _():
        use(own_ref)

    @pl.when(pl.program_id(0) > 0)
    def _():
        use(rest_ref)


def weight_specs(own_all):
    chunk_count, _, chunk, cols = own_all.shape
    shape = (chunk_count, 1, chunk, cols)
    return [
        pl.BlockSpec(shape, lambda t: (0, 0, 0, 0)),
        pl.BlockSpec(shape, lambda t: (0, jnp.maximum(t - 1, 0), 0, 0)),
    ]


def block_specs(local, count):
    return [
        pl.BlockSpec((local, 128), lambda t, k=k: (0, lax.rem(t - k + count, count)))
        for k in range(count)
    ]


def project_kernel(lead_ref, cos_ref, low_ref, high_ref, own_ref, rest_ref, query_ref):
    def use(wq_ref):
        chunk_count, _, chunk, cols = wq_ref.shape
        query = jnp.zeros((lead_ref.shape[0], cols), wide_type)
        for k in range(chunk_count):
            query = query + mm(lead_ref[:, k * chunk : (k + 1) * chunk], wq_ref[k, 0])
        query = turn(query, cos_ref[...], low_ref[...], high_ref[...])
        query_ref[...] = (query * (LHD ** (-0.5))).astype(low_type)

    own_or_rest(own_ref, rest_ref, use)


def project(lead, tables, own_all, rest_all):
    local, dim = lead.shape
    ranks = rest_all.shape[1] + 1
    cols = own_all.shape[3]
    whole = lambda shape: pl.BlockSpec(shape, lambda t: (0, 0))
    return pl.pallas_call(
        project_kernel,
        grid=(ranks,),
        in_specs=[whole((local, dim))] + [whole((local, 128))] * 3 + weight_specs(own_all),
        out_specs=pl.BlockSpec((local, cols), lambda t: (0, t)),
        out_shape=jax.ShapeDtypeStruct((local, ranks * cols), low_type),
        compiler_params=pltpu.CompilerParams(vmem_limit_bytes=vmem_bytes),
        cost_estimate=pl.CostEstimate(
            flops=2 * local * dim * ranks * cols,
            bytes_accessed=2 * dim * ranks * cols + 4 * local * dim,
            transcendentals=0,
        ),
        name="project",
    )(lead, *tables[:3], own_all, rest_all)


def key_place(start, index, local, seq_len):
    block = index // local
    return lax.rem(start + seq_len - block * local, seq_len) + index - block * local


def attend_kernel(
    scalar_ref, query_ref, own_ref, one_ref, two_ref, three_ref, mixed_ref, log_ref, bias_ref
):
    local = query_ref.shape[0]
    seq_len = bias_ref.shape[1]

    @pl.when(pl.program_id(0) == 0)
    def _():
        row = scalar_ref[0] + lax.broadcasted_iota(jnp.int32, (local, seq_len), 0)
        col = lax.broadcasted_iota(jnp.int32, (1, seq_len), 1)
        col = key_place(scalar_ref[0], col, local, seq_len)
        allowed = jnp.where(col <= row, jnp.where(col < scalar_ref[1], 0.0, masked), masked)
        bias_ref[...] = allowed

    first, second = half_masks()
    lane = lax.broadcasted_iota(jnp.int32, (1, 128), 1)
    both = jnp.concatenate([own_ref[...], one_ref[...], two_ref[...], three_ref[...]], axis=0)
    swapped = pltpu.roll(both.astype(wide_type), LHD, axis=1).astype(low_type)
    keys = both * first + swapped * second
    value_low = swapped * first
    value_high = both * second
    logs = jnp.zeros((local, 128), wide_type)
    for pair in range(query_ref.shape[1] // 128):
        cols = slice(pair * 128, (pair + 1) * 128)
        mixed = jnp.zeros((local, 128), wide_type)
        for half, (mask, values) in enumerate(((first, value_low), (second, value_high))):
            scores = mm_nt(query_ref[:, cols] * mask, keys) + bias_ref[...]
            row_top = jnp.max(scores, axis=-1, keepdims=True)
            exp_scores = jnp.exp(scores - row_top)
            exp_total = jnp.sum(exp_scores, axis=-1, keepdims=True)
            prob = (exp_scores * (1.0 / exp_total)).astype(low_type)
            mixed = mixed + mm(prob, values)
            logs = jnp.where(lane == 2 * pair + half, row_top + jnp.log(exp_total), logs)
        mixed_ref[:, cols] = mixed.astype(low_type)
    log_ref[...] = logs.T[0:8]


def attend(scalars, query, blocks):
    local, dim = query.shape
    ranks = len(blocks)
    seq_len = local * ranks
    cols = dim // ranks
    return pl.pallas_call(
        attend_kernel,
        grid=(ranks,),
        in_specs=[
            pl.BlockSpec(memory_space=pltpu.SMEM),
            pl.BlockSpec((local, cols), lambda t: (0, t)),
        ]
        + block_specs(local, ranks),
        out_specs=[
            pl.BlockSpec((local, cols), lambda t: (0, t)),
            pl.BlockSpec((8, local), lambda t: (t, 0)),
        ],
        out_shape=[
            jax.ShapeDtypeStruct((local, dim), low_type),
            jax.ShapeDtypeStruct((8 * ranks, local), wide_type),
        ],
        scratch_shapes=[pltpu.VMEM((local, seq_len), wide_type)],
        compiler_params=pltpu.CompilerParams(vmem_limit_bytes=vmem_bytes),
        cost_estimate=pl.CostEstimate(
            flops=16 * local * seq_len * dim,
            bytes_accessed=8 * local * dim,
            transcendentals=local * seq_len * dim // LHD,
        ),
        name="attend",
    )(scalars, query, *blocks)


def attend_out_kernel(mixed_ref, embed_ref, gain_ref, wo_own, wo_rest, mid_ref, lead_ref, total):
    @pl.when(pl.program_id(0) == 0)
    def _():
        total[...] = embed_ref[...].astype(wide_type)

    def use(wo_ref):
        chunk_count, _, chunk, cols = wo_ref.shape
        for k in range(chunk_count):
            part = slice(k * chunk, (k + 1) * chunk)
            for col in range(0, cols, chunk):
                total[:, part] += mm(
                    mixed_ref[:, col : col + chunk], wo_ref[k, 0, :, col : col + chunk]
                )

    own_or_rest(wo_own, wo_rest, use)

    @pl.when(pl.program_id(0) == pl.num_programs(0) - 1)
    def _():
        mid_ref[...] = total[...]
        lead_ref[...] = rms_norm(total[...], gain_ref[1:2]).astype(low_type)


def attend_out(mixed, embed, gains, own_all, rest_all):
    local, dim = embed.shape
    ranks = rest_all.shape[1] + 1
    cols = own_all.shape[3]
    whole = lambda shape: pl.BlockSpec(shape, lambda t: (0, 0))
    return pl.pallas_call(
        attend_out_kernel,
        grid=(ranks,),
        in_specs=[
            pl.BlockSpec((local, cols), lambda t: (0, t)), whole((local, dim)), whole(gains.shape),
        ]
        + weight_specs(own_all),
        out_specs=[whole((local, dim)), whole((local, dim))],
        out_shape=[
            jax.ShapeDtypeStruct((local, dim), wide_type),
            jax.ShapeDtypeStruct((local, dim), low_type),
        ],
        scratch_shapes=[pltpu.VMEM((local, dim), wide_type)],
        compiler_params=pltpu.CompilerParams(vmem_limit_bytes=vmem_bytes),
        cost_estimate=pl.CostEstimate(
            flops=2 * local * dim * dim,
            bytes_accessed=2 * dim * dim + 8 * local * dim,
            transcendentals=0,
        ),
        name="attend_out",
    )(mixed, embed, gains, own_all, rest_all)


def attend_back_kernel(
    scalar_ref, mlp_ref, cot_ref, mid_ref, gain_ref, query_ref, own_ref, one_ref, two_ref,
    three_ref, mixed_ref, log_ref, cos_ref, low_ref, high_ref, wo_own, wo_rest,
    resid_ref, qgrad_ref, own_grad, one_grad, two_grad, three_grad, low_grad, bias_ref, out_grad,
):
    local = query_ref.shape[0]
    seq_len = bias_ref.shape[0]

    @pl.when(pl.program_id(0) == 0)
    def _():
        row = scalar_ref[0] + lax.broadcasted_iota(jnp.int32, (local, 1), 0)
        own = jnp.where(row < scalar_ref[1], cot_ref[...].astype(wide_type), 0.0)
        grad = own + rms_back(mid_ref[...], gain_ref[1:2], mlp_ref[...].astype(wide_type))
        resid_ref[...] = grad
        low_grad[...] = grad.astype(low_type)
        col = scalar_ref[0] + lax.broadcasted_iota(jnp.int32, (seq_len, local), 1)
        key = lax.broadcasted_iota(jnp.int32, (seq_len, 1), 0)
        key = key_place(scalar_ref[0], key, local, seq_len)
        bias_ref[...] = jnp.where(
            key <= col, jnp.where(key < scalar_ref[1], 0.0, masked), masked
        )

    def use(wo_ref):
        chunk_count, _, chunk, cols = wo_ref.shape
        for col in range(0, cols, chunk):
            part_sum = jnp.zeros((local, chunk), wide_type)
            for k in range(chunk_count):
                part_sum = part_sum + mm_nt(
                    low_grad[:, k * chunk : (k + 1) * chunk], wo_ref[k, 0, :, col : col + chunk]
                )
            out_grad[:, col : col + chunk] = part_sum.astype(low_type)

    own_or_rest(wo_own, wo_rest, use)
    first, second = half_masks()
    lane = lax.broadcasted_iota(jnp.int32, (1, 128), 1)
    low_lane = lane < LHD
    both = jnp.concatenate([own_ref[...], one_ref[...], two_ref[...], three_ref[...]], axis=0)
    swapped = pltpu.roll(both.astype(wide_type), LHD, axis=1).astype(low_type)
    keys = both * first + swapped * second
    values = swapped * first + both * second
    key_low = both * first
    key_high = swapped * second
    sums = jnp.zeros((local, 128), wide_type)
    for pair in range(query_ref.shape[1] // 128):
        part = slice(pair * 128, (pair + 1) * 128)
        product = mixed_ref[:, part].astype(wide_type) * out_grad[:, part].astype(wide_type)
        one = jnp.sum(jnp.where(low_lane, product, 0.0), axis=-1, keepdims=True)
        two = jnp.sum(jnp.where(low_lane, 0.0, product), axis=-1, keepdims=True)
        sums = jnp.where(lane == 2 * pair, one, sums)
        sums = jnp.where(lane == 2 * pair + 1, two, sums)
    sums = sums.T[0:8]
    key_sum = jnp.zeros((seq_len, 128), wide_type)
    value_sum = jnp.zeros((seq_len, 128), wide_type)
    for pair in range(query_ref.shape[1] // 128):
        part = slice(pair * 128, (pair + 1) * 128)
        query_grad = jnp.zeros((local, 128), wide_type)
        for half, (mask, key_side) in enumerate(((first, key_low), (second, key_high))):
            head = 2 * pair + half
            query = query_ref[:, part] * mask
            grads = out_grad[:, part] * mask
            scores = mm_nt(keys, query) + bias_ref[...]
            prob = jnp.exp(scores - log_ref[head : head + 1])
            prob_grad = mm_nt(values, grads)
            score_grad = (prob * (prob_grad - sums[head : head + 1])).astype(low_type)
            key_sum = key_sum + mm(score_grad, query)
            value_sum = value_sum + mm(prob.astype(low_type), grads)
            query_grad = query_grad + mm_tn(score_grad, key_side)
        query_grad = query_grad * (LHD ** (-0.5))
        spun = query_grad * low_ref[...]
        spin = query_grad * high_ref[...]
        query_grad = (
            query_grad * cos_ref[...]
            + pltpu.roll(spin, 96, axis=1)
            + pltpu.roll(spun, 32, axis=1)
        )
        qgrad_ref[:, part] = query_grad.astype(low_type)
    key_sum = key_sum + pltpu.roll(key_sum, LHD, axis=1)
    value_sum = value_sum + pltpu.roll(value_sum, LHD, axis=1)
    both_grad = jnp.where(low_lane, key_sum, value_sum).astype(low_type)
    for k, ref in enumerate((own_grad, one_grad, two_grad, three_grad)):
        ref[...] = both_grad[k * local : (k + 1) * local]


def attend_back(
    scalars, mlp_grad, cot_own, mid, gains, query, blocks, mixed, logs, tables, own_all, rest_all
):
    local, dim = mid.shape
    ranks = len(blocks)
    seq_len = local * ranks
    cols = own_all.shape[3]
    whole = lambda shape: pl.BlockSpec(shape, lambda t: (0, 0))
    by_block = block_specs(local, ranks)
    by_rank = pl.BlockSpec((local, cols), lambda t: (0, t))
    return pl.pallas_call(
        attend_back_kernel,
        grid=(ranks,),
        in_specs=[
            pl.BlockSpec(memory_space=pltpu.SMEM),
            whole((local, dim)),
            whole((local, dim)),
            whole((local, dim)),
            whole(gains.shape),
            by_rank,
        ]
        + by_block
        + [
            by_rank,
            pl.BlockSpec((8, local), lambda t: (t, 0)),
            whole((local, 128)),
            whole((local, 128)),
            whole((local, 128)),
        ]
        + weight_specs(own_all),
        out_specs=[
            whole((local, dim)),
            by_rank,
        ]
        + by_block,
        out_shape=[
            jax.ShapeDtypeStruct((local, dim), wide_type),
            jax.ShapeDtypeStruct((local, ranks * cols), low_type),
        ]
        + [jax.ShapeDtypeStruct((local, ranks * 128), low_type)] * len(blocks),
        scratch_shapes=[
            pltpu.VMEM((local, dim), low_type),
            pltpu.VMEM((seq_len, local), wide_type),
            pltpu.VMEM((local, cols), low_type),
        ],
        compiler_params=pltpu.CompilerParams(vmem_limit_bytes=vmem_bytes),
        cost_estimate=pl.CostEstimate(
            flops=2 * local * dim * dim + 40 * local * seq_len * dim,
            bytes_accessed=2 * dim * dim + 20 * local * dim,
            transcendentals=local * seq_len * dim // LHD,
        ),
        name="attend_back",
    )(
        scalars, mlp_grad, cot_own, mid, gains, query, *blocks, mixed, logs, *tables[:3], own_all,
        rest_all,
    )


def project_back_query_kernel(qgrad_ref, own_ref, rest_ref, total_ref):
    @pl.when(pl.program_id(0) == 0)
    def _():
        total_ref[...] = jnp.zeros_like(total_ref)

    def use(wq_ref):
        chunk_count, _, chunk, _ = wq_ref.shape
        for k in range(chunk_count):
            total_ref[:, k * chunk : (k + 1) * chunk] += mm_nt(qgrad_ref[...], wq_ref[k, 0])

    own_or_rest(own_ref, rest_ref, use)


def project_back_query(query_grad, own_all, rest_all):
    chunk_count, _, chunk, _ = own_all.shape
    ranks = rest_all.shape[1] + 1
    cols = own_all.shape[3]
    local = query_grad.shape[0]
    dim = chunk_count * chunk
    return pl.pallas_call(
        project_back_query_kernel,
        grid=(ranks,),
        in_specs=[pl.BlockSpec((local, cols), lambda t: (0, t))] + weight_specs(own_all),
        out_specs=pl.BlockSpec((local, dim), lambda t: (0, 0)),
        out_shape=jax.ShapeDtypeStruct((local, dim), wide_type),
        compiler_params=pltpu.CompilerParams(vmem_limit_bytes=vmem_bytes),
        cost_estimate=pl.CostEstimate(
            flops=2 * local * dim * ranks * cols,
            bytes_accessed=2 * dim * ranks * cols + 8 * local * dim,
            transcendentals=0,
        ),
        name="project_back_query",
    )(query_grad, own_all, rest_all)


def project_back_kernel(
    scalar_ref, embed_ref, gain_ref, resid_ref, part_ref, kcos_ref, klow_ref, khigh_ref, own_ref, one_ref,
    two_ref, three_ref, wkv_ref, grad_ref, total,
):
    step = pl.program_id(0)

    @pl.when(step == 0)
    def _():
        total[...] = part_ref[...]

    both = own_ref[...].astype(wide_type)
    for ref in (one_ref, two_ref, three_ref):
        both = both + ref[...].astype(wide_type)
    both = (
        both * kcos_ref[...]
        + pltpu.roll(both * khigh_ref[...], 96, axis=1)
        + pltpu.roll(both * klow_ref[...], 32, axis=1)
    ).astype(low_type)
    chunk_count, _, chunk, _ = wkv_ref.shape
    for k in range(chunk_count):
        total[:, k * chunk : (k + 1) * chunk] += mm_nt(both, wkv_ref[k, 0])

    @pl.when(step == pl.num_programs(0) - 1)
    def _():
        grad = resid_ref[...] + rms_back(
            embed_ref[...].astype(wide_type), gain_ref[0:1], total[...]
        )
        grad_ref[...] = grad.astype(low_type)


def project_back(scalars, embed, gains, resid, part, tables, blocks, wkv_all):
    local, dim = embed.shape
    chunk_count, ranks, chunk, _ = wkv_all.shape
    whole = lambda shape: pl.BlockSpec(shape, lambda t, place: (0, 0))
    return pl.pallas_call(
        project_back_kernel,
        grid_spec=pltpu.PrefetchScalarGridSpec(
            num_scalar_prefetch=1,
            grid=(ranks,),
            in_specs=[whole((local, dim)), whole(gains.shape)]
            + [whole((local, dim))] * 2
            + [whole((local, 128))] * 3
            + [pl.BlockSpec((local, 128), lambda t, place: (0, t))] * len(blocks)
            + [
                pl.BlockSpec(
                    (chunk_count, 1, chunk, 128),
                    lambda t, place: (0, lax.rem(place[2] - t + ranks, ranks), 0, 0),
                )
            ],
            out_specs=whole((local, dim)),
            scratch_shapes=[pltpu.VMEM((local, dim), wide_type)],
        ),
        out_shape=jax.ShapeDtypeStruct((local, dim), low_type),
        compiler_params=pltpu.CompilerParams(vmem_limit_bytes=vmem_bytes),
        cost_estimate=pl.CostEstimate(
            flops=2 * local * dim * ranks * 128,
            bytes_accessed=2 * dim * ranks * 128 + 16 * local * dim,
            transcendentals=0,
        ),
        name="project_back",
    )(scalars, embed, gains, resid, part, *tables[3:], *blocks, wkv_all)


def join_kernel(low_ref, high_ref, out_ref):
    half = low_ref.shape[1]
    out_ref[:, :half] = low_ref[...]
    out_ref[:, half:] = high_ref[...]


def join_columns(low, high):
    rows, cols = low.shape
    spec = pl.BlockSpec((rows // 4, cols), lambda i: (i, 0))
    return pl.pallas_call(
        join_kernel,
        grid=(4,),
        in_specs=[spec, spec],
        out_specs=pl.BlockSpec((rows // 4, 2 * cols), lambda i: (i, 0)),
        out_shape=jax.ShapeDtypeStruct((rows, 2 * cols), low.dtype),
        cost_estimate=pl.CostEstimate(flops=0, bytes_accessed=8 * low.size, transcendentals=0),
        name="join_columns",
    )(low, high)


def gather_sum_kernel(cuts, place_ref, own_ref, *refs):
    came, outs = refs[: len(refs) - len(cuts)], refs[len(refs) - len(cuts) :]
    *total_refs, square_ref = outs
    squares = jnp.zeros((1, 1), wide_type)
    for total_ref, start, end in zip(total_refs, cuts[:-1], cuts[1:]):
        total = own_ref[0, :, start:end].astype(wide_type)
        for ref in came:
            total = total + ref[:, start:end].astype(wide_type)
        total_ref[...] = total
        part = jnp.sum(total * total, axis=1, keepdims=True)
        squares = squares + jnp.sum(part, axis=0, keepdims=True)
    square_ref[...] = jnp.broadcast_to(squares, square_ref.shape)


def gather_sum(place, blocks, came, cuts):
    _, rows, cols = blocks.shape
    whole = lambda shape: pl.BlockSpec(shape, lambda i, place: (0, 0))
    shapes = [(rows, end - start) for start, end in zip(cuts[:-1], cuts[1:])] + [(8, 128)]
    return pl.pallas_call(
        functools.partial(gather_sum_kernel, tuple(cuts)),
        grid_spec=pltpu.PrefetchScalarGridSpec(
            num_scalar_prefetch=1,
            grid=(1,),
            in_specs=[pl.BlockSpec((1, rows, cols), lambda i, place: (place[0], 0, 0))]
            + [whole((rows, cols))] * len(came),
            out_specs=[whole(shape) for shape in shapes],
        ),
        out_shape=[jax.ShapeDtypeStruct(shape, wide_type) for shape in shapes],
        name="gather_sum",
    )(place, blocks, *came)


def update_kernel(count, scalar_ref, square_ref, *refs):
    ins, outs = refs[: 4 * count], refs[4 * count :]
    first_fix, second_fix = scalar_ref[0], scalar_ref[1]
    clip_scale = jnp.minimum(1.0, clip_max / (jnp.sqrt(square_ref[0:1, 0:1]) + 1e-06))
    for k in range(count):
        grad, master, first_old, second_old = (ins[j * count + k][...] for j in range(4))
        clipped = grad * clip_scale
        moment = beta_one * first_old + (1.0 - beta_one) * clipped
        square = beta_two * second_old + (1.0 - beta_two) * clipped * clipped
        update = moment / first_fix / (jnp.sqrt(square / second_fix) + adam_eps)
        if k < count - 1:
            new = master - learn_rate * (update + weight_decay * master)
        else:
            new = master - norms_rate * update
        outs[k][...] = new
        outs[count + k][...] = moment
        outs[2 * count + k][...] = square


def update_params(scalars, squares, grads, masters, firsts, seconds):
    count = len(grads)
    arrays = [*grads, *masters, *firsts, *seconds]
    vmem = pl.BlockSpec(memory_space=pltpu.VMEM)
    return pl.pallas_call(
        functools.partial(update_kernel, count),
        in_specs=[pl.BlockSpec(memory_space=pltpu.SMEM)] + [vmem] * (len(arrays) + 1),
        out_specs=[vmem] * (3 * count),
        out_shape=[jax.ShapeDtypeStruct(x.shape, wide_type) for x in masters] * 3,
        name="update_params",
    )(scalars, squares, *arrays)


def feed_kernel(
    place_ref, rows_ref, grad_ref, weight_ref, part_ref, product_ref, gate, up, gate_grad, up_grad
):
    step = pl.program_id(0)
    half = pl.num_programs(0) // 2
    depth = weight_ref.shape[1]

    @pl.when(step < half)
    def _():
        part = rows_ref[:, pl.ds(pl.multiple_of(step * depth, depth), depth)]

        @pl.when(step == 0)
        def _():
            gate[...] = mm(part, weight_ref[0])
            up[...] = mm(part, weight_ref[1])

        @pl.when(step > 0)
        def _():
            gate[...] += mm(part, weight_ref[0])
            up[...] += mm(part, weight_ref[1])

    @pl.when(step == half)
    def _():
        gate_val, up_val, grad = gate[...], up[...], grad_ref[...].astype(wide_type)
        sigma = 1.0 / (1.0 + jnp.exp(-gate_val))
        swish = gate_val * sigma
        product_ref[...] = (swish * up_val).astype(low_type)
        up_grad[...] = (swish * grad).astype(low_type)
        slope = sigma * (1.0 + gate_val * (1.0 - sigma))
        gate_grad[...] = (slope * up_val * grad).astype(low_type)

    @pl.when(step >= half)
    def _():
        part_ref[...] = (
            mm_nt(gate_grad[...], weight_ref[0]) + mm_nt(up_grad[...], weight_ref[1])
        ).astype(low_type)


def feed(place, rows_in, product_grad, w_gate_up):
    local, dim = rows_in.shape
    hidden = w_gate_up.shape[2]
    depth = 512
    half = dim // depth
    return pl.pallas_call(
        feed_kernel,
        grid_spec=pltpu.PrefetchScalarGridSpec(
            num_scalar_prefetch=1,
            grid=(2 * half,),
            in_specs=[
                pl.BlockSpec((local, dim), lambda i, place: (0, 0)),
                pl.BlockSpec((local, hidden), lambda i, place: (place[0], 0)),
                pl.BlockSpec((2, depth, hidden), lambda i, place: (0, lax.rem(i, half), 0)),
            ],
            out_specs=[
                pl.BlockSpec((local, depth), lambda i, place: (0, jnp.maximum(i - half, 0))),
                pl.BlockSpec((local, hidden), lambda i, place: (0, 0)),
            ],
            scratch_shapes=[
                pltpu.VMEM((local, hidden), wide_type),
                pltpu.VMEM((local, hidden), wide_type),
                pltpu.VMEM((local, hidden), low_type),
                pltpu.VMEM((local, hidden), low_type),
            ],
        ),
        out_shape=[
            jax.ShapeDtypeStruct((local, dim), low_type),
            jax.ShapeDtypeStruct((local, hidden), low_type),
        ],
        compiler_params=pltpu.CompilerParams(vmem_limit_bytes=vmem_bytes),
        cost_estimate=pl.CostEstimate(
            flops=8 * local * dim * hidden,
            bytes_accessed=4 * w_gate_up.size,
            transcendentals=local * hidden,
        ),
        name="feed",
    )(place, rows_in, product_grad, w_gate_up)


def shift(values_in, step, first, last, ranks):
    pairs = [(k, k + step) for k in range(first, last + 1) if 0 <= k + step < ranks]
    return lax.ppermute(values_in, "tensor", pairs)


def scatter_sum(joined, tensor_ranks, cuts):
    bits = lax.axis_size("dp").bit_length() - 1
    place = lax.axis_index("dp")
    size = lax.axis_size("dp")
    cols = joined.shape[1]
    depth = joined.shape[0] // size
    split = cols // 256 * 128

    def halve(block, spans, bit):
        axis = spans.index(bit)
        mine = (place >> bit) & 1
        away = lax.dynamic_index_in_dim(block, 1 - mine, axis, keepdims=False)
        kept = lax.dynamic_index_in_dim(block, mine, axis, keepdims=False)
        came = lax.ppermute(away, "dp", [(k, k ^ (1 << bit)) for k in range(size)])
        total = kept.astype(wide_type) + came.astype(wide_type)
        return total.astype(low_type), spans[:axis] + spans[axis + 1 :]

    spans = list(range(bits - 1, -1, -1))
    block = joined.reshape((2,) * bits + (depth, cols))
    block, spans = halve(block, spans, 0)
    parts = []
    for index, part in enumerate((block[..., :split], block[..., split:])):
        left = list(spans)
        order = list(reversed(spans)) if index == 0 else list(spans)
        for bit in order:
            part, left = halve(part, left, bit)
        parts.append(part)
    block = jnp.concatenate(parts, axis=1).reshape(tensor_ranks, depth // tensor_ranks, cols)
    rank = lax.axis_index("tensor")
    came = []
    for k in range(1, tensor_ranks):
        away = lax.dynamic_index_in_dim(block, (rank + k) % tensor_ranks, 0, keepdims=False)
        pairs = [(j, (j + k) % tensor_ranks) for j in range(tensor_ranks)]
        came.append(lax.ppermute(away, "tensor", pairs))
    *totals, squares = gather_sum(rank.astype(jnp.int32)[None], block, came, cuts)
    return totals, squares


def on_device(
    piece_table,
    piece_ids,
    piece_counts,
    text_ids,
    text_lengths,
    lm_gains,
    w_query,
    w_kv,
    w_attn_out,
    w_gate_up,
    w_down,
    cotangent,
    step_count,
    hyper_qkv,
    hyper_out,
    hyper_in,
    hyper_back,
    hyper_proj,
    hyper_norms,
    first_qkv,
    first_out,
    first_in,
    first_back,
    first_proj,
    first_norms,
    second_qkv,
    second_out,
    second_in,
    second_back,
    second_proj,
    second_norms,
):
    axes = ("dp", "tensor")
    rank = lax.axis_index("tensor")
    ranks = lax.axis_size("tensor")
    seq_len = text_ids.shape[1]
    local = seq_len // ranks
    length = text_lengths[0]
    gains = lm_gains.astype(jnp.float32)
    cosine, sine_rows = rope_tables(seq_len, LHD)
    start_row = rank * local
    cosine = lax.dynamic_slice_in_dim(cosine[:, 0], start_row, local, 0)
    sine_rows = lax.dynamic_slice_in_dim(sine_rows[:, 0], start_row, local, 0)
    early_half = (jnp.arange(LHD) < LHD // 2)[None, :]
    sine_low = jnp.where(early_half, -sine_rows, 0.0)
    sine_high = jnp.where(early_half, 0.0, sine_rows)
    zeros = jnp.zeros_like(sine_rows)
    tables = [jnp.concatenate([part, part], axis=1) for part in (cosine, sine_low, sine_high)]
    tables += [
        jnp.concatenate(part, axis=1)
        for part in ((cosine, zeros + 1.0), (sine_low, zeros), (sine_high, zeros))
    ]
    entry_rows, slots = piece_ids.shape
    pairs = piece_ids[:, 0::2] + piece_ids[:, 1::2] * 65536
    words = jnp.concatenate(
        [pairs, piece_counts[:, None], jnp.zeros((entry_rows, 3), jnp.int32)], axis=1
    )
    words = words.reshape(entry_rows * 8 // 128, 128)
    words = lax.all_gather(words, "dp", axis=0, tiled=True)

    def from_rank(values_in, step):
        pairs = [(j, (j + step) % ranks) for j in range(ranks)]
        return lax.ppermute(values_in, "tensor", pairs)

    rows = hyper_qkv.shape[0]
    width = hyper_out.shape[1]
    fold = hyper_in.shape[1] // width
    packed = jnp.concatenate(
        [
            hyper_qkv,
            hyper_out,
            hyper_in.reshape(rows, width, fold).swapaxes(1, 2).reshape(rows, fold * width),
            hyper_proj,
            hyper_back.reshape(rows, fold * width),
            jnp.pad(hyper_norms.T, ((0, 0), (0, 124))),
        ],
        axis=1,
    ).astype(jnp.bfloat16)
    dim = w_query.shape[0]
    chunk = 256
    chunk_count = dim // chunk
    head_cols = w_query.shape[1]
    kv_local = jnp.concatenate([w_kv[0], w_kv[1]], axis=1)
    spread_out = lax.axis_size("dp") == chunk_count
    if spread_out:
        mine = lax.dynamic_slice_in_dim(kv_local, lax.axis_index("dp") * chunk, chunk, 0)
        mine = mine.reshape(chunk // rows, rows, 128).swapaxes(0, 1).reshape(rows, -1)
        packed = jnp.concatenate([packed, mine], axis=1)
    stacked = jnp.stack([packed] + [from_rank(packed, k) for k in range(1, ranks)])
    packed = jnp.concatenate(
        [
            lax.dynamic_index_in_dim(stacked, (rank - k) % ranks, 0, keepdims=False)
            for k in range(ranks)
        ],
        axis=0,
    )
    own_query = w_query.reshape(chunk_count, 1, chunk, head_cols)
    own_out = w_attn_out.reshape(head_cols // chunk, chunk, chunk_count, chunk)
    own_out = own_out.transpose(2, 1, 0, 3).reshape(chunk_count, 1, chunk, head_cols)
    words, packed, tables, gains, own_out = lax.optimization_barrier(
        (words, packed, tables, gains, own_out)
    )
    words = lax.all_gather(words, "tensor", axis=0, tiled=True)
    words, rank_done, late_grad = lax.optimization_barrier(
        (words, lax.axis_index("dp"), cotangent[0])
    )
    gathered = lax.all_gather(packed, "dp", axis=0, tiled=True)
    param_cols = hyper_qkv.shape[1] + width + 2 * fold * width + dim + 128
    params = gathered

    def attn_chunk(index):
        start = index * chunk
        out_cols = lax.dynamic_slice_in_dim(w_attn_out, start, chunk, 1)
        return jnp.concatenate(
            [lax.dynamic_slice_in_dim(w_query, start, chunk, 0)]
            + [out_cols[k : k + chunk] for k in range(0, head_cols, chunk)],
            axis=1,
        )

    if spread_out:
        mine = attn_chunk(rank_done)
        rest_all = jnp.concatenate([from_rank(mine, k) for k in range(1, ranks)], axis=0)
        wkv_all = gathered[:, param_cols:].reshape(
            chunk_count, ranks, rows, chunk // rows, 128
        )
        wkv_all = wkv_all.swapaxes(2, 3).reshape(chunk_count, ranks, chunk, 128)
    else:
        own_all = jnp.concatenate([own_query, own_out], axis=3)
        rest_all = jnp.concatenate([from_rank(own_all, k) for k in range(1, ranks)], axis=1)
        wkv_all = lax.all_gather(
            kv_local.reshape(chunk_count, chunk, 128), "tensor", axis=1, tiled=False
        )

    my_ids = lax.dynamic_slice_in_dim(text_ids[0], rank * local, local, 0)
    owner = my_ids // entry_rows
    place = (owner % ranks) * lax.axis_size("dp") + owner // ranks
    my_words = words[place * (entry_rows // 16) + (my_ids % entry_rows) // 16]
    pick = (jnp.arange(16)[None, :] == (my_ids % 16)[:, None])[:, :, None]
    my_words = jnp.sum(jnp.where(pick, my_words.reshape(local, 16, 8), 0), axis=1)
    my_pieces = jnp.stack([my_words[:, :4] % 65536, my_words[:, :4] // 65536], axis=2)
    my_counts = my_words[:, 4]
    pieces = piece_table[my_pieces.reshape(local * slots)]
    live = (jnp.arange(slots)[None, :] < my_counts[:, None]).astype(jnp.float32)
    live_rows = live.reshape(local * slots, 1)
    live_lanes = live.reshape(1, local * slots)
    counts = my_counts.astype(jnp.float32)[:, None]
    alive = (jnp.arange(seq_len) < length)[:, None]
    out_low = jnp.where(alive, late_grad, jnp.zeros((), jnp.bfloat16))
    product_grad = jnp.einsum("ld,fd->lf", out_low, w_down, preferred_element_type=jnp.float32)
    pieces, live_rows, live_lanes, counts, rest_all, product_grad = lax.optimization_barrier(
        (pieces, live_rows, live_lanes, counts, rest_all, product_grad)
    )
    rest_query, rest_out = rest_all[..., :head_cols], rest_all[..., head_cols:]
    if spread_out:
        rest_query, rest_out = (
            lax.all_gather(part, "dp", axis=0, tiled=True).reshape(
                chunk_count, ranks - 1, chunk, head_cols
            )
            for part in (rest_query, rest_out)
        )
    qkv, mixed, mid_rows, pre, pooled, embed, norms = hyper_forward(
        params, param_cols, pieces, live_rows, live_lanes, counts, slots, dim
    )


    scalars = jnp.stack([start_row, length, rank]).astype(jnp.int32)
    both, lead = project_both(scalars, embed, gains, tables, wkv_all)
    blocks = [both] + [from_rank(both, k) for k in range(1, ranks)]
    query = project(lead, tables, own_query, rest_query)
    attn_mixed, logs = attend(scalars, query, blocks)
    resid_mid, mlp_own = attend_out(attn_mixed, embed, gains, own_out, rest_out)

    def plus(left, right):
        return (left.astype(wide_type) + right.astype(wide_type)).astype(low_type)

    top = ranks - 1
    table_of = lambda *values_in: jnp.array(values_in, jnp.int32)[rank]
    near, mid_index, far = table_of(1, 2, 3, 2), table_of(2, 0, 1, 1), table_of(3, 3, 0, 0)
    order = (rank.astype(jnp.int32), near, mid_index, far)
    up_one, down_one = shift(mlp_own, 1, 0, top, ranks), shift(mlp_own, -1, 0, top, ranks)
    own_done = feed(order[0][None], mlp_own, product_grad, w_gate_up)
    up_one, down_one, own_done = lax.optimization_barrier((up_one, down_one, own_done))
    up_two, down_two = shift(up_one, 1, 1, top, ranks), shift(down_one, -1, 0, top - 1, ranks)
    near_rows = jnp.where(rank == top, up_one, down_one)
    near_done = feed(near[None], near_rows, product_grad, w_gate_up)
    up_two, down_two, near_done = lax.optimization_barrier((up_two, down_two, near_done))
    up_three, down_three = shift(up_two, 1, 2, top, ranks), shift(down_two, -1, 0, 1, ranks)
    mid_in = jnp.where(rank == 0, down_two, jnp.where(rank == top, up_two, up_one))
    mid_done = feed(mid_index[None], mid_in, product_grad, w_gate_up)
    up_three, down_three, mid_done = lax.optimization_barrier((up_three, down_three, mid_done))
    far_rows = jnp.where(
        rank == 0,
        down_three,
        jnp.where(rank == 1, down_two, jnp.where(rank == 2, up_two, up_three)),
    )
    far_done = feed(far[None], far_rows, product_grad, w_gate_up)
    products = jnp.zeros((seq_len, w_down.shape[0]), low_type)
    sums = []
    for index, (part, product) in zip(order, (own_done, near_done, mid_done, far_done)):
        sums.append(part)
        products = lax.dynamic_update_slice_in_dim(products, product, index * local, 0)
    part_own, part_near, part_mid, part_far = sums
    pre, qkv, part_far = lax.optimization_barrier((pre, qkv, part_far))
    down_came = shift(part_far, -1, top, top, ranks)
    up_came = shift(part_far, 1, 0, 0, ranks)
    hidden, slope = bends(pre)
    down_came, up_came, hidden, slope, qkv = lax.optimization_barrier(
        (down_came, up_came, hidden, slope, qkv)
    )
    down_came = shift(
        plus(jnp.where(rank == top, part_mid, part_far), down_came), -1, top - 1, top, ranks
    )
    up_came = shift(plus(jnp.where(rank == 0, part_mid, part_far), up_came), 1, 0, 1, ranks)
    probs = slot_probs(qkv, live_rows, slots)
    cot_own = lax.dynamic_slice_in_dim(cotangent[0], start_row, local, 0)
    down_came, up_came, probs, cot_own = lax.optimization_barrier(
        (down_came, up_came, probs, cot_own)
    )
    down_came = shift(
        plus(jnp.where(rank == top, part_near, part_mid), down_came), -1, 1, top, ranks
    )
    up_came = shift(plus(part_near, up_came), 1, 0, top - 1, ranks)
    mlp_grad = (
        part_own.astype(wide_type) + down_came.astype(wide_type) + up_came.astype(wide_type)
    ).astype(low_type)
    down_part = jnp.dot(products, w_down, preferred_element_type=jnp.float32).astype(jnp.bfloat16)
    mlp_grad, down_low, down_high = lax.optimization_barrier(
        (mlp_grad, down_part[:, : dim // 2], down_part[:, dim // 2 :])
    )
    low_own = lax.psum_scatter(down_low, "tensor", scatter_dimension=0, tiled=True)
    resid_grad, query_grad, *block_grads = attend_back(
        scalars, mlp_grad, cot_own, resid_mid, gains, query, blocks, attn_mixed, logs, tables,
        own_out, rest_out,
    )
    for k in range(1, ranks):
        block_grads[k] = from_rank(block_grads[k], -k)
    query_part = project_back_query(query_grad, own_query, rest_query)
    block_grads, query_part, down_high = lax.optimization_barrier(
        (block_grads, query_part, down_high)
    )
    high_own = lax.psum_scatter(down_high, "tensor", scatter_dimension=0, tiled=True)
    half = dim // 2
    layer_low = (resid_mid[:, :half] + low_own.astype(wide_type)).astype(low_type)
    embed_grad = project_back(
        scalars, embed, gains, resid_grad, query_part, tables, block_grads, wkv_all
    )
    embed_grad, layer_low = lax.optimization_barrier((embed_grad, layer_low))
    output_low = lax.all_gather(layer_low, "tensor", axis=0, tiled=True)
    shard = hyper_backward(
        params, param_cols, norms, embed_grad, pooled, pieces, live_rows, counts, qkv, mixed,
        mid_rows, hidden, slope, probs, slots,
    )
    shard, high_own, output_low = lax.optimization_barrier((shard, high_own, output_low))
    layer_high = (resid_mid[:, half:] + high_own.astype(wide_type)).astype(low_type)
    shard, layer_high = lax.optimization_barrier((shard, layer_high))
    output_high = lax.all_gather(layer_high, "tensor", axis=0, tiled=True)
    lm_output = join_columns(output_low, output_high)[None]
    cuts = [0]
    for extent in (3 * width, width, fold * width, dim, fold * width, 128):
        cuts.append(cuts[-1] + extent)
    (qkv_shard, out_shard, in_shard, proj_shard, back_shard, norm_shard), squares = scatter_sum(
        shard, ranks, cuts
    )
    in_shard = in_shard.reshape(rows, fold, width).swapaxes(1, 2)
    grad_shards = (
        qkv_shard,
        out_shard,
        in_shard.reshape(rows, fold * width),
        back_shard.reshape(rows * fold, width),
        proj_shard,
        norm_shard[:, :4].T,
    )
    squares, lm_output = lax.optimization_barrier((squares, lm_output))
    for bit in range(lax.axis_size("dp").bit_length() - 1):
        pairs = [(k, k ^ (1 << bit)) for k in range(lax.axis_size("dp"))]
        squares = squares + lax.ppermute(squares, "dp", pairs)
    for bit in range(ranks.bit_length() - 1):
        pairs = [(k, k ^ (1 << bit)) for k in range(ranks)]
        squares = squares + lax.ppermute(squares, "tensor", pairs)
    square_sum = squares[0, 0]
    grad_norm = jnp.sqrt(square_sum)
    step_value = step_count[0].astype(jnp.float32)
    first_fix = 1.0 - jnp.power(beta_one, step_value)
    second_fix = 1.0 - jnp.power(beta_two, step_value)
    masters = (hyper_qkv, hyper_out, hyper_in, hyper_back, hyper_proj, hyper_norms)
    firsts = (first_qkv, first_out, first_in, first_back, first_proj, first_norms)
    seconds = (second_qkv, second_out, second_in, second_back, second_proj, second_norms)
    factors = jnp.stack([first_fix, second_fix])
    return (
        lm_output,
        grad_norm,
        *update_params(factors, squares, grad_shards, masters, firsts, seconds),
    )


def solution(mesh):
    in_specs = (
        P(),
        P(("dp", "tensor"), None),
        P(("dp", "tensor")),
        P("dp", None),
        P("dp"),
        P(),
        P(None, "tensor"),
        P(None, None, "tensor"),
        P("tensor", None),
        P(None, None, "tensor"),
        P("tensor", None),
        P("dp", None, None),
        P(),
        P(("dp", "tensor"), None),
        P(("dp", "tensor"), None),
        P(("dp", "tensor"), None),
        P(("dp", "tensor"), None),
        P(("dp", "tensor"), None),
        P(None, ("dp", "tensor")),
        P(("dp", "tensor"), None),
        P(("dp", "tensor"), None),
        P(("dp", "tensor"), None),
        P(("dp", "tensor"), None),
        P(("dp", "tensor"), None),
        P(None, ("dp", "tensor")),
        P(("dp", "tensor"), None),
        P(("dp", "tensor"), None),
        P(("dp", "tensor"), None),
        P(("dp", "tensor"), None),
        P(("dp", "tensor"), None),
        P(None, ("dp", "tensor")),
    )
    out_specs = (
        P("dp", None, None),
        P(),
        P(("dp", "tensor"), None),
        P(("dp", "tensor"), None),
        P(("dp", "tensor"), None),
        P(("dp", "tensor"), None),
        P(("dp", "tensor"), None),
        P(None, ("dp", "tensor")),
        P(("dp", "tensor"), None),
        P(("dp", "tensor"), None),
        P(("dp", "tensor"), None),
        P(("dp", "tensor"), None),
        P(("dp", "tensor"), None),
        P(None, ("dp", "tensor")),
        P(("dp", "tensor"), None),
        P(("dp", "tensor"), None),
        P(("dp", "tensor"), None),
        P(("dp", "tensor"), None),
        P(("dp", "tensor"), None),
        P(None, ("dp", "tensor")),
    )
    return jax.shard_map(
        on_device, mesh=mesh, in_specs=in_specs, out_specs=out_specs, check_vma=False
    )
```

```python
import functools

import jax
import jax.numpy as jnp
from jax import lax
from jax.experimental import pallas as pl
from jax.experimental.pallas import tpu as pltpu
from jax.sharding import PartitionSpec as P

HHD = 64
LHD = 64


eps_norm = 1e-05
learn_rate = 0.05
norms_rate = 0.5
beta_one = 0.9
beta_two = 0.999
adam_eps = 1e-08
weight_decay = 0.1
clip_max = 1.0
masked = -1e30


def rope_tables(seq_len, head_width):
    half_width = head_width // 2
    frequency = 10000.0 ** (-jnp.arange(half_width, dtype=jnp.float32) * 2.0 / head_width)
    angles = jnp.arange(seq_len, dtype=jnp.float32)[:, None] * frequency[None, :]
    cosine = jnp.concatenate([jnp.cos(angles), jnp.cos(angles)], axis=1)
    sine_rows = jnp.concatenate([jnp.sin(angles), jnp.sin(angles)], axis=1)
    return (cosine[:, None, :], sine_rows[:, None, :])


def rms_norm(values_in, gain):
    return (
        values_in
        * lax.rsqrt(jnp.mean(values_in * values_in, axis=-1, keepdims=True) + eps_norm)
        * gain
    )


def softmax_rows(scores):
    row_top = jnp.max(scores, axis=-1, keepdims=True)
    exp_scores = jnp.exp(scores - row_top)
    return exp_scores / jnp.sum(exp_scores, axis=-1, keepdims=True)


low_type = jnp.bfloat16
wide_type = jnp.float32
vmem_bytes = 62 * 1024 * 1024


def mm(left, right):
    return lax.dot_general(
        left, right, (((1,), (0,)), ((), ())), preferred_element_type=wide_type
    )


def mm_nt(left, right):
    return lax.dot_general(
        left, right, (((1,), (1,)), ((), ())), preferred_element_type=wide_type
    )


def mm_tn(left, right):
    return lax.dot_general(
        left, right, (((0,), (0,)), ((), ())), preferred_element_type=wide_type
    )


def half_masks():
    lane = lax.broadcasted_iota(jnp.int32, (1, 128), 1)
    first = (lane < LHD).astype(wide_type).astype(low_type)
    second = (lane >= LHD).astype(wide_type).astype(low_type)
    return first, second


def stack_heads(pair, first, second):
    return jnp.concatenate([pair * first, pair * second], axis=0)


def norm_hat(values_in):
    centred = values_in - jnp.mean(values_in, axis=-1, keepdims=True)
    scale = lax.rsqrt(jnp.mean(centred * centred, axis=-1, keepdims=True) + eps_norm)
    return centred * scale, scale


def norm_back(hat, scale, grad):
    return scale * (
        grad
        - jnp.mean(grad, axis=-1, keepdims=True)
        - hat * jnp.mean(grad * hat, axis=-1, keepdims=True)
    )


def rms_back(values_in, gain, grad):
    scale = lax.rsqrt(jnp.mean(values_in * values_in, axis=-1, keepdims=True) + eps_norm)
    scaled = grad * gain
    hat = values_in * scale
    return scale * (scaled - hat * jnp.mean(scaled * hat, axis=-1, keepdims=True))


gelu_in = 0.7978845608028654
gelu_cube = 0.044715


def slot_mask(live, slots, axis=0):
    row_entry = lax.broadcasted_iota(jnp.int32, (128, 128), 0) // slots
    col_entry = lax.broadcasted_iota(jnp.int32, (128, 128), 1) // slots
    keep = jnp.where(row_entry == col_entry, live, 0.0)
    bias = jnp.where(keep > 0.0, 0.0, masked)
    return jnp.concatenate([bias, bias], axis=axis)


def slot_softmax(stacked, keys, bias):
    scores = mm_nt(keys, stacked) * (HHD ** (-0.5)) + bias
    exp_scores = jnp.exp(scores - jnp.max(scores, axis=0, keepdims=True))
    return exp_scores / jnp.sum(exp_scores, axis=0, keepdims=True)


def hyper_forward_kernel(
    slots, piece_ref, live_ref, count_ref, param_ref,
    qkv_ref, mixed_ref, second_ref, pre_ref, pool_ref, embed_ref, norm_ref,
):
    tile, width = piece_ref.shape

    @pl.when(pl.program_id(0) == 0)
    def _():
        norm_ref[...] = param_ref[:, param_ref.shape[1] - 128 :].astype(wide_type).T[0:8]

    first, second = half_masks()
    inputs = piece_ref[...].astype(wide_type)
    lead = (norm_hat(inputs)[0] * norm_ref[0:1] + norm_ref[1:2]).astype(low_type)
    for k in range(3):
        part = slice(k * width, (k + 1) * width)
        qkv_ref[:, part] = mm(lead, param_ref[:, part]).astype(low_type)
    low_lane = lax.broadcasted_iota(jnp.int32, (1, 128), 1) < HHD

    for block in range(tile // 128):
        rows = slice(block * 128, (block + 1) * 128)
        bias = slot_mask(live_ref[rows], slots, 1)
        for col in range(0, width, 128):
            stacked = stack_heads(qkv_ref[rows, col : col + 128], first, second)
            keys = qkv_ref[rows, width + col : width + col + 128]
            values = qkv_ref[rows, 2 * width + col : 2 * width + col + 128]
            prob = slot_softmax(stacked, keys, bias).astype(low_type)
            both = mm_tn(prob, values)
            mixed_ref[rows, col : col + 128] = jnp.where(low_lane, both[:128], both[128:]).astype(
                low_type
            )
    start = 3 * width
    second_in = inputs + mm(mixed_ref[...], param_ref[:, start : start + width])
    second_ref[...] = second_in
    mid = (norm_hat(second_in)[0] * norm_ref[2:3] + norm_ref[3:4]).astype(low_type)
    hidden_count = pre_ref.shape[1]
    start = start + width
    proj = start + hidden_count
    back = proj + embed_ref.shape[1]
    third = second_in
    for col in range(0, hidden_count, width):
        pre = mm(mid, param_ref[:, start + col : start + col + width])
        pre_ref[:, col : col + width] = pre.astype(low_type)
        hidden = (
            0.5 * pre * (1.0 + jnp.tanh(gelu_in * (pre + gelu_cube * pre * pre * pre)))
        ).astype(low_type)
        third = third + mm(hidden, param_ref[:, back + col : back + col + width])
    third = jnp.where(live_ref[...] > 0.0, third, 0.0)
    pooled = jnp.sum(third.reshape(tile // slots, slots, width), axis=1) / count_ref[...]
    pooled = pooled.astype(low_type)
    pool_ref[...] = pooled
    embed_ref[...] = mm(pooled, param_ref[:, proj:back]).astype(low_type)


def hyper_forward(
    params, param_cols, pieces, live_rows, counts, slots, dim
):
    row_count, width = pieces.shape
    tile = 256
    fold = (param_cols - 128 - dim - 4 * width) // 2
    by_row = lambda cols: pl.BlockSpec((tile, cols), lambda i: (i, 0))
    by_entry = lambda cols: pl.BlockSpec((tile // slots, cols), lambda i: (i, 0))
    entries = row_count // slots
    struct = jax.ShapeDtypeStruct
    return pl.pallas_call(
        functools.partial(hyper_forward_kernel, slots),
        grid=(row_count // tile,),
        in_specs=[
            by_row(width),
            by_row(1),
            by_entry(1),
            pl.BlockSpec((width, param_cols), lambda i: (0, 0), pipeline_mode=pl.Buffered(1)),
        ],
        out_specs=[
            by_row(3 * width), by_row(width), by_row(width), by_row(fold),
            by_entry(width), by_entry(dim), pl.BlockSpec((8, width), lambda i: (0, 0)),
        ],
        out_shape=[
            struct((row_count, 3 * width), low_type),
            struct((row_count, width), low_type),
            struct((row_count, width), wide_type),
            struct((row_count, fold), low_type),
            struct((entries, width), low_type),
            struct((entries, dim), low_type),
            struct((8, width), wide_type),
        ],
        compiler_params=pltpu.CompilerParams(vmem_limit_bytes=vmem_bytes),
        cost_estimate=pl.CostEstimate(
            flops=2 * row_count * width * 12 * width,
            bytes_accessed=2 * params.size + 12 * row_count * width,
            transcendentals=row_count * fold,
        ),
        name="hyper_forward",
    )(pieces, live_rows, counts, params)


def bend_kernel(pre_ref, hidden_ref, slope_ref):
    for col in range(0, pre_ref.shape[1], 512):
        part = slice(col, col + 512)
        pre = pre_ref[:, part].astype(wide_type)
        square = pre * pre
        bend = jnp.tanh(gelu_in * pre * (1.0 + gelu_cube * square))
        hidden_ref[:, part] = (0.5 * pre * (1.0 + bend)).astype(low_type)
        slope = 0.5 * (1.0 + bend) + 0.5 * pre * (1.0 - bend * bend) * gelu_in * (
            1.0 + 3.0 * gelu_cube * square
        )
        slope_ref[:, part] = slope.astype(low_type)


def bends(pre):
    rows, cols = pre.shape
    tile = 256
    spec = pl.BlockSpec((tile, cols), lambda i: (i, 0))
    struct = jax.ShapeDtypeStruct(pre.shape, low_type)
    return pl.pallas_call(
        bend_kernel,
        grid=(rows // tile,),
        in_specs=[spec],
        out_specs=[spec, spec],
        out_shape=[struct, struct],
        cost_estimate=pl.CostEstimate(
            flops=20 * pre.size, bytes_accessed=6 * pre.size, transcendentals=pre.size
        ),
        name="bends",
    )(pre)


def slot_prob_kernel(slots, qkv_ref, live_ref, prob_ref):
    tile = live_ref.shape[0]
    width = qkv_ref.shape[1] // 3
    first, second = half_masks()
    for block in range(tile // 128):
        rows = slice(block * 128, (block + 1) * 128)
        bias = slot_mask(live_ref[rows], slots, 1)
        for col in range(0, width, 128):
            stacked = stack_heads(qkv_ref[rows, col : col + 128], first, second)
            keys = qkv_ref[rows, width + col : width + col + 128]
            prob = slot_softmax(stacked, keys, bias)
            prob_ref[rows, 2 * col : 2 * col + 256] = prob.astype(low_type)


def slot_probs(qkv, live_rows, slots):
    rows, cols = qkv.shape
    tile = 256
    width = cols // 3
    return pl.pallas_call(
        functools.partial(slot_prob_kernel, slots),
        grid=(rows // tile,),
        in_specs=[
            pl.BlockSpec((tile, cols), lambda i: (i, 0)),
            pl.BlockSpec((tile, 1), lambda i: (i, 0)),
        ],
        out_specs=pl.BlockSpec((tile, 2 * width), lambda i: (i, 0)),
        out_shape=jax.ShapeDtypeStruct((rows, 2 * width), low_type),
        cost_estimate=pl.CostEstimate(
            flops=600 * rows * width, bytes_accessed=10 * rows * width,
            transcendentals=2 * rows * width,
        ),
        name="slot_probs",
    )(qkv, live_rows)


def hyper_backward_kernel(
    slots, grad_ref, pool_ref, piece_ref, live_ref, count_ref, qkv_ref, mixed_ref, second_ref,
    hidden_ref, slope_ref, prob_ref, param_ref, norm_ref, out_ref,
    sums, norm_sums, mix_grad, qkv_grad, pre_grad,
):
    tile, width = piece_ref.shape
    hidden_count = hidden_ref.shape[1]
    dim = grad_ref.shape[1]
    out_at = 3 * width
    in_at = out_at + width
    proj = in_at + hidden_count
    back = proj + dim
    first, second = half_masks()

    @pl.when(pl.program_id(0) == 0)
    def _():
        sums[...] = jnp.zeros_like(sums)
        norm_sums[...] = jnp.zeros_like(norm_sums)

    embed_grad = grad_ref[...]
    pooled = pool_ref[...]
    for col in range(0, dim, width):
        part = slice(proj + col, proj + col + width)
        sums[:, part] += mm_tn(pooled, embed_grad[:, col : col + width])
    pool_grad = mm_nt(embed_grad, param_ref[:, proj:back]) / count_ref[...]
    spread = jnp.broadcast_to(pool_grad[:, None, :], (tile // slots, slots, width))
    third_grad = jnp.where(live_ref[...] > 0.0, spread.reshape(tile, width), 0.0)
    back_in = third_grad.astype(low_type)
    for col in range(0, hidden_count, width):
        hidden_grad = mm_nt(back_in, param_ref[:, back + col : back + col + width])
        slope = slope_ref[:, col : col + width].astype(wide_type)
        pre_grad[:, col : col + width] = (slope * hidden_grad).astype(low_type)
        part = slice(back + col, back + col + width)
        sums[:, part] += mm_tn(back_in, hidden_ref[:, col : col + width])
    second_in = second_ref[...]
    hat, scale = norm_hat(second_in)
    mid = (hat * norm_ref[2:3] + norm_ref[3:4]).astype(low_type)
    mid_grad = jnp.zeros((tile, width), wide_type)
    for col in range(0, hidden_count, width):
        part = slice(in_at + col, in_at + col + width)
        grads = pre_grad[:, col : col + width]
        sums[:, part] += mm_tn(mid, grads)
        mid_grad = mid_grad + mm_nt(grads, param_ref[:, part])
    norm_sums[2:3] += jnp.sum(mid_grad * hat, axis=0, keepdims=True)
    norm_sums[3:4] += jnp.sum(mid_grad, axis=0, keepdims=True)
    second_grad = third_grad + norm_back(hat, scale, mid_grad * norm_ref[2:3])
    out_in = second_grad.astype(low_type)
    sums[:, out_at:in_at] += mm_tn(mixed_ref[...], out_in)
    mix_grad[...] = mm_nt(out_in, param_ref[:, out_at:in_at]).astype(low_type)

    score_scale = HHD ** (-0.5)
    low_lane = lax.broadcasted_iota(jnp.int32, (1, 128), 1) < HHD
    for block in range(tile // 128):
        rows = slice(block * 128, (block + 1) * 128)
        for col in range(0, width, 128):
            stacked = stack_heads(qkv_ref[rows, col : col + 128], first, second)
            keys = qkv_ref[rows, width + col : width + col + 128]
            values = qkv_ref[rows, 2 * width + col : 2 * width + col + 128]
            prob_low = prob_ref[rows, 2 * col : 2 * col + 256]
            prob = prob_low.astype(wide_type)
            grads = stack_heads(mix_grad[rows, col : col + 128], first, second)
            prob_grad = mm_nt(values, grads)
            score_grad = prob * (prob_grad - jnp.sum(prob * prob_grad, axis=0, keepdims=True))
            score_grad = score_grad.astype(low_type)
            key_grad = mm(score_grad, stacked) * score_scale
            value_grad = mm(prob_low, grads)
            both = mm_tn(score_grad, keys)
            query_grad = jnp.where(low_lane, both[:128], both[128:]) * score_scale
            qkv_grad[rows, col : col + 128] = query_grad.astype(low_type)
            qkv_grad[rows, width + col : width + col + 128] = key_grad.astype(low_type)
            qkv_grad[rows, 2 * width + col : 2 * width + col + 128] = value_grad.astype(low_type)

    inputs = piece_ref[...].astype(wide_type)
    hat_one = norm_hat(inputs)[0]
    lead = (hat_one * norm_ref[0:1] + norm_ref[1:2]).astype(low_type)
    lead_grad = jnp.zeros((tile, width), wide_type)
    for col in range(0, 3 * width, width):
        part = slice(col, col + width)
        grads = qkv_grad[:, part]
        sums[:, part] += mm_tn(lead, grads)
        lead_grad = lead_grad + mm_nt(grads, param_ref[:, part])
    norm_sums[0:1] += jnp.sum(lead_grad * hat_one, axis=0, keepdims=True)
    norm_sums[1:2] += jnp.sum(lead_grad, axis=0, keepdims=True)

    @pl.when(pl.program_id(0) == pl.num_programs(0) - 1)
    def _():
        out_ref[:, :back] = sums[:, :back].astype(low_type)
        for col in range(back, back + hidden_count, width):
            out_ref[:, col : col + width] = sums[:, col : col + width].T.astype(low_type)
        out_ref[:, back + hidden_count :] = norm_sums[...].T.astype(low_type)


def hyper_backward(
    params, param_cols, norms, embed_grad, pooled, pieces, live_rows, counts, qkv, mixed,
    second_in, hidden, slope, probs, slots,
):
    row_count, width = pieces.shape
    dim = embed_grad.shape[1]
    fold = hidden.shape[1]
    tile = 512
    by_row = lambda cols: pl.BlockSpec((tile, cols), lambda i: (i, 0))
    by_entry = lambda cols: pl.BlockSpec((tile // slots, cols), lambda i: (i, 0))
    whole = lambda shape: pl.BlockSpec(shape, lambda i: (0, 0), pipeline_mode=pl.Buffered(1))
    return pl.pallas_call(
        functools.partial(hyper_backward_kernel, slots),
        grid=(row_count // tile,),
        in_specs=[
            by_entry(dim),
            by_entry(width),
            by_row(width),
            by_row(1),
            by_entry(1),
            by_row(3 * width),
            by_row(width),
            by_row(width),
            by_row(fold),
            by_row(fold),
            by_row(2 * width),
            whole((width, param_cols)),
            whole(norms.shape),
        ],
        out_specs=whole((width, param_cols)),
        out_shape=jax.ShapeDtypeStruct((width, param_cols), low_type),
        scratch_shapes=[
            pltpu.VMEM((width, param_cols - 128), wide_type),
            pltpu.VMEM((128, width), wide_type),
            pltpu.VMEM((tile, width), low_type),
            pltpu.VMEM((tile, 3 * width), low_type),
            pltpu.VMEM((tile, fold), low_type),
        ],
        compiler_params=pltpu.CompilerParams(vmem_limit_bytes=vmem_bytes),
        cost_estimate=pl.CostEstimate(
            flops=4 * row_count * width * 12 * width,
            bytes_accessed=4 * params.size + 24 * row_count * width,
            transcendentals=row_count * fold,
        ),
        name="hyper_backward",
    )(
        embed_grad, pooled, pieces, live_rows, counts, qkv, mixed, second_in, hidden, slope, probs,
        params, norms,
    )


def turn(values_in, cosine, sine_low, sine_high):
    parts = []
    for col in range(0, values_in.shape[1], 128):
        part = values_in[:, col : col + 128]
        parts.append(
            part * cosine
            + pltpu.roll(part, 96, axis=1) * sine_low
            + pltpu.roll(part, 32, axis=1) * sine_high
        )
    return parts[0] if len(parts) == 1 else jnp.concatenate(parts, axis=1)


def project_both_kernel(
    scalar_ref, embed_ref, gain_ref, kcos_ref, klow_ref, khigh_ref, wkv_ref, both_ref, lead_ref
):
    @pl.when(pl.program_id(0) == 0)
    def _():
        inputs = embed_ref[...].astype(wide_type)
        lead_ref[...] = rms_norm(inputs, gain_ref[0:1]).astype(low_type)

    chunk_count, _, chunk, _ = wkv_ref.shape
    both = jnp.zeros(both_ref.shape, wide_type)
    for k in range(chunk_count):
        both = both + mm(lead_ref[:, k * chunk : (k + 1) * chunk], wkv_ref[k, 0])
    both_ref[...] = turn(both, kcos_ref[...], klow_ref[...], khigh_ref[...]).astype(low_type)


def project_both(scalars, embed, gains, tables, wkv_all):
    local, dim = embed.shape
    chunk_count, ranks, chunk, _ = wkv_all.shape
    whole = lambda shape: pl.BlockSpec(shape, lambda t, place: (0, 0))
    return pl.pallas_call(
        project_both_kernel,
        grid_spec=pltpu.PrefetchScalarGridSpec(
            num_scalar_prefetch=1,
            grid=(ranks,),
            in_specs=[whole((local, dim)), whole(gains.shape)]
            + [whole((local, 128))] * 3
            + [
                pl.BlockSpec(
                    (chunk_count, 1, chunk, 128),
                    lambda t, place: (0, lax.rem(place[2] - t + ranks, ranks), 0, 0),
                )
            ],
            out_specs=[
                pl.BlockSpec((local, 128), lambda t, place: (0, t)), whole((local, dim)),
            ],
        ),
        out_shape=[
            jax.ShapeDtypeStruct((local, ranks * 128), low_type),
            jax.ShapeDtypeStruct((local, dim), low_type),
        ],
        compiler_params=pltpu.CompilerParams(vmem_limit_bytes=vmem_bytes),
        cost_estimate=pl.CostEstimate(
            flops=2 * local * dim * ranks * 128,
            bytes_accessed=2 * dim * ranks * 128 + 4 * local * dim,
            transcendentals=0,
        ),
        name="project_both",
    )(scalars, embed, gains, *tables[3:], wkv_all)


def own_or_rest(own_ref, rest_ref, use):
    @pl.when(pl.program_id(0) == 0)
    def _():
        use(own_ref)

    @pl.when(pl.program_id(0) > 0)
    def _():
        use(rest_ref)


def weight_specs(own_all):
    chunk_count, _, chunk, cols = own_all.shape
    shape = (chunk_count, 1, chunk, cols)
    return [
        pl.BlockSpec(shape, lambda t: (0, 0, 0, 0)),
        pl.BlockSpec(shape, lambda t: (0, jnp.maximum(t - 1, 0), 0, 0)),
    ]


def block_specs(local, count):
    return [
        pl.BlockSpec((local, 128), lambda t, k=k: (0, lax.rem(t - k + count, count)))
        for k in range(count)
    ]


def project_kernel(lead_ref, cos_ref, low_ref, high_ref, own_ref, rest_ref, query_ref):
    def use(wq_ref):
        chunk_count, _, chunk, cols = wq_ref.shape
        query = jnp.zeros((lead_ref.shape[0], cols), wide_type)
        for k in range(chunk_count):
            query = query + mm(lead_ref[:, k * chunk : (k + 1) * chunk], wq_ref[k, 0])
        query = turn(query, cos_ref[...], low_ref[...], high_ref[...])
        query_ref[...] = (query * (LHD ** (-0.5))).astype(low_type)

    own_or_rest(own_ref, rest_ref, use)


def project(lead, tables, own_all, rest_all):
    local, dim = lead.shape
    ranks = rest_all.shape[1] + 1
    cols = own_all.shape[3]
    whole = lambda shape: pl.BlockSpec(shape, lambda t: (0, 0))
    return pl.pallas_call(
        project_kernel,
        grid=(ranks,),
        in_specs=[whole((local, dim))] + [whole((local, 128))] * 3 + weight_specs(own_all),
        out_specs=pl.BlockSpec((local, cols), lambda t: (0, t)),
        out_shape=jax.ShapeDtypeStruct((local, ranks * cols), low_type),
        compiler_params=pltpu.CompilerParams(vmem_limit_bytes=vmem_bytes),
        cost_estimate=pl.CostEstimate(
            flops=2 * local * dim * ranks * cols,
            bytes_accessed=2 * dim * ranks * cols + 4 * local * dim,
            transcendentals=0,
        ),
        name="project",
    )(lead, *tables[:3], own_all, rest_all)


def key_place(start, index, local, seq_len):
    block = index // local
    return lax.rem(start + seq_len - block * local, seq_len) + index - block * local


def attend_kernel(
    scalar_ref, query_ref, own_ref, one_ref, two_ref, three_ref, mixed_ref, log_ref, bias_ref
):
    local = query_ref.shape[0]
    seq_len = bias_ref.shape[1]

    @pl.when(pl.program_id(0) == 0)
    def _():
        row = scalar_ref[0] + lax.broadcasted_iota(jnp.int32, (local, seq_len), 0)
        col = lax.broadcasted_iota(jnp.int32, (1, seq_len), 1)
        col = key_place(scalar_ref[0], col, local, seq_len)
        allowed = jnp.where(col <= row, jnp.where(col < scalar_ref[1], 0.0, masked), masked)
        bias_ref[...] = allowed

    first, second = half_masks()
    lane = lax.broadcasted_iota(jnp.int32, (1, 128), 1)
    both = jnp.concatenate([own_ref[...], one_ref[...], two_ref[...], three_ref[...]], axis=0)
    swapped = pltpu.roll(both.astype(wide_type), LHD, axis=1).astype(low_type)
    keys = both * first + swapped * second
    value_low = swapped * first
    value_high = both * second
    logs = jnp.zeros((local, 128), wide_type)
    for pair in range(query_ref.shape[1] // 128):
        cols = slice(pair * 128, (pair + 1) * 128)
        mixed = jnp.zeros((local, 128), wide_type)
        for half, (mask, values) in enumerate(((first, value_low), (second, value_high))):
            scores = mm_nt(query_ref[:, cols] * mask, keys) + bias_ref[...]
            row_top = jnp.max(scores, axis=-1, keepdims=True)
            exp_scores = jnp.exp(scores - row_top)
            exp_total = jnp.sum(exp_scores, axis=-1, keepdims=True)
            prob = (exp_scores * (1.0 / exp_total)).astype(low_type)
            mixed = mixed + mm(prob, values)
            logs = jnp.where(lane == 2 * pair + half, row_top + jnp.log(exp_total), logs)
        mixed_ref[:, cols] = mixed.astype(low_type)
    log_ref[...] = logs.T[0:8]


def attend(scalars, query, blocks):
    local, dim = query.shape
    ranks = len(blocks)
    seq_len = local * ranks
    cols = dim // ranks
    return pl.pallas_call(
        attend_kernel,
        grid=(ranks,),
        in_specs=[
            pl.BlockSpec(memory_space=pltpu.SMEM),
            pl.BlockSpec((local, cols), lambda t: (0, t)),
        ]
        + block_specs(local, ranks),
        out_specs=[
            pl.BlockSpec((local, cols), lambda t: (0, t)),
            pl.BlockSpec((8, local), lambda t: (t, 0)),
        ],
        out_shape=[
            jax.ShapeDtypeStruct((local, dim), low_type),
            jax.ShapeDtypeStruct((8 * ranks, local), wide_type),
        ],
        scratch_shapes=[pltpu.VMEM((local, seq_len), wide_type)],
        compiler_params=pltpu.CompilerParams(vmem_limit_bytes=vmem_bytes),
        cost_estimate=pl.CostEstimate(
            flops=16 * local * seq_len * dim,
            bytes_accessed=8 * local * dim,
            transcendentals=local * seq_len * dim // LHD,
        ),
        name="attend",
    )(scalars, query, *blocks)


def attend_out_kernel(mixed_ref, embed_ref, gain_ref, wo_own, wo_rest, mid_ref, lead_ref, total):
    @pl.when(pl.program_id(0) == 0)
    def _():
        total[...] = embed_ref[...].astype(wide_type)

    def use(wo_ref):
        chunk_count, _, chunk, cols = wo_ref.shape
        for k in range(chunk_count):
            part = slice(k * chunk, (k + 1) * chunk)
            for col in range(0, cols, chunk):
                total[:, part] += mm(
                    mixed_ref[:, col : col + chunk], wo_ref[k, 0, :, col : col + chunk]
                )

    own_or_rest(wo_own, wo_rest, use)

    @pl.when(pl.program_id(0) == pl.num_programs(0) - 1)
    def _():
        mid_ref[...] = total[...]
        lead_ref[...] = rms_norm(total[...], gain_ref[1:2]).astype(low_type)


def attend_out(mixed, embed, gains, own_all, rest_all):
    local, dim = embed.shape
    ranks = rest_all.shape[1] + 1
    cols = own_all.shape[3]
    whole = lambda shape: pl.BlockSpec(shape, lambda t: (0, 0))
    return pl.pallas_call(
        attend_out_kernel,
        grid=(ranks,),
        in_specs=[
            pl.BlockSpec((local, cols), lambda t: (0, t)), whole((local, dim)), whole(gains.shape),
        ]
        + weight_specs(own_all),
        out_specs=[whole((local, dim)), whole((local, dim))],
        out_shape=[
            jax.ShapeDtypeStruct((local, dim), wide_type),
            jax.ShapeDtypeStruct((local, dim), low_type),
        ],
        scratch_shapes=[pltpu.VMEM((local, dim), wide_type)],
        compiler_params=pltpu.CompilerParams(vmem_limit_bytes=vmem_bytes),
        cost_estimate=pl.CostEstimate(
            flops=2 * local * dim * dim,
            bytes_accessed=2 * dim * dim + 8 * local * dim,
            transcendentals=0,
        ),
        name="attend_out",
    )(mixed, embed, gains, own_all, rest_all)


def attend_back_kernel(
    scalar_ref, mlp_ref, cot_ref, mid_ref, gain_ref, query_ref, own_ref, one_ref, two_ref,
    three_ref, mixed_ref, log_ref, cos_ref, low_ref, high_ref, wo_own, wo_rest,
    resid_ref, qgrad_ref, own_grad, one_grad, two_grad, three_grad, low_grad, bias_ref, out_grad,
):
    local = query_ref.shape[0]
    seq_len = bias_ref.shape[0]

    @pl.when(pl.program_id(0) == 0)
    def _():
        row = scalar_ref[0] + lax.broadcasted_iota(jnp.int32, (local, 1), 0)
        own = jnp.where(row < scalar_ref[1], cot_ref[...].astype(wide_type), 0.0)
        grad = own + rms_back(mid_ref[...], gain_ref[1:2], mlp_ref[...].astype(wide_type))
        resid_ref[...] = grad
        low_grad[...] = grad.astype(low_type)
        col = scalar_ref[0] + lax.broadcasted_iota(jnp.int32, (seq_len, local), 1)
        key = lax.broadcasted_iota(jnp.int32, (seq_len, 1), 0)
        key = key_place(scalar_ref[0], key, local, seq_len)
        bias_ref[...] = jnp.where(
            key <= col, jnp.where(key < scalar_ref[1], 0.0, masked), masked
        )

    def use(wo_ref):
        chunk_count, _, chunk, cols = wo_ref.shape
        for col in range(0, cols, chunk):
            part_sum = jnp.zeros((local, chunk), wide_type)
            for k in range(chunk_count):
                part_sum = part_sum + mm_nt(
                    low_grad[:, k * chunk : (k + 1) * chunk], wo_ref[k, 0, :, col : col + chunk]
                )
            out_grad[:, col : col + chunk] = part_sum.astype(low_type)

    own_or_rest(wo_own, wo_rest, use)
    first, second = half_masks()
    lane = lax.broadcasted_iota(jnp.int32, (1, 128), 1)
    low_lane = lane < LHD
    both = jnp.concatenate([own_ref[...], one_ref[...], two_ref[...], three_ref[...]], axis=0)
    swapped = pltpu.roll(both.astype(wide_type), LHD, axis=1).astype(low_type)
    keys = both * first + swapped * second
    values = swapped * first + both * second
    key_low = both * first
    key_high = swapped * second
    sums = jnp.zeros((local, 128), wide_type)
    for pair in range(query_ref.shape[1] // 128):
        part = slice(pair * 128, (pair + 1) * 128)
        product = mixed_ref[:, part].astype(wide_type) * out_grad[:, part].astype(wide_type)
        one = jnp.sum(jnp.where(low_lane, product, 0.0), axis=-1, keepdims=True)
        two = jnp.sum(jnp.where(low_lane, 0.0, product), axis=-1, keepdims=True)
        sums = jnp.where(lane == 2 * pair, one, sums)
        sums = jnp.where(lane == 2 * pair + 1, two, sums)
    sums = sums.T[0:8]
    key_sum = jnp.zeros((seq_len, 128), wide_type)
    value_sum = jnp.zeros((seq_len, 128), wide_type)
    for pair in range(query_ref.shape[1] // 128):
        part = slice(pair * 128, (pair + 1) * 128)
        query_grad = jnp.zeros((local, 128), wide_type)
        for half, (mask, key_side) in enumerate(((first, key_low), (second, key_high))):
            head = 2 * pair + half
            query = query_ref[:, part] * mask
            grads = out_grad[:, part] * mask
            scores = mm_nt(keys, query) + bias_ref[...]
            prob = jnp.exp(scores - log_ref[head : head + 1])
            prob_grad = mm_nt(values, grads)
            score_grad = (prob * (prob_grad - sums[head : head + 1])).astype(low_type)
            key_sum = key_sum + mm(score_grad, query)
            value_sum = value_sum + mm(prob.astype(low_type), grads)
            query_grad = query_grad + mm_tn(score_grad, key_side)
        query_grad = query_grad * (LHD ** (-0.5))
        spun = query_grad * low_ref[...]
        spin = query_grad * high_ref[...]
        query_grad = (
            query_grad * cos_ref[...]
            + pltpu.roll(spin, 96, axis=1)
            + pltpu.roll(spun, 32, axis=1)
        )
        qgrad_ref[:, part] = query_grad.astype(low_type)
    key_sum = key_sum + pltpu.roll(key_sum, LHD, axis=1)
    value_sum = value_sum + pltpu.roll(value_sum, LHD, axis=1)
    both_grad = jnp.where(low_lane, key_sum, value_sum).astype(low_type)
    for k, ref in enumerate((own_grad, one_grad, two_grad, three_grad)):
        ref[...] = both_grad[k * local : (k + 1) * local]


def attend_back(
    scalars, mlp_grad, cot_own, mid, gains, query, blocks, mixed, logs, tables, own_all, rest_all
):
    local, dim = mid.shape
    ranks = len(blocks)
    seq_len = local * ranks
    cols = own_all.shape[3]
    whole = lambda shape: pl.BlockSpec(shape, lambda t: (0, 0))
    by_block = block_specs(local, ranks)
    by_rank = pl.BlockSpec((local, cols), lambda t: (0, t))
    return pl.pallas_call(
        attend_back_kernel,
        grid=(ranks,),
        in_specs=[
            pl.BlockSpec(memory_space=pltpu.SMEM),
            whole((local, dim)),
            whole((local, dim)),
            whole((local, dim)),
            whole(gains.shape),
            by_rank,
        ]
        + by_block
        + [
            by_rank,
            pl.BlockSpec((8, local), lambda t: (t, 0)),
            whole((local, 128)),
            whole((local, 128)),
            whole((local, 128)),
        ]
        + weight_specs(own_all),
        out_specs=[
            whole((local, dim)),
            by_rank,
        ]
        + by_block,
        out_shape=[
            jax.ShapeDtypeStruct((local, dim), wide_type),
            jax.ShapeDtypeStruct((local, ranks * cols), low_type),
        ]
        + [jax.ShapeDtypeStruct((local, ranks * 128), low_type)] * len(blocks),
        scratch_shapes=[
            pltpu.VMEM((local, dim), low_type),
            pltpu.VMEM((seq_len, local), wide_type),
            pltpu.VMEM((local, cols), low_type),
        ],
        compiler_params=pltpu.CompilerParams(vmem_limit_bytes=vmem_bytes),
        cost_estimate=pl.CostEstimate(
            flops=2 * local * dim * dim + 40 * local * seq_len * dim,
            bytes_accessed=2 * dim * dim + 20 * local * dim,
            transcendentals=local * seq_len * dim // LHD,
        ),
        name="attend_back",
    )(
        scalars, mlp_grad, cot_own, mid, gains, query, *blocks, mixed, logs, *tables[:3], own_all,
        rest_all,
    )


def project_back_query_kernel(qgrad_ref, own_ref, rest_ref, total_ref):
    @pl.when(pl.program_id(0) == 0)
    def _():
        total_ref[...] = jnp.zeros_like(total_ref)

    def use(wq_ref):
        chunk_count, _, chunk, _ = wq_ref.shape
        for k in range(chunk_count):
            total_ref[:, k * chunk : (k + 1) * chunk] += mm_nt(qgrad_ref[...], wq_ref[k, 0])

    own_or_rest(own_ref, rest_ref, use)


def project_back_query(query_grad, own_all, rest_all):
    chunk_count, _, chunk, _ = own_all.shape
    ranks = rest_all.shape[1] + 1
    cols = own_all.shape[3]
    local = query_grad.shape[0]
    dim = chunk_count * chunk
    return pl.pallas_call(
        project_back_query_kernel,
        grid=(ranks,),
        in_specs=[pl.BlockSpec((local, cols), lambda t: (0, t))] + weight_specs(own_all),
        out_specs=pl.BlockSpec((local, dim), lambda t: (0, 0)),
        out_shape=jax.ShapeDtypeStruct((local, dim), wide_type),
        compiler_params=pltpu.CompilerParams(vmem_limit_bytes=vmem_bytes),
        cost_estimate=pl.CostEstimate(
            flops=2 * local * dim * ranks * cols,
            bytes_accessed=2 * dim * ranks * cols + 8 * local * dim,
            transcendentals=0,
        ),
        name="project_back_query",
    )(query_grad, own_all, rest_all)


def project_back_kernel(
    scalar_ref, embed_ref, gain_ref, resid_ref, part_ref, kcos_ref, klow_ref, khigh_ref, own_ref, one_ref,
    two_ref, three_ref, wkv_ref, grad_ref, total,
):
    step = pl.program_id(0)

    @pl.when(step == 0)
    def _():
        total[...] = part_ref[...]

    both = own_ref[...].astype(wide_type)
    for ref in (one_ref, two_ref, three_ref):
        both = both + ref[...].astype(wide_type)
    both = (
        both * kcos_ref[...]
        + pltpu.roll(both * khigh_ref[...], 96, axis=1)
        + pltpu.roll(both * klow_ref[...], 32, axis=1)
    ).astype(low_type)
    chunk_count, _, chunk, _ = wkv_ref.shape
    for k in range(chunk_count):
        total[:, k * chunk : (k + 1) * chunk] += mm_nt(both, wkv_ref[k, 0])

    @pl.when(step == pl.num_programs(0) - 1)
    def _():
        grad = resid_ref[...] + rms_back(
            embed_ref[...].astype(wide_type), gain_ref[0:1], total[...]
        )
        grad_ref[...] = grad.astype(low_type)


def project_back(scalars, embed, gains, resid, part, tables, blocks, wkv_all):
    local, dim = embed.shape
    chunk_count, ranks, chunk, _ = wkv_all.shape
    whole = lambda shape: pl.BlockSpec(shape, lambda t, place: (0, 0))
    return pl.pallas_call(
        project_back_kernel,
        grid_spec=pltpu.PrefetchScalarGridSpec(
            num_scalar_prefetch=1,
            grid=(ranks,),
            in_specs=[whole((local, dim)), whole(gains.shape)]
            + [whole((local, dim))] * 2
            + [whole((local, 128))] * 3
            + [pl.BlockSpec((local, 128), lambda t, place: (0, t))] * len(blocks)
            + [
                pl.BlockSpec(
                    (chunk_count, 1, chunk, 128),
                    lambda t, place: (0, lax.rem(place[2] - t + ranks, ranks), 0, 0),
                )
            ],
            out_specs=whole((local, dim)),
            scratch_shapes=[pltpu.VMEM((local, dim), wide_type)],
        ),
        out_shape=jax.ShapeDtypeStruct((local, dim), low_type),
        compiler_params=pltpu.CompilerParams(vmem_limit_bytes=vmem_bytes),
        cost_estimate=pl.CostEstimate(
            flops=2 * local * dim * ranks * 128,
            bytes_accessed=2 * dim * ranks * 128 + 16 * local * dim,
            transcendentals=0,
        ),
        name="project_back",
    )(scalars, embed, gains, resid, part, *tables[3:], *blocks, wkv_all)


def join_kernel(low_ref, high_ref, out_ref):
    half = low_ref.shape[1]
    out_ref[:, :half] = low_ref[...]
    out_ref[:, half:] = high_ref[...]


def join_columns(low, high):
    rows, cols = low.shape[0], low.shape[1] + high.shape[1]
    spec = lambda width: pl.BlockSpec((rows // 4, width), lambda i: (i, 0))
    return pl.pallas_call(
        join_kernel,
        grid=(4,),
        in_specs=[spec(low.shape[1]), spec(high.shape[1])],
        out_specs=spec(cols),
        out_shape=jax.ShapeDtypeStruct((rows, cols), low.dtype),
        cost_estimate=pl.CostEstimate(
            flops=0, bytes_accessed=4 * rows * cols, transcendentals=0
        ),
        name="join_columns",
    )(low, high)


def gather_sum_kernel(cuts, place_ref, own_ref, *refs):
    came, outs = refs[: len(refs) - len(cuts)], refs[len(refs) - len(cuts) :]
    *total_refs, square_ref = outs
    squares = jnp.zeros((1, 1), wide_type)
    for total_ref, start, end in zip(total_refs, cuts[:-1], cuts[1:]):
        total = own_ref[0, :, start:end].astype(wide_type)
        for ref in came:
            total = total + ref[:, start:end].astype(wide_type)
        total_ref[...] = total
        part = jnp.sum(total * total, axis=1, keepdims=True)
        squares = squares + jnp.sum(part, axis=0, keepdims=True)
    square_ref[...] = jnp.broadcast_to(squares, square_ref.shape)


def gather_sum(place, blocks, came, cuts):
    _, rows, cols = blocks.shape
    whole = lambda shape: pl.BlockSpec(shape, lambda i, place: (0, 0))
    shapes = [(rows, end - start) for start, end in zip(cuts[:-1], cuts[1:])] + [(8, 128)]
    return pl.pallas_call(
        functools.partial(gather_sum_kernel, tuple(cuts)),
        grid_spec=pltpu.PrefetchScalarGridSpec(
            num_scalar_prefetch=1,
            grid=(1,),
            in_specs=[pl.BlockSpec((1, rows, cols), lambda i, place: (place[0], 0, 0))]
            + [whole((rows, cols))] * len(came),
            out_specs=[whole(shape) for shape in shapes],
        ),
        out_shape=[jax.ShapeDtypeStruct(shape, wide_type) for shape in shapes],
        name="gather_sum",
    )(place, blocks, *came)


def update_kernel(count, scalar_ref, square_ref, *refs):
    ins, outs = refs[: 4 * count], refs[4 * count :]
    first_fix, second_fix = scalar_ref[0], scalar_ref[1]
    clip_scale = jnp.minimum(1.0, clip_max / (jnp.sqrt(square_ref[0:1, 0:1]) + 1e-06))
    for k in range(count):
        grad, master, first_old, second_old = (ins[j * count + k][...] for j in range(4))
        clipped = grad * clip_scale
        moment = beta_one * first_old + (1.0 - beta_one) * clipped
        square = beta_two * second_old + (1.0 - beta_two) * clipped * clipped
        update = moment / first_fix / (jnp.sqrt(square / second_fix) + adam_eps)
        if k < count - 1:
            new = master - learn_rate * (update + weight_decay * master)
        else:
            new = master - norms_rate * update
        outs[k][...] = new
        outs[count + k][...] = moment
        outs[2 * count + k][...] = square


def update_params(scalars, squares, grads, masters, firsts, seconds):
    count = len(grads)
    arrays = [*grads, *masters, *firsts, *seconds]
    vmem = pl.BlockSpec(memory_space=pltpu.VMEM)
    return pl.pallas_call(
        functools.partial(update_kernel, count),
        in_specs=[pl.BlockSpec(memory_space=pltpu.SMEM)] + [vmem] * (len(arrays) + 1),
        out_specs=[vmem] * (3 * count),
        out_shape=[jax.ShapeDtypeStruct(x.shape, wide_type) for x in masters] * 3,
        name="update_params",
    )(scalars, squares, *arrays)


def feed_kernel(
    place_ref, rows_ref, grad_ref, weight_ref, part_ref, product_ref, gate, up, gate_grad, up_grad
):
    step = pl.program_id(0)
    half = pl.num_programs(0) // 2
    depth = weight_ref.shape[1]

    @pl.when(step < half)
    def _():
        part = rows_ref[:, pl.ds(pl.multiple_of(step * depth, depth), depth)]

        @pl.when(step == 0)
        def _():
            gate[...] = mm(part, weight_ref[0])
            up[...] = mm(part, weight_ref[1])

        @pl.when(step > 0)
        def _():
            gate[...] += mm(part, weight_ref[0])
            up[...] += mm(part, weight_ref[1])

    @pl.when(step == half)
    def _():
        gate_val, up_val, grad = gate[...], up[...], grad_ref[...].astype(wide_type)
        sigma = 1.0 / (1.0 + jnp.exp(-gate_val))
        swish = gate_val * sigma
        product_ref[...] = (swish * up_val).astype(low_type)
        up_grad[...] = (swish * grad).astype(low_type)
        slope = sigma * (1.0 + gate_val * (1.0 - sigma))
        gate_grad[...] = (slope * up_val * grad).astype(low_type)

    @pl.when(step >= half)
    def _():
        part_ref[...] = (
            mm_nt(gate_grad[...], weight_ref[0]) + mm_nt(up_grad[...], weight_ref[1])
        ).astype(low_type)


def feed(place, rows_in, product_grad, w_gate_up):
    local, dim = rows_in.shape
    hidden = w_gate_up.shape[2]
    depth = 512
    half = dim // depth
    return pl.pallas_call(
        feed_kernel,
        grid_spec=pltpu.PrefetchScalarGridSpec(
            num_scalar_prefetch=1,
            grid=(2 * half,),
            in_specs=[
                pl.BlockSpec((local, dim), lambda i, place: (0, 0)),
                pl.BlockSpec((local, hidden), lambda i, place: (place[0], 0)),
                pl.BlockSpec((2, depth, hidden), lambda i, place: (0, lax.rem(i, half), 0)),
            ],
            out_specs=[
                pl.BlockSpec((local, depth), lambda i, place: (0, jnp.maximum(i - half, 0))),
                pl.BlockSpec((local, hidden), lambda i, place: (0, 0)),
            ],
            scratch_shapes=[
                pltpu.VMEM((local, hidden), wide_type),
                pltpu.VMEM((local, hidden), wide_type),
                pltpu.VMEM((local, hidden), low_type),
                pltpu.VMEM((local, hidden), low_type),
            ],
        ),
        out_shape=[
            jax.ShapeDtypeStruct((local, dim), low_type),
            jax.ShapeDtypeStruct((local, hidden), low_type),
        ],
        compiler_params=pltpu.CompilerParams(vmem_limit_bytes=vmem_bytes),
        cost_estimate=pl.CostEstimate(
            flops=8 * local * dim * hidden,
            bytes_accessed=4 * w_gate_up.size,
            transcendentals=local * hidden,
        ),
        name="feed",
    )(place, rows_in, product_grad, w_gate_up)


def shift(values_in, step, first, last, ranks):
    pairs = [(k, k + step) for k in range(first, last + 1) if 0 <= k + step < ranks]
    return lax.ppermute(values_in, "tensor", pairs)


def scatter_sum(joined, tensor_ranks, cuts):
    bits = lax.axis_size("dp").bit_length() - 1
    place = lax.axis_index("dp")
    size = lax.axis_size("dp")
    cols = joined.shape[1]
    depth = joined.shape[0] // size
    split = cols // 256 * 128

    def halve(block, spans, bit):
        axis = spans.index(bit)
        mine = (place >> bit) & 1
        away = lax.dynamic_index_in_dim(block, 1 - mine, axis, keepdims=False)
        kept = lax.dynamic_index_in_dim(block, mine, axis, keepdims=False)
        came = lax.ppermute(away, "dp", [(k, k ^ (1 << bit)) for k in range(size)])
        total = kept.astype(wide_type) + came.astype(wide_type)
        return total.astype(low_type), spans[:axis] + spans[axis + 1 :]

    spans = list(range(bits - 1, -1, -1))
    block = joined.reshape((2,) * bits + (depth, cols))
    block, spans = halve(block, spans, 0)
    parts = []
    for index, part in enumerate((block[..., :split], block[..., split:])):
        left = list(spans)
        order = list(reversed(spans)) if index == 0 else list(spans)
        for bit in order:
            part, left = halve(part, left, bit)
        parts.append(part)
    block = jnp.concatenate(parts, axis=1).reshape(tensor_ranks, depth // tensor_ranks, cols)
    rank = lax.axis_index("tensor")
    came = []
    for k in range(1, tensor_ranks):
        away = lax.dynamic_index_in_dim(block, (rank + k) % tensor_ranks, 0, keepdims=False)
        pairs = [(j, (j + k) % tensor_ranks) for j in range(tensor_ranks)]
        came.append(lax.ppermute(away, "tensor", pairs))
    *totals, squares = gather_sum(rank.astype(jnp.int32)[None], block, came, cuts)
    return totals, squares


def on_device(
    piece_table,
    piece_ids,
    piece_counts,
    text_ids,
    text_lengths,
    lm_gains,
    w_query,
    w_kv,
    w_attn_out,
    w_gate_up,
    w_down,
    cotangent,
    step_count,
    hyper_qkv,
    hyper_out,
    hyper_in,
    hyper_back,
    hyper_proj,
    hyper_norms,
    first_qkv,
    first_out,
    first_in,
    first_back,
    first_proj,
    first_norms,
    second_qkv,
    second_out,
    second_in,
    second_back,
    second_proj,
    second_norms,
):
    axes = ("dp", "tensor")
    rank = lax.axis_index("tensor")
    ranks = lax.axis_size("tensor")
    seq_len = text_ids.shape[1]
    local = seq_len // ranks
    length = text_lengths[0]
    gains = lm_gains.astype(jnp.float32)
    cosine, sine_rows = rope_tables(seq_len, LHD)
    start_row = rank * local
    cosine = lax.dynamic_slice_in_dim(cosine[:, 0], start_row, local, 0)
    sine_rows = lax.dynamic_slice_in_dim(sine_rows[:, 0], start_row, local, 0)
    early_half = (jnp.arange(LHD) < LHD // 2)[None, :]
    sine_low = jnp.where(early_half, -sine_rows, 0.0)
    sine_high = jnp.where(early_half, 0.0, sine_rows)
    zeros = jnp.zeros_like(sine_rows)
    tables = [jnp.concatenate([part, part], axis=1) for part in (cosine, sine_low, sine_high)]
    tables += [
        jnp.concatenate(part, axis=1)
        for part in ((cosine, zeros + 1.0), (sine_low, zeros), (sine_high, zeros))
    ]
    entry_rows, slots = piece_ids.shape
    pairs = piece_ids[:, 0::2] + piece_ids[:, 1::2] * 65536
    words = jnp.concatenate(
        [pairs, piece_counts[:, None], jnp.zeros((entry_rows, 3), jnp.int32)], axis=1
    )
    words = words.reshape(entry_rows * 8 // 128, 128)
    words = lax.all_gather(words, "dp", axis=0, tiled=True)

    def from_rank(values_in, step):
        pairs = [(j, (j + step) % ranks) for j in range(ranks)]
        return lax.ppermute(values_in, "tensor", pairs)

    rows = hyper_qkv.shape[0]
    width = hyper_out.shape[1]
    fold = hyper_in.shape[1] // width
    packed = jnp.concatenate(
        [
            hyper_qkv,
            hyper_out,
            hyper_in.reshape(rows, width, fold).swapaxes(1, 2).reshape(rows, fold * width),
            hyper_proj,
            hyper_back.reshape(rows, fold * width),
            jnp.pad(hyper_norms.T, ((0, 0), (0, 124))),
        ],
        axis=1,
    ).astype(jnp.bfloat16)
    dim = w_query.shape[0]
    chunk = 256
    chunk_count = dim // chunk
    head_cols = w_query.shape[1]
    kv_local = jnp.concatenate([w_kv[0], w_kv[1]], axis=1)
    spread_out = lax.axis_size("dp") == chunk_count
    if spread_out:
        mine = lax.dynamic_slice_in_dim(kv_local, lax.axis_index("dp") * chunk, chunk, 0)
        mine = mine.reshape(chunk // rows, rows, 128).swapaxes(0, 1).reshape(rows, -1)
        packed = jnp.concatenate([packed, mine], axis=1)
    stacked = jnp.stack([packed] + [from_rank(packed, k) for k in range(1, ranks)])
    packed = jnp.concatenate(
        [
            lax.dynamic_index_in_dim(stacked, (rank - k) % ranks, 0, keepdims=False)
            for k in range(ranks)
        ],
        axis=0,
    )
    own_query = w_query.reshape(chunk_count, 1, chunk, head_cols)
    own_out = w_attn_out.reshape(head_cols // chunk, chunk, chunk_count, chunk)
    own_out = own_out.transpose(2, 1, 0, 3).reshape(chunk_count, 1, chunk, head_cols)
    words, packed, tables, gains = lax.optimization_barrier((words, packed, tables, gains))
    words = lax.all_gather(words, "tensor", axis=0, tiled=True)
    words, rank_done, late_grad = lax.optimization_barrier(
        (words, lax.axis_index("dp"), cotangent[0])
    )
    gathered = lax.all_gather(packed, "dp", axis=0, tiled=True)
    param_cols = hyper_qkv.shape[1] + width + 2 * fold * width + dim + 128
    params = gathered

    def attn_chunk(index):
        start = index * chunk
        out_cols = lax.dynamic_slice_in_dim(w_attn_out, start, chunk, 1)
        return jnp.concatenate(
            [lax.dynamic_slice_in_dim(w_query, start, chunk, 0)]
            + [out_cols[k : k + chunk] for k in range(0, head_cols, chunk)],
            axis=1,
        )

    if spread_out:
        mine = attn_chunk(rank_done)
        rest_all = jnp.concatenate([from_rank(mine, k) for k in range(1, ranks)], axis=0)
        wkv_all = gathered[:, param_cols:].reshape(
            chunk_count, ranks, rows, chunk // rows, 128
        )
        wkv_all = wkv_all.swapaxes(2, 3).reshape(chunk_count, ranks, chunk, 128)
    else:
        own_all = jnp.concatenate([own_query, own_out], axis=3)
        rest_all = jnp.concatenate([from_rank(own_all, k) for k in range(1, ranks)], axis=1)
        wkv_all = lax.all_gather(
            kv_local.reshape(chunk_count, chunk, 128), "tensor", axis=1, tiled=False
        )

    my_ids = lax.dynamic_slice_in_dim(text_ids[0], rank * local, local, 0)
    owner = my_ids // entry_rows
    place = (owner % ranks) * lax.axis_size("dp") + owner // ranks
    my_words = words[place * (entry_rows // 16) + (my_ids % entry_rows) // 16]
    pick = (jnp.arange(16)[None, :] == (my_ids % 16)[:, None])[:, :, None]
    my_words = jnp.sum(jnp.where(pick, my_words.reshape(local, 16, 8), 0), axis=1)
    my_pieces = jnp.stack([my_words[:, :4] % 65536, my_words[:, :4] // 65536], axis=2)
    my_counts = my_words[:, 4]
    pieces = piece_table[my_pieces.reshape(local * slots)]
    live = (jnp.arange(slots)[None, :] < my_counts[:, None]).astype(jnp.float32)
    live_rows = live.reshape(local * slots, 1)
    counts = my_counts.astype(jnp.float32)[:, None]
    alive = (jnp.arange(seq_len) < length)[:, None]
    out_low = jnp.where(alive, late_grad, jnp.zeros((), jnp.bfloat16))
    product_grad = jnp.einsum("ld,fd->lf", out_low, w_down, preferred_element_type=jnp.float32)
    pieces, live_rows, counts, rest_all, product_grad, own_out = lax.optimization_barrier(
        (pieces, live_rows, counts, rest_all, product_grad, own_out)
    )
    rest_query, rest_out = rest_all[..., :head_cols], rest_all[..., head_cols:]
    if spread_out:
        rest_query, rest_out = (
            lax.all_gather(part, "dp", axis=0, tiled=True).reshape(
                chunk_count, ranks - 1, chunk, head_cols
            )
            for part in (rest_query, rest_out)
        )
    qkv, mixed, mid_rows, pre, pooled, embed, norms = hyper_forward(
        params, param_cols, pieces, live_rows, counts, slots, dim
    )


    scalars = jnp.stack([start_row, length, rank]).astype(jnp.int32)
    both, lead = project_both(scalars, embed, gains, tables, wkv_all)
    blocks = [both] + [from_rank(both, k) for k in range(1, ranks)]
    query = project(lead, tables, own_query, rest_query)
    attn_mixed, logs = attend(scalars, query, blocks)
    resid_mid, mlp_own = attend_out(attn_mixed, embed, gains, own_out, rest_out)

    def plus(left, right):
        return (left.astype(wide_type) + right.astype(wide_type)).astype(low_type)

    top = ranks - 1
    table_of = lambda *values_in: jnp.array(values_in, jnp.int32)[rank]
    near, mid_index, far = table_of(1, 2, 3, 2), table_of(2, 0, 1, 1), table_of(3, 3, 0, 0)
    order = (rank.astype(jnp.int32), near, mid_index, far)
    up_one, down_one = shift(mlp_own, 1, 0, top, ranks), shift(mlp_own, -1, 0, top, ranks)
    own_done = feed(order[0][None], mlp_own, product_grad, w_gate_up)
    up_one, down_one, own_done = lax.optimization_barrier((up_one, down_one, own_done))
    up_two, down_two = shift(up_one, 1, 1, top, ranks), shift(down_one, -1, 0, top - 1, ranks)
    near_rows = jnp.where(rank == top, up_one, down_one)
    near_done = feed(near[None], near_rows, product_grad, w_gate_up)
    up_two, down_two, near_done = lax.optimization_barrier((up_two, down_two, near_done))
    up_three, down_three = shift(up_two, 1, 2, top, ranks), shift(down_two, -1, 0, 1, ranks)
    mid_in = jnp.where(rank == 0, down_two, jnp.where(rank == top, up_two, up_one))
    mid_done = feed(mid_index[None], mid_in, product_grad, w_gate_up)
    up_three, down_three, mid_done = lax.optimization_barrier((up_three, down_three, mid_done))
    far_rows = jnp.where(
        rank == 0,
        down_three,
        jnp.where(rank == 1, down_two, jnp.where(rank == 2, up_two, up_three)),
    )
    far_done = feed(far[None], far_rows, product_grad, w_gate_up)
    products = jnp.zeros((seq_len, w_down.shape[0]), low_type)
    sums = []
    for index, (part, product) in zip(order, (own_done, near_done, mid_done, far_done)):
        sums.append(part)
        products = lax.dynamic_update_slice_in_dim(products, product, index * local, 0)
    part_own, part_near, part_mid, part_far = sums
    pre, qkv, part_far = lax.optimization_barrier((pre, qkv, part_far))
    down_came = shift(part_far, -1, top, top, ranks)
    up_came = shift(part_far, 1, 0, 0, ranks)
    hidden, slope = bends(pre)
    down_came, up_came, hidden, slope, qkv = lax.optimization_barrier(
        (down_came, up_came, hidden, slope, qkv)
    )
    down_came = shift(
        plus(jnp.where(rank == top, part_mid, part_far), down_came), -1, top - 1, top, ranks
    )
    up_came = shift(plus(jnp.where(rank == 0, part_mid, part_far), up_came), 1, 0, 1, ranks)
    probs = slot_probs(qkv, live_rows, slots)
    cot_own = lax.dynamic_slice_in_dim(cotangent[0], start_row, local, 0)
    down_came, up_came, probs, cot_own = lax.optimization_barrier(
        (down_came, up_came, probs, cot_own)
    )
    down_came = shift(
        plus(jnp.where(rank == top, part_near, part_mid), down_came), -1, 1, top, ranks
    )
    up_came = shift(plus(part_near, up_came), 1, 0, top - 1, ranks)
    mlp_grad = (
        part_own.astype(wide_type) + down_came.astype(wide_type) + up_came.astype(wide_type)
    ).astype(low_type)
    down_part = jnp.dot(products, w_down, preferred_element_type=jnp.float32).astype(jnp.bfloat16)
    mlp_grad, down_low, down_high = lax.optimization_barrier(
        (mlp_grad, down_part[:, : dim // 2], down_part[:, dim // 2 :])
    )
    low_own = lax.psum_scatter(down_low, "tensor", scatter_dimension=0, tiled=True)
    resid_grad, query_grad, *block_grads = attend_back(
        scalars, mlp_grad, cot_own, resid_mid, gains, query, blocks, attn_mixed, logs, tables,
        own_out, rest_out,
    )
    for k in range(1, ranks):
        block_grads[k] = from_rank(block_grads[k], -k)
    query_part = project_back_query(query_grad, own_query, rest_query)
    block_grads, query_part, down_high = lax.optimization_barrier(
        (block_grads, query_part, down_high)
    )
    high_own = lax.psum_scatter(down_high, "tensor", scatter_dimension=0, tiled=True)
    half = dim // 2
    layer_low = (resid_mid[:, :half] + low_own.astype(wide_type)).astype(low_type)
    embed_grad = project_back(
        scalars, embed, gains, resid_grad, query_part, tables, block_grads, wkv_all
    )
    embed_grad, layer_low = lax.optimization_barrier((embed_grad, layer_low))
    output_low = lax.all_gather(layer_low, "tensor", axis=0, tiled=True)
    shard = hyper_backward(
        params, param_cols, norms, embed_grad, pooled, pieces, live_rows, counts, qkv, mixed,
        mid_rows, hidden, slope, probs, slots,
    )
    shard, high_own, output_low = lax.optimization_barrier((shard, high_own, output_low))
    layer_high = (resid_mid[:, half:] + high_own.astype(wide_type)).astype(low_type)
    shard, layer_high = lax.optimization_barrier((shard, layer_high))
    output_high = lax.all_gather(layer_high, "tensor", axis=0, tiled=True)
    lm_output = join_columns(output_low, output_high)[None]
    cuts = [0]
    for extent in (3 * width, width, fold * width, dim, fold * width, 128):
        cuts.append(cuts[-1] + extent)
    (qkv_shard, out_shard, in_shard, proj_shard, back_shard, norm_shard), squares = scatter_sum(
        shard, ranks, cuts
    )
    in_shard = in_shard.reshape(rows, fold, width).swapaxes(1, 2)
    grad_shards = (
        qkv_shard,
        out_shard,
        in_shard.reshape(rows, fold * width),
        back_shard.reshape(rows * fold, width),
        proj_shard,
        norm_shard[:, :4].T,
    )
    squares, lm_output = lax.optimization_barrier((squares, lm_output))
    for bit in range(lax.axis_size("dp").bit_length() - 1):
        pairs = [(k, k ^ (1 << bit)) for k in range(lax.axis_size("dp"))]
        squares = squares + lax.ppermute(squares, "dp", pairs)
    for bit in range(ranks.bit_length() - 1):
        pairs = [(k, k ^ (1 << bit)) for k in range(ranks)]
        squares = squares + lax.ppermute(squares, "tensor", pairs)
    square_sum = squares[0, 0]
    grad_norm = jnp.sqrt(square_sum)
    step_value = step_count[0].astype(jnp.float32)
    first_fix = 1.0 - jnp.power(beta_one, step_value)
    second_fix = 1.0 - jnp.power(beta_two, step_value)
    masters = (hyper_qkv, hyper_out, hyper_in, hyper_back, hyper_proj, hyper_norms)
    firsts = (first_qkv, first_out, first_in, first_back, first_proj, first_norms)
    seconds = (second_qkv, second_out, second_in, second_back, second_proj, second_norms)
    factors = jnp.stack([first_fix, second_fix])
    return (
        lm_output,
        grad_norm,
        *update_params(factors, squares, grad_shards, masters, firsts, seconds),
    )


def solution(mesh):
    in_specs = (
        P(),
        P(("dp", "tensor"), None),
        P(("dp", "tensor")),
        P("dp", None),
        P("dp"),
        P(),
        P(None, "tensor"),
        P(None, None, "tensor"),
        P("tensor", None),
        P(None, None, "tensor"),
        P("tensor", None),
        P("dp", None, None),
        P(),
        P(("dp", "tensor"), None),
        P(("dp", "tensor"), None),
        P(("dp", "tensor"), None),
        P(("dp", "tensor"), None),
        P(("dp", "tensor"), None),
        P(None, ("dp", "tensor")),
        P(("dp", "tensor"), None),
        P(("dp", "tensor"), None),
        P(("dp", "tensor"), None),
        P(("dp", "tensor"), None),
        P(("dp", "tensor"), None),
        P(None, ("dp", "tensor")),
        P(("dp", "tensor"), None),
        P(("dp", "tensor"), None),
        P(("dp", "tensor"), None),
        P(("dp", "tensor"), None),
        P(("dp", "tensor"), None),
        P(None, ("dp", "tensor")),
    )
    out_specs = (
        P("dp", None, None),
        P(),
        P(("dp", "tensor"), None),
        P(("dp", "tensor"), None),
        P(("dp", "tensor"), None),
        P(("dp", "tensor"), None),
        P(("dp", "tensor"), None),
        P(None, ("dp", "tensor")),
        P(("dp", "tensor"), None),
        P(("dp", "tensor"), None),
        P(("dp", "tensor"), None),
        P(("dp", "tensor"), None),
        P(("dp", "tensor"), None),
        P(None, ("dp", "tensor")),
        P(("dp", "tensor"), None),
        P(("dp", "tensor"), None),
        P(("dp", "tensor"), None),
        P(("dp", "tensor"), None),
        P(("dp", "tensor"), None),
        P(None, ("dp", "tensor")),
    )
    return jax.shard_map(
        on_device, mesh=mesh, in_specs=in_specs, out_specs=out_specs, check_vma=False
    )
```

```python
import functools

import jax
import jax.numpy as jnp
from jax import lax
from jax.experimental import pallas as pl
from jax.experimental.pallas import tpu as pltpu
from jax.sharding import PartitionSpec as P

HHD = 64
LHD = 64


eps_norm = 1e-05
learn_rate = 0.05
norms_rate = 0.5
beta_one = 0.9
beta_two = 0.999
adam_eps = 1e-08
weight_decay = 0.1
clip_max = 1.0
masked = -1e30


def rope_tables(seq_len, head_width):
    half_width = head_width // 2
    frequency = 10000.0 ** (-jnp.arange(half_width, dtype=jnp.float32) * 2.0 / head_width)
    angles = jnp.arange(seq_len, dtype=jnp.float32)[:, None] * frequency[None, :]
    cosine = jnp.concatenate([jnp.cos(angles), jnp.cos(angles)], axis=1)
    sine_rows = jnp.concatenate([jnp.sin(angles), jnp.sin(angles)], axis=1)
    return (cosine[:, None, :], sine_rows[:, None, :])


def rms_norm(values_in, gain):
    return (
        values_in
        * lax.rsqrt(jnp.mean(values_in * values_in, axis=-1, keepdims=True) + eps_norm)
        * gain
    )


def softmax_rows(scores):
    row_top = jnp.max(scores, axis=-1, keepdims=True)
    exp_scores = jnp.exp(scores - row_top)
    return exp_scores / jnp.sum(exp_scores, axis=-1, keepdims=True)


low_type = jnp.bfloat16
wide_type = jnp.float32
vmem_bytes = 62 * 1024 * 1024


def mm(left, right):
    return lax.dot_general(
        left, right, (((1,), (0,)), ((), ())), preferred_element_type=wide_type
    )


def mm_nt(left, right):
    return lax.dot_general(
        left, right, (((1,), (1,)), ((), ())), preferred_element_type=wide_type
    )


def mm_tn(left, right):
    return lax.dot_general(
        left, right, (((0,), (0,)), ((), ())), preferred_element_type=wide_type
    )


def half_masks():
    lane = lax.broadcasted_iota(jnp.int32, (1, 128), 1)
    first = (lane < LHD).astype(wide_type).astype(low_type)
    second = (lane >= LHD).astype(wide_type).astype(low_type)
    return first, second


def stack_heads(pair, first, second):
    return jnp.concatenate([pair * first, pair * second], axis=0)


def norm_hat(values_in):
    centred = values_in - jnp.mean(values_in, axis=-1, keepdims=True)
    scale = lax.rsqrt(jnp.mean(centred * centred, axis=-1, keepdims=True) + eps_norm)
    return centred * scale, scale


def norm_back(hat, scale, grad):
    return scale * (
        grad
        - jnp.mean(grad, axis=-1, keepdims=True)
        - hat * jnp.mean(grad * hat, axis=-1, keepdims=True)
    )


def rms_back(values_in, gain, grad):
    scale = lax.rsqrt(jnp.mean(values_in * values_in, axis=-1, keepdims=True) + eps_norm)
    scaled = grad * gain
    hat = values_in * scale
    return scale * (scaled - hat * jnp.mean(scaled * hat, axis=-1, keepdims=True))


gelu_in = 0.7978845608028654
gelu_cube = 0.044715


def slot_mask(live, slots, axis=0):
    row_entry = lax.broadcasted_iota(jnp.int32, (128, 128), 0) // slots
    col_entry = lax.broadcasted_iota(jnp.int32, (128, 128), 1) // slots
    keep = jnp.where(row_entry == col_entry, live, 0.0)
    bias = jnp.where(keep > 0.0, 0.0, masked)
    return jnp.concatenate([bias, bias], axis=axis)


def slot_softmax(stacked, keys, bias):
    scores = mm_nt(keys, stacked) * (HHD ** (-0.5)) + bias
    exp_scores = jnp.exp(scores - jnp.max(scores, axis=0, keepdims=True))
    return exp_scores / jnp.sum(exp_scores, axis=0, keepdims=True)


def hyper_forward_kernel(
    slots, piece_ref, live_ref, count_ref, param_ref,
    qkv_ref, mixed_ref, second_ref, pre_ref, pool_ref, embed_ref, norm_ref,
):
    tile, width = piece_ref.shape

    @pl.when(pl.program_id(0) == 0)
    def _():
        norm_ref[...] = param_ref[:, param_ref.shape[1] - 128 :].astype(wide_type).T[0:8]

    first, second = half_masks()
    inputs = piece_ref[...].astype(wide_type)
    lead = (norm_hat(inputs)[0] * norm_ref[0:1] + norm_ref[1:2]).astype(low_type)
    for k in range(3):
        part = slice(k * width, (k + 1) * width)
        qkv_ref[:, part] = mm(lead, param_ref[:, part]).astype(low_type)
    low_lane = lax.broadcasted_iota(jnp.int32, (1, 128), 1) < HHD

    for block in range(tile // 128):
        rows = slice(block * 128, (block + 1) * 128)
        bias = slot_mask(live_ref[rows], slots, 1)
        for col in range(0, width, 128):
            stacked = stack_heads(qkv_ref[rows, col : col + 128], first, second)
            keys = qkv_ref[rows, width + col : width + col + 128]
            values = qkv_ref[rows, 2 * width + col : 2 * width + col + 128]
            prob = slot_softmax(stacked, keys, bias).astype(low_type)
            both = mm_tn(prob, values)
            mixed_ref[rows, col : col + 128] = jnp.where(low_lane, both[:128], both[128:]).astype(
                low_type
            )
    start = 3 * width
    second_in = inputs + mm(mixed_ref[...], param_ref[:, start : start + width])
    second_ref[...] = second_in
    mid = (norm_hat(second_in)[0] * norm_ref[2:3] + norm_ref[3:4]).astype(low_type)
    hidden_count = pre_ref.shape[1]
    start = start + width
    proj = start + hidden_count
    back = proj + embed_ref.shape[1]
    third = second_in
    for col in range(0, hidden_count, width):
        pre = mm(mid, param_ref[:, start + col : start + col + width])
        pre_ref[:, col : col + width] = pre.astype(low_type)
        hidden = (
            0.5 * pre * (1.0 + jnp.tanh(gelu_in * (pre + gelu_cube * pre * pre * pre)))
        ).astype(low_type)
        third = third + mm(hidden, param_ref[:, back + col : back + col + width])
    third = jnp.where(live_ref[...] > 0.0, third, 0.0)
    pooled = jnp.sum(third.reshape(tile // slots, slots, width), axis=1) / count_ref[...]
    pooled = pooled.astype(low_type)
    pool_ref[...] = pooled
    embed_ref[...] = mm(pooled, param_ref[:, proj:back]).astype(low_type)


def hyper_forward(
    params, param_cols, pieces, live_rows, counts, slots, dim
):
    row_count, width = pieces.shape
    tile = 256
    fold = (param_cols - 128 - dim - 4 * width) // 2
    by_row = lambda cols: pl.BlockSpec((tile, cols), lambda i: (i, 0))
    by_entry = lambda cols: pl.BlockSpec((tile // slots, cols), lambda i: (i, 0))
    entries = row_count // slots
    struct = jax.ShapeDtypeStruct
    return pl.pallas_call(
        functools.partial(hyper_forward_kernel, slots),
        grid=(row_count // tile,),
        in_specs=[
            by_row(width),
            by_row(1),
            by_entry(1),
            pl.BlockSpec((width, param_cols), lambda i: (0, 0), pipeline_mode=pl.Buffered(1)),
        ],
        out_specs=[
            by_row(3 * width), by_row(width), by_row(width), by_row(fold),
            by_entry(width), by_entry(dim), pl.BlockSpec((8, width), lambda i: (0, 0)),
        ],
        out_shape=[
            struct((row_count, 3 * width), low_type),
            struct((row_count, width), low_type),
            struct((row_count, width), wide_type),
            struct((row_count, fold), low_type),
            struct((entries, width), low_type),
            struct((entries, dim), low_type),
            struct((8, width), wide_type),
        ],
        compiler_params=pltpu.CompilerParams(vmem_limit_bytes=vmem_bytes),
        cost_estimate=pl.CostEstimate(
            flops=2 * row_count * width * 12 * width,
            bytes_accessed=2 * params.size + 12 * row_count * width,
            transcendentals=row_count * fold,
        ),
        name="hyper_forward",
    )(pieces, live_rows, counts, params)


def bend_kernel(pre_ref, hidden_ref, slope_ref):
    for col in range(0, pre_ref.shape[1], 512):
        part = slice(col, col + 512)
        pre = pre_ref[:, part].astype(wide_type)
        square = pre * pre
        bend = jnp.tanh(gelu_in * pre * (1.0 + gelu_cube * square))
        hidden_ref[:, part] = (0.5 * pre * (1.0 + bend)).astype(low_type)
        slope = 0.5 * (1.0 + bend) + 0.5 * pre * (1.0 - bend * bend) * gelu_in * (
            1.0 + 3.0 * gelu_cube * square
        )
        slope_ref[:, part] = slope.astype(low_type)


def bends(pre):
    rows, cols = pre.shape
    tile = 256
    spec = pl.BlockSpec((tile, cols), lambda i: (i, 0))
    struct = jax.ShapeDtypeStruct(pre.shape, low_type)
    return pl.pallas_call(
        bend_kernel,
        grid=(rows // tile,),
        in_specs=[spec],
        out_specs=[spec, spec],
        out_shape=[struct, struct],
        cost_estimate=pl.CostEstimate(
            flops=20 * pre.size, bytes_accessed=6 * pre.size, transcendentals=pre.size
        ),
        name="bends",
    )(pre)


def slot_prob_kernel(slots, qkv_ref, live_ref, prob_ref):
    tile = live_ref.shape[0]
    width = qkv_ref.shape[1] // 3
    first, second = half_masks()
    for block in range(tile // 128):
        rows = slice(block * 128, (block + 1) * 128)
        bias = slot_mask(live_ref[rows], slots, 1)
        for col in range(0, width, 128):
            stacked = stack_heads(qkv_ref[rows, col : col + 128], first, second)
            keys = qkv_ref[rows, width + col : width + col + 128]
            prob = slot_softmax(stacked, keys, bias)
            prob_ref[rows, 2 * col : 2 * col + 256] = prob.astype(low_type)


def slot_probs(qkv, live_rows, slots):
    rows, cols = qkv.shape
    tile = 256
    width = cols // 3
    return pl.pallas_call(
        functools.partial(slot_prob_kernel, slots),
        grid=(rows // tile,),
        in_specs=[
            pl.BlockSpec((tile, cols), lambda i: (i, 0)),
            pl.BlockSpec((tile, 1), lambda i: (i, 0)),
        ],
        out_specs=pl.BlockSpec((tile, 2 * width), lambda i: (i, 0)),
        out_shape=jax.ShapeDtypeStruct((rows, 2 * width), low_type),
        cost_estimate=pl.CostEstimate(
            flops=600 * rows * width, bytes_accessed=10 * rows * width,
            transcendentals=2 * rows * width,
        ),
        name="slot_probs",
    )(qkv, live_rows)


def hyper_backward_kernel(
    slots, grad_ref, pool_ref, piece_ref, live_ref, count_ref, qkv_ref, mixed_ref, second_ref,
    hidden_ref, slope_ref, prob_ref, param_ref, norm_ref, out_ref,
    sums, norm_sums, mix_grad, qkv_grad, pre_grad,
):
    tile, width = piece_ref.shape
    hidden_count = hidden_ref.shape[1]
    dim = grad_ref.shape[1]
    out_at = 3 * width
    in_at = out_at + width
    proj = in_at + hidden_count
    back = proj + dim
    first, second = half_masks()

    @pl.when(pl.program_id(0) == 0)
    def _():
        sums[...] = jnp.zeros_like(sums)
        norm_sums[...] = jnp.zeros_like(norm_sums)

    embed_grad = grad_ref[...]
    pooled = pool_ref[...]
    for col in range(0, dim, width):
        part = slice(proj + col, proj + col + width)
        sums[:, part] += mm_tn(pooled, embed_grad[:, col : col + width])
    pool_grad = mm_nt(embed_grad, param_ref[:, proj:back]) / count_ref[...]
    spread = jnp.broadcast_to(pool_grad[:, None, :], (tile // slots, slots, width))
    third_grad = jnp.where(live_ref[...] > 0.0, spread.reshape(tile, width), 0.0)
    back_in = third_grad.astype(low_type)
    for col in range(0, hidden_count, width):
        hidden_grad = mm_nt(back_in, param_ref[:, back + col : back + col + width])
        slope = slope_ref[:, col : col + width].astype(wide_type)
        pre_grad[:, col : col + width] = (slope * hidden_grad).astype(low_type)
        part = slice(back + col, back + col + width)
        sums[:, part] += mm_tn(back_in, hidden_ref[:, col : col + width])
    second_in = second_ref[...]
    hat, scale = norm_hat(second_in)
    mid = (hat * norm_ref[2:3] + norm_ref[3:4]).astype(low_type)
    mid_grad = jnp.zeros((tile, width), wide_type)
    for col in range(0, hidden_count, width):
        part = slice(in_at + col, in_at + col + width)
        grads = pre_grad[:, col : col + width]
        sums[:, part] += mm_tn(mid, grads)
        mid_grad = mid_grad + mm_nt(grads, param_ref[:, part])
    norm_sums[2:3] += jnp.sum(mid_grad * hat, axis=0, keepdims=True)
    norm_sums[3:4] += jnp.sum(mid_grad, axis=0, keepdims=True)
    second_grad = third_grad + norm_back(hat, scale, mid_grad * norm_ref[2:3])
    out_in = second_grad.astype(low_type)
    sums[:, out_at:in_at] += mm_tn(mixed_ref[...], out_in)
    mix_grad[...] = mm_nt(out_in, param_ref[:, out_at:in_at]).astype(low_type)

    score_scale = HHD ** (-0.5)
    low_lane = lax.broadcasted_iota(jnp.int32, (1, 128), 1) < HHD
    for block in range(tile // 128):
        rows = slice(block * 128, (block + 1) * 128)
        for col in range(0, width, 128):
            stacked = stack_heads(qkv_ref[rows, col : col + 128], first, second)
            keys = qkv_ref[rows, width + col : width + col + 128]
            values = qkv_ref[rows, 2 * width + col : 2 * width + col + 128]
            prob_low = prob_ref[rows, 2 * col : 2 * col + 256]
            prob = prob_low.astype(wide_type)
            grads = stack_heads(mix_grad[rows, col : col + 128], first, second)
            prob_grad = mm_nt(values, grads)
            score_grad = prob * (prob_grad - jnp.sum(prob * prob_grad, axis=0, keepdims=True))
            score_grad = score_grad.astype(low_type)
            key_grad = mm(score_grad, stacked) * score_scale
            value_grad = mm(prob_low, grads)
            both = mm_tn(score_grad, keys)
            query_grad = jnp.where(low_lane, both[:128], both[128:]) * score_scale
            qkv_grad[rows, col : col + 128] = query_grad.astype(low_type)
            qkv_grad[rows, width + col : width + col + 128] = key_grad.astype(low_type)
            qkv_grad[rows, 2 * width + col : 2 * width + col + 128] = value_grad.astype(low_type)

    inputs = piece_ref[...].astype(wide_type)
    hat_one = norm_hat(inputs)[0]
    lead = (hat_one * norm_ref[0:1] + norm_ref[1:2]).astype(low_type)
    lead_grad = jnp.zeros((tile, width), wide_type)
    for col in range(0, 3 * width, width):
        part = slice(col, col + width)
        grads = qkv_grad[:, part]
        sums[:, part] += mm_tn(lead, grads)
        lead_grad = lead_grad + mm_nt(grads, param_ref[:, part])
    norm_sums[0:1] += jnp.sum(lead_grad * hat_one, axis=0, keepdims=True)
    norm_sums[1:2] += jnp.sum(lead_grad, axis=0, keepdims=True)

    @pl.when(pl.program_id(0) == pl.num_programs(0) - 1)
    def _():
        out_ref[:, :back] = sums[:, :back].astype(low_type)
        for col in range(back, back + hidden_count, width):
            out_ref[:, col : col + width] = sums[:, col : col + width].T.astype(low_type)
        out_ref[:, back + hidden_count :] = norm_sums[...].T.astype(low_type)


def hyper_backward(
    params, param_cols, norms, embed_grad, pooled, pieces, live_rows, counts, qkv, mixed,
    second_in, hidden, slope, probs, slots,
):
    row_count, width = pieces.shape
    dim = embed_grad.shape[1]
    fold = hidden.shape[1]
    tile = 512
    by_row = lambda cols: pl.BlockSpec((tile, cols), lambda i: (i, 0))
    by_entry = lambda cols: pl.BlockSpec((tile // slots, cols), lambda i: (i, 0))
    whole = lambda shape: pl.BlockSpec(shape, lambda i: (0, 0), pipeline_mode=pl.Buffered(1))
    return pl.pallas_call(
        functools.partial(hyper_backward_kernel, slots),
        grid=(row_count // tile,),
        in_specs=[
            by_entry(dim),
            by_entry(width),
            by_row(width),
            by_row(1),
            by_entry(1),
            by_row(3 * width),
            by_row(width),
            by_row(width),
            by_row(fold),
            by_row(fold),
            by_row(2 * width),
            whole((width, param_cols)),
            whole(norms.shape),
        ],
        out_specs=whole((width, param_cols)),
        out_shape=jax.ShapeDtypeStruct((width, param_cols), low_type),
        scratch_shapes=[
            pltpu.VMEM((width, param_cols - 128), wide_type),
            pltpu.VMEM((128, width), wide_type),
            pltpu.VMEM((tile, width), low_type),
            pltpu.VMEM((tile, 3 * width), low_type),
            pltpu.VMEM((tile, fold), low_type),
        ],
        compiler_params=pltpu.CompilerParams(vmem_limit_bytes=vmem_bytes),
        cost_estimate=pl.CostEstimate(
            flops=4 * row_count * width * 12 * width,
            bytes_accessed=4 * params.size + 24 * row_count * width,
            transcendentals=row_count * fold,
        ),
        name="hyper_backward",
    )(
        embed_grad, pooled, pieces, live_rows, counts, qkv, mixed, second_in, hidden, slope, probs,
        params, norms,
    )


def turn(values_in, cosine, sine_low, sine_high):
    parts = []
    for col in range(0, values_in.shape[1], 128):
        part = values_in[:, col : col + 128]
        parts.append(
            part * cosine
            + pltpu.roll(part, 96, axis=1) * sine_low
            + pltpu.roll(part, 32, axis=1) * sine_high
        )
    return parts[0] if len(parts) == 1 else jnp.concatenate(parts, axis=1)


def project_both_kernel(
    scalar_ref, embed_ref, gain_ref, kcos_ref, klow_ref, khigh_ref, wkv_ref, both_ref, lead_ref
):
    @pl.when(pl.program_id(0) == 0)
    def _():
        inputs = embed_ref[...].astype(wide_type)
        lead_ref[...] = rms_norm(inputs, gain_ref[0:1]).astype(low_type)

    chunk_count, _, chunk, _ = wkv_ref.shape
    both = jnp.zeros(both_ref.shape, wide_type)
    for k in range(chunk_count):
        both = both + mm(lead_ref[:, k * chunk : (k + 1) * chunk], wkv_ref[k, 0])
    both_ref[...] = turn(both, kcos_ref[...], klow_ref[...], khigh_ref[...]).astype(low_type)


def project_both(scalars, embed, gains, tables, wkv_all):
    local, dim = embed.shape
    chunk_count, ranks, chunk, _ = wkv_all.shape
    whole = lambda shape: pl.BlockSpec(shape, lambda t, place: (0, 0))
    return pl.pallas_call(
        project_both_kernel,
        grid_spec=pltpu.PrefetchScalarGridSpec(
            num_scalar_prefetch=1,
            grid=(ranks,),
            in_specs=[whole((local, dim)), whole(gains.shape)]
            + [whole((local, 128))] * 3
            + [
                pl.BlockSpec(
                    (chunk_count, 1, chunk, 128),
                    lambda t, place: (0, lax.rem(place[2] - t + ranks, ranks), 0, 0),
                )
            ],
            out_specs=[
                pl.BlockSpec((local, 128), lambda t, place: (0, t)), whole((local, dim)),
            ],
        ),
        out_shape=[
            jax.ShapeDtypeStruct((local, ranks * 128), low_type),
            jax.ShapeDtypeStruct((local, dim), low_type),
        ],
        compiler_params=pltpu.CompilerParams(vmem_limit_bytes=vmem_bytes),
        cost_estimate=pl.CostEstimate(
            flops=2 * local * dim * ranks * 128,
            bytes_accessed=2 * dim * ranks * 128 + 4 * local * dim,
            transcendentals=0,
        ),
        name="project_both",
    )(scalars, embed, gains, *tables[3:], wkv_all)


def own_or_rest(own_ref, rest_ref, use):
    @pl.when(pl.program_id(0) == 0)
    def _():
        use(own_ref)

    @pl.when(pl.program_id(0) > 0)
    def _():
        use(rest_ref)


def weight_specs(own_all):
    chunk_count, _, chunk, cols = own_all.shape
    shape = (chunk_count, 1, chunk, cols)
    return [
        pl.BlockSpec(shape, lambda t: (0, 0, 0, 0)),
        pl.BlockSpec(shape, lambda t: (0, jnp.maximum(t - 1, 0), 0, 0)),
    ]


def block_specs(local, count):
    return [
        pl.BlockSpec((local, 128), lambda t, k=k: (0, lax.rem(t - k + count, count)))
        for k in range(count)
    ]


def project_kernel(lead_ref, cos_ref, low_ref, high_ref, own_ref, rest_ref, query_ref):
    def use(wq_ref):
        chunk_count, _, chunk, cols = wq_ref.shape
        query = jnp.zeros((lead_ref.shape[0], cols), wide_type)
        for k in range(chunk_count):
            query = query + mm(lead_ref[:, k * chunk : (k + 1) * chunk], wq_ref[k, 0])
        query = turn(query, cos_ref[...], low_ref[...], high_ref[...])
        query_ref[...] = (query * (LHD ** (-0.5))).astype(low_type)

    own_or_rest(own_ref, rest_ref, use)


def project(lead, tables, own_all, rest_all):
    local, dim = lead.shape
    ranks = rest_all.shape[1] + 1
    cols = own_all.shape[3]
    whole = lambda shape: pl.BlockSpec(shape, lambda t: (0, 0))
    return pl.pallas_call(
        project_kernel,
        grid=(ranks,),
        in_specs=[whole((local, dim))] + [whole((local, 128))] * 3 + weight_specs(own_all),
        out_specs=pl.BlockSpec((local, cols), lambda t: (0, t)),
        out_shape=jax.ShapeDtypeStruct((local, ranks * cols), low_type),
        compiler_params=pltpu.CompilerParams(vmem_limit_bytes=vmem_bytes),
        cost_estimate=pl.CostEstimate(
            flops=2 * local * dim * ranks * cols,
            bytes_accessed=2 * dim * ranks * cols + 4 * local * dim,
            transcendentals=0,
        ),
        name="project",
    )(lead, *tables[:3], own_all, rest_all)


def key_place(start, index, local, seq_len):
    block = index // local
    return lax.rem(start + seq_len - block * local, seq_len) + index - block * local


def attend_kernel(
    scalar_ref, query_ref, own_ref, one_ref, two_ref, three_ref, mixed_ref, log_ref, bias_ref
):
    local = query_ref.shape[0]
    seq_len = bias_ref.shape[1]

    @pl.when(pl.program_id(0) == 0)
    def _():
        row = scalar_ref[0] + lax.broadcasted_iota(jnp.int32, (local, seq_len), 0)
        col = lax.broadcasted_iota(jnp.int32, (1, seq_len), 1)
        col = key_place(scalar_ref[0], col, local, seq_len)
        allowed = jnp.where(col <= row, jnp.where(col < scalar_ref[1], 0.0, masked), masked)
        bias_ref[...] = allowed

    first, second = half_masks()
    lane = lax.broadcasted_iota(jnp.int32, (1, 128), 1)
    both = jnp.concatenate([own_ref[...], one_ref[...], two_ref[...], three_ref[...]], axis=0)
    swapped = pltpu.roll(both.astype(wide_type), LHD, axis=1).astype(low_type)
    keys = both * first + swapped * second
    value_low = swapped * first
    value_high = both * second
    logs = jnp.zeros((local, 128), wide_type)
    for pair in range(query_ref.shape[1] // 128):
        cols = slice(pair * 128, (pair + 1) * 128)
        mixed = jnp.zeros((local, 128), wide_type)
        for half, (mask, values) in enumerate(((first, value_low), (second, value_high))):
            scores = mm_nt(query_ref[:, cols] * mask, keys) + bias_ref[...]
            row_top = jnp.max(scores, axis=-1, keepdims=True)
            exp_scores = jnp.exp(scores - row_top)
            exp_total = jnp.sum(exp_scores, axis=-1, keepdims=True)
            prob = (exp_scores * (1.0 / exp_total)).astype(low_type)
            mixed = mixed + mm(prob, values)
            logs = jnp.where(lane == 2 * pair + half, row_top + jnp.log(exp_total), logs)
        mixed_ref[:, cols] = mixed.astype(low_type)
    log_ref[...] = logs.T[0:8]


def attend(scalars, query, blocks):
    local, dim = query.shape
    ranks = len(blocks)
    seq_len = local * ranks
    cols = dim // ranks
    return pl.pallas_call(
        attend_kernel,
        grid=(ranks,),
        in_specs=[
            pl.BlockSpec(memory_space=pltpu.SMEM),
            pl.BlockSpec((local, cols), lambda t: (0, t)),
        ]
        + block_specs(local, ranks),
        out_specs=[
            pl.BlockSpec((local, cols), lambda t: (0, t)),
            pl.BlockSpec((8, local), lambda t: (t, 0)),
        ],
        out_shape=[
            jax.ShapeDtypeStruct((local, dim), low_type),
            jax.ShapeDtypeStruct((8 * ranks, local), wide_type),
        ],
        scratch_shapes=[pltpu.VMEM((local, seq_len), wide_type)],
        compiler_params=pltpu.CompilerParams(vmem_limit_bytes=vmem_bytes),
        cost_estimate=pl.CostEstimate(
            flops=16 * local * seq_len * dim,
            bytes_accessed=8 * local * dim,
            transcendentals=local * seq_len * dim // LHD,
        ),
        name="attend",
    )(scalars, query, *blocks)


def attend_out_kernel(mixed_ref, embed_ref, gain_ref, wo_own, wo_rest, mid_ref, lead_ref, total):
    @pl.when(pl.program_id(0) == 0)
    def _():
        total[...] = embed_ref[...].astype(wide_type)

    def use(wo_ref):
        chunk_count, _, chunk, cols = wo_ref.shape
        for k in range(chunk_count):
            part = slice(k * chunk, (k + 1) * chunk)
            for col in range(0, cols, chunk):
                total[:, part] += mm(
                    mixed_ref[:, col : col + chunk], wo_ref[k, 0, :, col : col + chunk]
                )

    own_or_rest(wo_own, wo_rest, use)

    @pl.when(pl.program_id(0) == pl.num_programs(0) - 1)
    def _():
        mid_ref[...] = total[...]
        lead_ref[...] = rms_norm(total[...], gain_ref[1:2]).astype(low_type)


def attend_out(mixed, embed, gains, own_all, rest_all):
    local, dim = embed.shape
    ranks = rest_all.shape[1] + 1
    cols = own_all.shape[3]
    whole = lambda shape: pl.BlockSpec(shape, lambda t: (0, 0))
    return pl.pallas_call(
        attend_out_kernel,
        grid=(ranks,),
        in_specs=[
            pl.BlockSpec((local, cols), lambda t: (0, t)), whole((local, dim)), whole(gains.shape),
        ]
        + weight_specs(own_all),
        out_specs=[whole((local, dim)), whole((local, dim))],
        out_shape=[
            jax.ShapeDtypeStruct((local, dim), wide_type),
            jax.ShapeDtypeStruct((local, dim), low_type),
        ],
        scratch_shapes=[pltpu.VMEM((local, dim), wide_type)],
        compiler_params=pltpu.CompilerParams(vmem_limit_bytes=vmem_bytes),
        cost_estimate=pl.CostEstimate(
            flops=2 * local * dim * dim,
            bytes_accessed=2 * dim * dim + 8 * local * dim,
            transcendentals=0,
        ),
        name="attend_out",
    )(mixed, embed, gains, own_all, rest_all)


def attend_back_kernel(
    scalar_ref, mlp_ref, cot_ref, mid_ref, gain_ref, query_ref, own_ref, one_ref, two_ref,
    three_ref, mixed_ref, log_ref, cos_ref, low_ref, high_ref, wo_own, wo_rest,
    resid_ref, qgrad_ref, own_grad, one_grad, two_grad, three_grad, low_grad, bias_ref, out_grad,
):
    local = query_ref.shape[0]
    seq_len = bias_ref.shape[0]

    @pl.when(pl.program_id(0) == 0)
    def _():
        row = scalar_ref[0] + lax.broadcasted_iota(jnp.int32, (local, 1), 0)
        own = jnp.where(row < scalar_ref[1], cot_ref[...].astype(wide_type), 0.0)
        grad = own + rms_back(mid_ref[...], gain_ref[1:2], mlp_ref[...].astype(wide_type))
        resid_ref[...] = grad
        low_grad[...] = grad.astype(low_type)
        col = scalar_ref[0] + lax.broadcasted_iota(jnp.int32, (seq_len, local), 1)
        key = lax.broadcasted_iota(jnp.int32, (seq_len, 1), 0)
        key = key_place(scalar_ref[0], key, local, seq_len)
        bias_ref[...] = jnp.where(
            key <= col, jnp.where(key < scalar_ref[1], 0.0, masked), masked
        )

    def use(wo_ref):
        chunk_count, _, chunk, cols = wo_ref.shape
        for col in range(0, cols, chunk):
            part_sum = jnp.zeros((local, chunk), wide_type)
            for k in range(chunk_count):
                part_sum = part_sum + mm_nt(
                    low_grad[:, k * chunk : (k + 1) * chunk], wo_ref[k, 0, :, col : col + chunk]
                )
            out_grad[:, col : col + chunk] = part_sum.astype(low_type)

    own_or_rest(wo_own, wo_rest, use)
    first, second = half_masks()
    lane = lax.broadcasted_iota(jnp.int32, (1, 128), 1)
    low_lane = lane < LHD
    both = jnp.concatenate([own_ref[...], one_ref[...], two_ref[...], three_ref[...]], axis=0)
    swapped = pltpu.roll(both.astype(wide_type), LHD, axis=1).astype(low_type)
    keys = both * first + swapped * second
    values = swapped * first + both * second
    key_low = both * first
    key_high = swapped * second
    sums = jnp.zeros((local, 128), wide_type)
    for pair in range(query_ref.shape[1] // 128):
        part = slice(pair * 128, (pair + 1) * 128)
        product = mixed_ref[:, part].astype(wide_type) * out_grad[:, part].astype(wide_type)
        one = jnp.sum(jnp.where(low_lane, product, 0.0), axis=-1, keepdims=True)
        two = jnp.sum(jnp.where(low_lane, 0.0, product), axis=-1, keepdims=True)
        sums = jnp.where(lane == 2 * pair, one, sums)
        sums = jnp.where(lane == 2 * pair + 1, two, sums)
    sums = sums.T[0:8]
    key_sum = jnp.zeros((seq_len, 128), wide_type)
    value_sum = jnp.zeros((seq_len, 128), wide_type)
    for pair in range(query_ref.shape[1] // 128):
        part = slice(pair * 128, (pair + 1) * 128)
        query_grad = jnp.zeros((local, 128), wide_type)
        for half, (mask, key_side) in enumerate(((first, key_low), (second, key_high))):
            head = 2 * pair + half
            query = query_ref[:, part] * mask
            grads = out_grad[:, part] * mask
            scores = mm_nt(keys, query) + bias_ref[...]
            prob = jnp.exp(scores - log_ref[head : head + 1])
            prob_grad = mm_nt(values, grads)
            score_grad = (prob * (prob_grad - sums[head : head + 1])).astype(low_type)
            key_sum = key_sum + mm(score_grad, query)
            value_sum = value_sum + mm(prob.astype(low_type), grads)
            query_grad = query_grad + mm_tn(score_grad, key_side)
        query_grad = query_grad * (LHD ** (-0.5))
        spun = query_grad * low_ref[...]
        spin = query_grad * high_ref[...]
        query_grad = (
            query_grad * cos_ref[...]
            + pltpu.roll(spin, 96, axis=1)
            + pltpu.roll(spun, 32, axis=1)
        )
        qgrad_ref[:, part] = query_grad.astype(low_type)
    key_sum = key_sum + pltpu.roll(key_sum, LHD, axis=1)
    value_sum = value_sum + pltpu.roll(value_sum, LHD, axis=1)
    both_grad = jnp.where(low_lane, key_sum, value_sum).astype(low_type)
    for k, ref in enumerate((own_grad, one_grad, two_grad, three_grad)):
        ref[...] = both_grad[k * local : (k + 1) * local]


def attend_back(
    scalars, mlp_grad, cot_own, mid, gains, query, blocks, mixed, logs, tables, own_all, rest_all
):
    local, dim = mid.shape
    ranks = len(blocks)
    seq_len = local * ranks
    cols = own_all.shape[3]
    whole = lambda shape: pl.BlockSpec(shape, lambda t: (0, 0))
    by_block = block_specs(local, ranks)
    by_rank = pl.BlockSpec((local, cols), lambda t: (0, t))
    return pl.pallas_call(
        attend_back_kernel,
        grid=(ranks,),
        in_specs=[
            pl.BlockSpec(memory_space=pltpu.SMEM),
            whole((local, dim)),
            whole((local, dim)),
            whole((local, dim)),
            whole(gains.shape),
            by_rank,
        ]
        + by_block
        + [
            by_rank,
            pl.BlockSpec((8, local), lambda t: (t, 0)),
            whole((local, 128)),
            whole((local, 128)),
            whole((local, 128)),
        ]
        + weight_specs(own_all),
        out_specs=[
            whole((local, dim)),
            by_rank,
        ]
        + by_block,
        out_shape=[
            jax.ShapeDtypeStruct((local, dim), wide_type),
            jax.ShapeDtypeStruct((local, ranks * cols), low_type),
        ]
        + [jax.ShapeDtypeStruct((local, ranks * 128), low_type)] * len(blocks),
        scratch_shapes=[
            pltpu.VMEM((local, dim), low_type),
            pltpu.VMEM((seq_len, local), wide_type),
            pltpu.VMEM((local, cols), low_type),
        ],
        compiler_params=pltpu.CompilerParams(vmem_limit_bytes=vmem_bytes),
        cost_estimate=pl.CostEstimate(
            flops=2 * local * dim * dim + 40 * local * seq_len * dim,
            bytes_accessed=2 * dim * dim + 20 * local * dim,
            transcendentals=local * seq_len * dim // LHD,
        ),
        name="attend_back",
    )(
        scalars, mlp_grad, cot_own, mid, gains, query, *blocks, mixed, logs, *tables[:3], own_all,
        rest_all,
    )


def project_back_query_kernel(qgrad_ref, own_ref, rest_ref, total_ref):
    @pl.when(pl.program_id(0) == 0)
    def _():
        total_ref[...] = jnp.zeros_like(total_ref)

    def use(wq_ref):
        chunk_count, _, chunk, _ = wq_ref.shape
        for k in range(chunk_count):
            total_ref[:, k * chunk : (k + 1) * chunk] += mm_nt(qgrad_ref[...], wq_ref[k, 0])

    own_or_rest(own_ref, rest_ref, use)


def project_back_query(query_grad, own_all, rest_all):
    chunk_count, _, chunk, _ = own_all.shape
    ranks = rest_all.shape[1] + 1
    cols = own_all.shape[3]
    local = query_grad.shape[0]
    dim = chunk_count * chunk
    return pl.pallas_call(
        project_back_query_kernel,
        grid=(ranks,),
        in_specs=[pl.BlockSpec((local, cols), lambda t: (0, t))] + weight_specs(own_all),
        out_specs=pl.BlockSpec((local, dim), lambda t: (0, 0)),
        out_shape=jax.ShapeDtypeStruct((local, dim), wide_type),
        compiler_params=pltpu.CompilerParams(vmem_limit_bytes=vmem_bytes),
        cost_estimate=pl.CostEstimate(
            flops=2 * local * dim * ranks * cols,
            bytes_accessed=2 * dim * ranks * cols + 8 * local * dim,
            transcendentals=0,
        ),
        name="project_back_query",
    )(query_grad, own_all, rest_all)


def project_back_kernel(
    scalar_ref, embed_ref, gain_ref, resid_ref, part_ref, kcos_ref, klow_ref, khigh_ref, own_ref, one_ref,
    two_ref, three_ref, wkv_ref, grad_ref, total,
):
    step = pl.program_id(0)

    @pl.when(step == 0)
    def _():
        total[...] = part_ref[...]

    both = own_ref[...].astype(wide_type)
    for ref in (one_ref, two_ref, three_ref):
        both = both + ref[...].astype(wide_type)
    both = (
        both * kcos_ref[...]
        + pltpu.roll(both * khigh_ref[...], 96, axis=1)
        + pltpu.roll(both * klow_ref[...], 32, axis=1)
    ).astype(low_type)
    chunk_count, _, chunk, _ = wkv_ref.shape
    for k in range(chunk_count):
        total[:, k * chunk : (k + 1) * chunk] += mm_nt(both, wkv_ref[k, 0])

    @pl.when(step == pl.num_programs(0) - 1)
    def _():
        grad = resid_ref[...] + rms_back(
            embed_ref[...].astype(wide_type), gain_ref[0:1], total[...]
        )
        grad_ref[...] = grad.astype(low_type)


def project_back(scalars, embed, gains, resid, part, tables, blocks, wkv_all):
    local, dim = embed.shape
    chunk_count, ranks, chunk, _ = wkv_all.shape
    whole = lambda shape: pl.BlockSpec(shape, lambda t, place: (0, 0))
    return pl.pallas_call(
        project_back_kernel,
        grid_spec=pltpu.PrefetchScalarGridSpec(
            num_scalar_prefetch=1,
            grid=(ranks,),
            in_specs=[whole((local, dim)), whole(gains.shape)]
            + [whole((local, dim))] * 2
            + [whole((local, 128))] * 3
            + [pl.BlockSpec((local, 128), lambda t, place: (0, t))] * len(blocks)
            + [
                pl.BlockSpec(
                    (chunk_count, 1, chunk, 128),
                    lambda t, place: (0, lax.rem(place[2] - t + ranks, ranks), 0, 0),
                )
            ],
            out_specs=whole((local, dim)),
            scratch_shapes=[pltpu.VMEM((local, dim), wide_type)],
        ),
        out_shape=jax.ShapeDtypeStruct((local, dim), low_type),
        compiler_params=pltpu.CompilerParams(vmem_limit_bytes=vmem_bytes),
        cost_estimate=pl.CostEstimate(
            flops=2 * local * dim * ranks * 128,
            bytes_accessed=2 * dim * ranks * 128 + 16 * local * dim,
            transcendentals=0,
        ),
        name="project_back",
    )(scalars, embed, gains, resid, part, *tables[3:], *blocks, wkv_all)


def join_kernel(low_ref, high_ref, out_ref):
    half = low_ref.shape[1]
    out_ref[:, :half] = low_ref[...]
    out_ref[:, half:] = high_ref[...]


def join_columns(low, high):
    rows, cols = low.shape[0], low.shape[1] + high.shape[1]
    spec = lambda width: pl.BlockSpec((rows // 4, width), lambda i: (i, 0))
    return pl.pallas_call(
        join_kernel,
        grid=(4,),
        in_specs=[spec(low.shape[1]), spec(high.shape[1])],
        out_specs=spec(cols),
        out_shape=jax.ShapeDtypeStruct((rows, cols), low.dtype),
        cost_estimate=pl.CostEstimate(
            flops=0, bytes_accessed=4 * rows * cols, transcendentals=0
        ),
        name="join_columns",
    )(low, high)


def gather_sum_kernel(cuts, place_ref, own_ref, *refs):
    came, outs = refs[: len(refs) - len(cuts)], refs[len(refs) - len(cuts) :]
    *total_refs, square_ref = outs
    squares = jnp.zeros((1, 1), wide_type)
    for total_ref, start, end in zip(total_refs, cuts[:-1], cuts[1:]):
        total = own_ref[0, :, start:end].astype(wide_type)
        for ref in came:
            total = total + ref[:, start:end].astype(wide_type)
        total_ref[...] = total
        part = jnp.sum(total * total, axis=1, keepdims=True)
        squares = squares + jnp.sum(part, axis=0, keepdims=True)
    square_ref[...] = jnp.broadcast_to(squares, square_ref.shape)


def gather_sum(place, blocks, came, cuts):
    _, rows, cols = blocks.shape
    whole = lambda shape: pl.BlockSpec(shape, lambda i, place: (0, 0))
    shapes = [(rows, end - start) for start, end in zip(cuts[:-1], cuts[1:])] + [(8, 128)]
    return pl.pallas_call(
        functools.partial(gather_sum_kernel, tuple(cuts)),
        grid_spec=pltpu.PrefetchScalarGridSpec(
            num_scalar_prefetch=1,
            grid=(1,),
            in_specs=[pl.BlockSpec((1, rows, cols), lambda i, place: (place[0], 0, 0))]
            + [whole((rows, cols))] * len(came),
            out_specs=[whole(shape) for shape in shapes],
        ),
        out_shape=[jax.ShapeDtypeStruct(shape, wide_type) for shape in shapes],
        name="gather_sum",
    )(place, blocks, *came)


def update_kernel(count, scalar_ref, square_ref, *refs):
    ins, outs = refs[: 4 * count], refs[4 * count :]
    first_fix, second_fix = scalar_ref[0], scalar_ref[1]
    clip_scale = jnp.minimum(1.0, clip_max / (jnp.sqrt(square_ref[0:1, 0:1]) + 1e-06))
    for k in range(count):
        grad, master, first_old, second_old = (ins[j * count + k][...] for j in range(4))
        clipped = grad * clip_scale
        moment = beta_one * first_old + (1.0 - beta_one) * clipped
        square = beta_two * second_old + (1.0 - beta_two) * clipped * clipped
        update = moment / first_fix / (jnp.sqrt(square / second_fix) + adam_eps)
        if k < count - 1:
            new = master - learn_rate * (update + weight_decay * master)
        else:
            new = master - norms_rate * update
        outs[k][...] = new
        outs[count + k][...] = moment
        outs[2 * count + k][...] = square


def update_params(scalars, squares, grads, masters, firsts, seconds):
    count = len(grads)
    arrays = [*grads, *masters, *firsts, *seconds]
    vmem = pl.BlockSpec(memory_space=pltpu.VMEM)
    return pl.pallas_call(
        functools.partial(update_kernel, count),
        in_specs=[pl.BlockSpec(memory_space=pltpu.SMEM)] + [vmem] * (len(arrays) + 1),
        out_specs=[vmem] * (3 * count),
        out_shape=[jax.ShapeDtypeStruct(x.shape, wide_type) for x in masters] * 3,
        name="update_params",
    )(scalars, squares, *arrays)


def feed_kernel(
    place_ref, rows_ref, grad_ref, weight_ref, part_ref, product_ref, gate, up, gate_grad, up_grad
):
    step = pl.program_id(0)
    half = pl.num_programs(0) // 2
    depth = weight_ref.shape[1]

    @pl.when(step < half)
    def _():
        part = rows_ref[:, pl.ds(pl.multiple_of(step * depth, depth), depth)]

        @pl.when(step == 0)
        def _():
            gate[...] = mm(part, weight_ref[0])
            up[...] = mm(part, weight_ref[1])

        @pl.when(step > 0)
        def _():
            gate[...] += mm(part, weight_ref[0])
            up[...] += mm(part, weight_ref[1])

    @pl.when(step == half)
    def _():
        gate_val, up_val, grad = gate[...], up[...], grad_ref[...].astype(wide_type)
        sigma = 1.0 / (1.0 + jnp.exp(-gate_val))
        swish = gate_val * sigma
        product_ref[...] = (swish * up_val).astype(low_type)
        up_grad[...] = (swish * grad).astype(low_type)
        slope = sigma * (1.0 + gate_val * (1.0 - sigma))
        gate_grad[...] = (slope * up_val * grad).astype(low_type)

    @pl.when(step >= half)
    def _():
        part_ref[...] = (
            mm_nt(gate_grad[...], weight_ref[0]) + mm_nt(up_grad[...], weight_ref[1])
        ).astype(low_type)


def feed(place, rows_in, product_grad, w_gate_up):
    local, dim = rows_in.shape
    hidden = w_gate_up.shape[2]
    depth = 512
    half = dim // depth
    return pl.pallas_call(
        feed_kernel,
        grid_spec=pltpu.PrefetchScalarGridSpec(
            num_scalar_prefetch=1,
            grid=(2 * half,),
            in_specs=[
                pl.BlockSpec((local, dim), lambda i, place: (0, 0)),
                pl.BlockSpec((local, hidden), lambda i, place: (place[0], 0)),
                pl.BlockSpec((2, depth, hidden), lambda i, place: (0, lax.rem(i, half), 0)),
            ],
            out_specs=[
                pl.BlockSpec((local, depth), lambda i, place: (0, jnp.maximum(i - half, 0))),
                pl.BlockSpec((local, hidden), lambda i, place: (0, 0)),
            ],
            scratch_shapes=[
                pltpu.VMEM((local, hidden), wide_type),
                pltpu.VMEM((local, hidden), wide_type),
                pltpu.VMEM((local, hidden), low_type),
                pltpu.VMEM((local, hidden), low_type),
            ],
        ),
        out_shape=[
            jax.ShapeDtypeStruct((local, dim), low_type),
            jax.ShapeDtypeStruct((local, hidden), low_type),
        ],
        compiler_params=pltpu.CompilerParams(vmem_limit_bytes=vmem_bytes),
        cost_estimate=pl.CostEstimate(
            flops=8 * local * dim * hidden,
            bytes_accessed=4 * w_gate_up.size,
            transcendentals=local * hidden,
        ),
        name="feed",
    )(place, rows_in, product_grad, w_gate_up)


def shift(values_in, step, first, last, ranks):
    pairs = [(k, k + step) for k in range(first, last + 1) if 0 <= k + step < ranks]
    return lax.ppermute(values_in, "tensor", pairs)


def scatter_sum(joined, tensor_ranks, cuts):
    bits = lax.axis_size("dp").bit_length() - 1
    place = lax.axis_index("dp")
    size = lax.axis_size("dp")
    cols = joined.shape[1]
    depth = joined.shape[0] // size
    split = cols // 256 * 128

    def halve(block, spans, bit):
        axis = spans.index(bit)
        mine = (place >> bit) & 1
        away = lax.dynamic_index_in_dim(block, 1 - mine, axis, keepdims=False)
        kept = lax.dynamic_index_in_dim(block, mine, axis, keepdims=False)
        came = lax.ppermute(away, "dp", [(k, k ^ (1 << bit)) for k in range(size)])
        total = kept.astype(wide_type) + came.astype(wide_type)
        return total.astype(low_type), spans[:axis] + spans[axis + 1 :]

    spans = list(range(bits - 1, -1, -1))
    block = joined.reshape((2,) * bits + (depth, cols))
    block, spans = halve(block, spans, 0)
    parts = []
    for index, part in enumerate((block[..., :split], block[..., split:])):
        left = list(spans)
        order = list(reversed(spans)) if index == 0 else list(spans)
        for bit in order:
            part, left = halve(part, left, bit)
        parts.append(part)
    block = jnp.concatenate(parts, axis=1).reshape(tensor_ranks, depth // tensor_ranks, cols)
    rank = lax.axis_index("tensor")
    came = []
    for k in range(1, tensor_ranks):
        away = lax.dynamic_index_in_dim(block, (rank + k) % tensor_ranks, 0, keepdims=False)
        pairs = [(j, (j + k) % tensor_ranks) for j in range(tensor_ranks)]
        came.append(lax.ppermute(away, "tensor", pairs))
    *totals, squares = gather_sum(rank.astype(jnp.int32)[None], block, came, cuts)
    return totals, squares


def on_device(
    piece_table,
    piece_ids,
    piece_counts,
    text_ids,
    text_lengths,
    lm_gains,
    w_query,
    w_kv,
    w_attn_out,
    w_gate_up,
    w_down,
    cotangent,
    step_count,
    hyper_qkv,
    hyper_out,
    hyper_in,
    hyper_back,
    hyper_proj,
    hyper_norms,
    first_qkv,
    first_out,
    first_in,
    first_back,
    first_proj,
    first_norms,
    second_qkv,
    second_out,
    second_in,
    second_back,
    second_proj,
    second_norms,
):
    axes = ("dp", "tensor")
    rank = lax.axis_index("tensor")
    ranks = lax.axis_size("tensor")
    seq_len = text_ids.shape[1]
    local = seq_len // ranks
    length = text_lengths[0]
    gains = lm_gains.astype(jnp.float32)
    cosine, sine_rows = rope_tables(seq_len, LHD)
    start_row = rank * local
    cosine = lax.dynamic_slice_in_dim(cosine[:, 0], start_row, local, 0)
    sine_rows = lax.dynamic_slice_in_dim(sine_rows[:, 0], start_row, local, 0)
    early_half = (jnp.arange(LHD) < LHD // 2)[None, :]
    sine_low = jnp.where(early_half, -sine_rows, 0.0)
    sine_high = jnp.where(early_half, 0.0, sine_rows)
    zeros = jnp.zeros_like(sine_rows)
    tables = [jnp.concatenate([part, part], axis=1) for part in (cosine, sine_low, sine_high)]
    tables += [
        jnp.concatenate(part, axis=1)
        for part in ((cosine, zeros + 1.0), (sine_low, zeros), (sine_high, zeros))
    ]
    entry_rows, slots = piece_ids.shape
    pairs = piece_ids[:, 0::2] + piece_ids[:, 1::2] * 65536
    words = jnp.concatenate(
        [pairs, piece_counts[:, None], jnp.zeros((entry_rows, 3), jnp.int32)], axis=1
    )
    words = words.reshape(entry_rows * 8 // 128, 128)
    words = lax.all_gather(words, "dp", axis=0, tiled=True)

    def from_rank(values_in, step):
        pairs = [(j, (j + step) % ranks) for j in range(ranks)]
        return lax.ppermute(values_in, "tensor", pairs)

    rows = hyper_qkv.shape[0]
    width = hyper_out.shape[1]
    fold = hyper_in.shape[1] // width
    packed = jnp.concatenate(
        [
            hyper_qkv,
            hyper_out,
            hyper_in.reshape(rows, width, fold).swapaxes(1, 2).reshape(rows, fold * width),
            hyper_proj,
            hyper_back.reshape(rows, fold * width),
            jnp.pad(hyper_norms.T, ((0, 0), (0, 124))),
        ],
        axis=1,
    ).astype(jnp.bfloat16)
    dim = w_query.shape[0]
    chunk = 256
    chunk_count = dim // chunk
    head_cols = w_query.shape[1]
    kv_local = jnp.concatenate([w_kv[0], w_kv[1]], axis=1)
    spread_out = lax.axis_size("dp") == chunk_count
    if spread_out:
        mine = lax.dynamic_slice_in_dim(kv_local, lax.axis_index("dp") * chunk, chunk, 0)
        mine = mine.reshape(chunk // rows, rows, 128).swapaxes(0, 1).reshape(rows, -1)
        packed = jnp.concatenate([packed, mine], axis=1)
    stacked = jnp.stack([packed] + [from_rank(packed, k) for k in range(1, ranks)])
    packed = jnp.concatenate(
        [
            lax.dynamic_index_in_dim(stacked, (rank - k) % ranks, 0, keepdims=False)
            for k in range(ranks)
        ],
        axis=0,
    )
    own_query = w_query.reshape(chunk_count, 1, chunk, head_cols)
    own_out = w_attn_out.reshape(head_cols // chunk, chunk, chunk_count, chunk)
    own_out = own_out.transpose(2, 1, 0, 3).reshape(chunk_count, 1, chunk, head_cols)
    words, packed, tables, gains = lax.optimization_barrier((words, packed, tables, gains))
    words = lax.all_gather(words, "tensor", axis=0, tiled=True)
    words, rank_done, late_grad = lax.optimization_barrier(
        (words, lax.axis_index("dp"), cotangent[0])
    )
    gathered = lax.all_gather(packed, "dp", axis=0, tiled=True)
    param_cols = hyper_qkv.shape[1] + width + 2 * fold * width + dim + 128
    params = gathered

    def attn_chunk(index):
        start = index * chunk
        out_cols = lax.dynamic_slice_in_dim(w_attn_out, start, chunk, 1)
        return jnp.concatenate(
            [lax.dynamic_slice_in_dim(w_query, start, chunk, 0)]
            + [out_cols[k : k + chunk] for k in range(0, head_cols, chunk)],
            axis=1,
        )

    if spread_out:
        mine = attn_chunk(rank_done)
        rest_all = jnp.concatenate([from_rank(mine, k) for k in range(1, ranks)], axis=0)
        wkv_all = gathered[:, param_cols:].reshape(
            chunk_count, ranks, rows, chunk // rows, 128
        )
        wkv_all = wkv_all.swapaxes(2, 3).reshape(chunk_count, ranks, chunk, 128)
    else:
        own_all = jnp.concatenate([own_query, own_out], axis=3)
        rest_all = jnp.concatenate([from_rank(own_all, k) for k in range(1, ranks)], axis=1)
        wkv_all = lax.all_gather(
            kv_local.reshape(chunk_count, chunk, 128), "tensor", axis=1, tiled=False
        )

    my_ids = lax.dynamic_slice_in_dim(text_ids[0], rank * local, local, 0)
    owner = my_ids // entry_rows
    place = (owner % ranks) * lax.axis_size("dp") + owner // ranks
    my_words = words[place * (entry_rows // 16) + (my_ids % entry_rows) // 16]
    pick = (jnp.arange(16)[None, :] == (my_ids % 16)[:, None])[:, :, None]
    my_words = jnp.sum(jnp.where(pick, my_words.reshape(local, 16, 8), 0), axis=1)
    my_pieces = jnp.stack([my_words[:, :4] % 65536, my_words[:, :4] // 65536], axis=2)
    my_counts = my_words[:, 4]
    pieces = piece_table[my_pieces.reshape(local * slots)]
    live = (jnp.arange(slots)[None, :] < my_counts[:, None]).astype(jnp.float32)
    live_rows = live.reshape(local * slots, 1)
    counts = my_counts.astype(jnp.float32)[:, None]
    alive = (jnp.arange(seq_len) < length)[:, None]
    out_low = jnp.where(alive, late_grad, jnp.zeros((), jnp.bfloat16))
    product_grad = jnp.einsum("ld,fd->lf", out_low, w_down, preferred_element_type=jnp.float32)
    pieces, live_rows, counts, rest_all, product_grad, own_out = lax.optimization_barrier(
        (pieces, live_rows, counts, rest_all, product_grad, own_out)
    )
    rest_query, rest_out = rest_all[..., :head_cols], rest_all[..., head_cols:]
    if spread_out:
        rest_query, rest_out = (
            lax.all_gather(part, "dp", axis=0, tiled=True).reshape(
                chunk_count, ranks - 1, chunk, head_cols
            )
            for part in (rest_query, rest_out)
        )
    qkv, mixed, mid_rows, pre, pooled, embed, norms = hyper_forward(
        params, param_cols, pieces, live_rows, counts, slots, dim
    )


    scalars = jnp.stack([start_row, length, rank]).astype(jnp.int32)
    both, lead = project_both(scalars, embed, gains, tables, wkv_all)
    blocks = [both] + [from_rank(both, k) for k in range(1, ranks)]
    query = project(lead, tables, own_query, rest_query)
    attn_mixed, logs = attend(scalars, query, blocks)
    resid_mid, mlp_own = attend_out(attn_mixed, embed, gains, own_out, rest_out)

    def plus(left, right):
        return (left.astype(wide_type) + right.astype(wide_type)).astype(low_type)

    top = ranks - 1
    table_of = lambda *values_in: jnp.array(values_in, jnp.int32)[rank]
    near, mid_index, far = table_of(1, 2, 3, 2), table_of(2, 0, 1, 1), table_of(3, 3, 0, 0)
    order = (rank.astype(jnp.int32), near, mid_index, far)
    up_one, down_one = shift(mlp_own, 1, 0, top, ranks), shift(mlp_own, -1, 0, top, ranks)
    own_done = feed(order[0][None], mlp_own, product_grad, w_gate_up)
    up_one, down_one, own_done = lax.optimization_barrier((up_one, down_one, own_done))
    up_two, down_two = shift(up_one, 1, 1, top, ranks), shift(down_one, -1, 0, top - 1, ranks)
    near_rows = jnp.where(rank == top, up_one, down_one)
    near_done = feed(near[None], near_rows, product_grad, w_gate_up)
    up_two, down_two, near_done = lax.optimization_barrier((up_two, down_two, near_done))
    up_three, down_three = shift(up_two, 1, 2, top, ranks), shift(down_two, -1, 0, 1, ranks)
    mid_in = jnp.where(rank == 0, down_two, jnp.where(rank == top, up_two, up_one))
    mid_done = feed(mid_index[None], mid_in, product_grad, w_gate_up)
    up_three, down_three, mid_done = lax.optimization_barrier((up_three, down_three, mid_done))
    far_rows = jnp.where(
        rank == 0,
        down_three,
        jnp.where(rank == 1, down_two, jnp.where(rank == 2, up_two, up_three)),
    )
    far_done = feed(far[None], far_rows, product_grad, w_gate_up)
    products = jnp.zeros((seq_len, w_down.shape[0]), low_type)
    sums = []
    for index, (part, product) in zip(order, (own_done, near_done, mid_done, far_done)):
        sums.append(part)
        products = lax.dynamic_update_slice_in_dim(products, product, index * local, 0)
    part_own, part_near, part_mid, part_far = sums
    pre, qkv, part_far = lax.optimization_barrier((pre, qkv, part_far))
    down_came = shift(part_far, -1, top, top, ranks)
    up_came = shift(part_far, 1, 0, 0, ranks)
    hidden, slope = bends(pre)
    down_came, up_came, hidden, slope, qkv = lax.optimization_barrier(
        (down_came, up_came, hidden, slope, qkv)
    )
    down_came = shift(
        plus(jnp.where(rank == top, part_mid, part_far), down_came), -1, top - 1, top, ranks
    )
    up_came = shift(plus(jnp.where(rank == 0, part_mid, part_far), up_came), 1, 0, 1, ranks)
    probs = slot_probs(qkv, live_rows, slots)
    cot_own = lax.dynamic_slice_in_dim(cotangent[0], start_row, local, 0)
    down_came, up_came, probs, cot_own = lax.optimization_barrier(
        (down_came, up_came, probs, cot_own)
    )
    down_came = shift(
        plus(jnp.where(rank == top, part_near, part_mid), down_came), -1, 1, top, ranks
    )
    up_came = shift(plus(part_near, up_came), 1, 0, top - 1, ranks)
    mlp_grad = (
        part_own.astype(wide_type) + down_came.astype(wide_type) + up_came.astype(wide_type)
    ).astype(low_type)
    down_part = jnp.dot(products, w_down, preferred_element_type=jnp.float32).astype(jnp.bfloat16)
    mlp_grad, down_low, down_high = lax.optimization_barrier(
        (mlp_grad, down_part[:, : dim // 2], down_part[:, dim // 2 :])
    )
    low_own = lax.psum_scatter(down_low, "tensor", scatter_dimension=0, tiled=True)
    resid_grad, query_grad, *block_grads = attend_back(
        scalars, mlp_grad, cot_own, resid_mid, gains, query, blocks, attn_mixed, logs, tables,
        own_out, rest_out,
    )
    for k in range(1, ranks):
        block_grads[k] = from_rank(block_grads[k], -k)
    query_part = project_back_query(query_grad, own_query, rest_query)
    query_part, down_high = lax.optimization_barrier((query_part, down_high))
    high_own = lax.psum_scatter(down_high, "tensor", scatter_dimension=0, tiled=True)
    half = dim // 2
    layer_low = (resid_mid[:, :half] + low_own.astype(wide_type)).astype(low_type)
    embed_grad = project_back(
        scalars, embed, gains, resid_grad, query_part, tables, block_grads, wkv_all
    )
    embed_grad, layer_low = lax.optimization_barrier((embed_grad, layer_low))
    output_low = lax.all_gather(layer_low, "tensor", axis=0, tiled=True)
    shard = hyper_backward(
        params, param_cols, norms, embed_grad, pooled, pieces, live_rows, counts, qkv, mixed,
        mid_rows, hidden, slope, probs, slots,
    )
    shard, high_own, output_low = lax.optimization_barrier((shard, high_own, output_low))
    layer_high = (resid_mid[:, half:] + high_own.astype(wide_type)).astype(low_type)
    shard, layer_high = lax.optimization_barrier((shard, layer_high))
    output_high = lax.all_gather(layer_high, "tensor", axis=0, tiled=True)
    lm_output = join_columns(output_low, output_high)[None]
    cuts = [0]
    for extent in (3 * width, width, fold * width, dim, fold * width, 128):
        cuts.append(cuts[-1] + extent)
    (qkv_shard, out_shard, in_shard, proj_shard, back_shard, norm_shard), squares = scatter_sum(
        shard, ranks, cuts
    )
    in_shard = in_shard.reshape(rows, fold, width).swapaxes(1, 2)
    grad_shards = (
        qkv_shard,
        out_shard,
        in_shard.reshape(rows, fold * width),
        back_shard.reshape(rows * fold, width),
        proj_shard,
        norm_shard[:, :4].T,
    )
    squares, lm_output = lax.optimization_barrier((squares, lm_output))
    for bit in range(lax.axis_size("dp").bit_length() - 1):
        pairs = [(k, k ^ (1 << bit)) for k in range(lax.axis_size("dp"))]
        squares = squares + lax.ppermute(squares, "dp", pairs)
    for bit in range(ranks.bit_length() - 1):
        pairs = [(k, k ^ (1 << bit)) for k in range(ranks)]
        squares = squares + lax.ppermute(squares, "tensor", pairs)
    square_sum = squares[0, 0]
    grad_norm = jnp.sqrt(square_sum)
    step_value = step_count[0].astype(jnp.float32)
    first_fix = 1.0 - jnp.power(beta_one, step_value)
    second_fix = 1.0 - jnp.power(beta_two, step_value)
    masters = (hyper_qkv, hyper_out, hyper_in, hyper_back, hyper_proj, hyper_norms)
    firsts = (first_qkv, first_out, first_in, first_back, first_proj, first_norms)
    seconds = (second_qkv, second_out, second_in, second_back, second_proj, second_norms)
    factors = jnp.stack([first_fix, second_fix])
    return (
        lm_output,
        grad_norm,
        *update_params(factors, squares, grad_shards, masters, firsts, seconds),
    )


def solution(mesh):
    in_specs = (
        P(),
        P(("dp", "tensor"), None),
        P(("dp", "tensor")),
        P("dp", None),
        P("dp"),
        P(),
        P(None, "tensor"),
        P(None, None, "tensor"),
        P("tensor", None),
        P(None, None, "tensor"),
        P("tensor", None),
        P("dp", None, None),
        P(),
        P(("dp", "tensor"), None),
        P(("dp", "tensor"), None),
        P(("dp", "tensor"), None),
        P(("dp", "tensor"), None),
        P(("dp", "tensor"), None),
        P(None, ("dp", "tensor")),
        P(("dp", "tensor"), None),
        P(("dp", "tensor"), None),
        P(("dp", "tensor"), None),
        P(("dp", "tensor"), None),
        P(("dp", "tensor"), None),
        P(None, ("dp", "tensor")),
        P(("dp", "tensor"), None),
        P(("dp", "tensor"), None),
        P(("dp", "tensor"), None),
        P(("dp", "tensor"), None),
        P(("dp", "tensor"), None),
        P(None, ("dp", "tensor")),
    )
    out_specs = (
        P("dp", None, None),
        P(),
        P(("dp", "tensor"), None),
        P(("dp", "tensor"), None),
        P(("dp", "tensor"), None),
        P(("dp", "tensor"), None),
        P(("dp", "tensor"), None),
        P(None, ("dp", "tensor")),
        P(("dp", "tensor"), None),
        P(("dp", "tensor"), None),
        P(("dp", "tensor"), None),
        P(("dp", "tensor"), None),
        P(("dp", "tensor"), None),
        P(None, ("dp", "tensor")),
        P(("dp", "tensor"), None),
        P(("dp", "tensor"), None),
        P(("dp", "tensor"), None),
        P(("dp", "tensor"), None),
        P(("dp", "tensor"), None),
        P(None, ("dp", "tensor")),
    )
    return jax.shard_map(
        on_device, mesh=mesh, in_specs=in_specs, out_specs=out_specs, check_vma=False
    )
```
